32 devices in a mesh: delay: 4 (over y, core), row: 8 (over z, x).
Axes of the slice: x: 2, y: 2, z: 4, core: 2. Of those that a mesh axis runs over, the one named last changes fastest.
Arguments:
- incident: bfloat16 [3, 4096, 128], P(None, 'row'), may hold values from -6 to 6
- history: float32 [16, 4096, 128], P('delay', 'row'), may hold values from -6 to 6
- couplings: bfloat16 [16, 4096, 2048], P('delay', 'row'), may hold values from -0.06591797 to 0.06591797
- block_inverse: float32 [32, 128, 128], P('row')
- load_coeff: float32 [4096], P('row'), may hold values from 0.02 to 0.2
- pattern: int32 [16, 32, 16], P('delay', 'row'), may hold values from 0 to 31, as said below
- wanted: int32 [8, 8, 4], replicated, may hold values from -1 to 3, as said below
Outputs:
- currents: bfloat16 [3, 4096, 128], P(None, 'row')
- future: float32 [16, 4096, 128], P('delay', 'row')
The draws below stay inside these ranges and needn't reach their ends.
Inputs may be any that keep to these rules, and one draw needn't show every extreme that they name: wanted[q, p, c] for c below a count is a distinct local block index of row owner p that owner q needs, and -1 after it; every owner needs between 2 and 4 blocks of every owner, and exactly 4 of its own. pattern[l, i, s] over s are 16 distinct slots p * 4 + c whose entry wanted[q, p, c] is not -1, q the row owner of block row i; every such slot of q is named by some row of that owner.
All inputs are finite; a program needn't handle non-finite values.
Results may differ from the reference program's by a relative error of at most 0.009.
Values may be sent and summed in bfloat16 or wider, within the bound.
No kernel may reach another device: no remote copies, remote signals or barrier semaphores. Data moves between devices by JAX's collectives and lax.ppermute only.
A program may use at most 64 MiB of HBM per device.

```python
import math
import jax
import jax.numpy as jnp
from jax import lax

BS = 128
ROWNZ = 16
DELAYS = 16
BLK_DEV = 4
EXC = 128
STEPS = 3
NB = 32
N = 4096
CAP = 4
N_ROW = 8


def draw_block_inverse(key, part):
    noise = jax.random.normal(jax.random.fold_in(key, 3), (NB, BS, BS), jnp.float32)
    return jnp.eye(BS, dtype=jnp.float32)[None] + noise * (0.6 / BS ** 0.5)


def routing_tables(key):
    base = jax.random.fold_in(key, 11)
    key_count, key_local, key_mix, key_offset = jax.random.split(base, 4)
    counts = jax.random.randint(key_count, (N_ROW, N_ROW), CAP // 2, CAP + 1)
    counts = jnp.where(jnp.eye(N_ROW, dtype=bool), CAP, counts)
    scores = jax.random.randint(key_local, (N_ROW, N_ROW, BLK_DEV), 0, 1 << 20) * BLK_DEV + jnp.arange(BLK_DEV)
    order = jnp.argsort(scores, axis=-1).astype(jnp.int32)
    picks = order[:, :, :CAP]
    live = jnp.arange(CAP)[None, None, :] < counts[:, :, None]
    wanted = jnp.where(live, picks, -1).astype(jnp.int32)
    width = N_ROW * CAP
    slot_ids = jnp.broadcast_to(jnp.arange(width, dtype=jnp.int32)[None, :], (N_ROW, width))
    flat_live = live.reshape(N_ROW, width)
    mixing = jax.random.randint(key_mix, (N_ROW, width), 0, 1 << 20) * width + jnp.arange(width)
    ranking = jnp.where(flat_live, mixing, (1 << 30) + jnp.arange(width))
    ranked = jnp.take_along_axis(slot_ids, jnp.argsort(ranking, axis=-1), axis=1)
    sizes_owner = jnp.sum(counts, axis=1)
    total_rows = DELAYS * BLK_DEV
    starts = jnp.arange(total_rows)[None, :] * ROWNZ
    randoms = jax.random.randint(key_offset, (N_ROW, total_rows), 0, 1 << 20) % sizes_owner[:, None]
    offsets = jnp.where(starts < sizes_owner[:, None], starts, randoms)
    picks_row = (offsets[:, :, None] + jnp.arange(ROWNZ)[None, None, :]) % sizes_owner[:, None, None]
    chosen = jnp.take_along_axis(ranked, picks_row.reshape(N_ROW, total_rows * ROWNZ), axis=1)
    chosen = chosen.reshape(N_ROW, DELAYS, BLK_DEV, ROWNZ).transpose(1, 0, 2, 3)
    return (chosen.reshape(DELAYS, N_ROW * BLK_DEV, ROWNZ).astype(jnp.int32), wanted)


def draw_pattern(key, part):
    return routing_tables(key)[0]


def draw_wanted(key, part):
    return routing_tables(key)[1]


def steps_of(own_key, dims, pieces, low, high):
    level, own = 1.0, jax.random.fold_in(own_key, 6)
    for position, shards_of in pieces:
        steps = jnp.exp(jax.random.uniform(jax.random.fold_in(own, position), (shards_of,), jnp.float32, low / len(pieces), high / len(pieces)))
        level = level * jnp.repeat(steps, dims[position] // shards_of).reshape([-1 if axis == position else 1 for axis in range(len(dims))])
    return level


def gaussian(rng, shape, deviation, reach, shards=(), kind=jnp.bfloat16):
    factor_of = steps_of(rng, shape, shards, -0.22, 0.18) if shards else 1.0
    result = jax.random.normal(rng, shape, jnp.float32) * deviation * factor_of
    return jnp.minimum(jnp.maximum(result, -reach), reach).astype(kind)


def setup_inputs(seed: int = 0) -> dict:
    splits = jax.random.split(jax.random.key(seed), 8)
    return {
        "incident": gaussian(splits[0], (STEPS, N, EXC), 1.0, 6.0, ((1, 8),)),
        "history": gaussian(splits[1], (DELAYS, N, EXC), 1.0, 6.0, ((0, 4), (1, 8)), jnp.float32),
        "couplings": gaussian(splits[2], (DELAYS, N, ROWNZ * BS), (0.5 / (ROWNZ * BS) ** 0.5), 0.06591797, ((0, 4), (1, 8))),
        "block_inverse": draw_block_inverse(jax.random.fold_in(splits[7], 71), 0),
        "load_coeff": jnp.clip(jnp.exp(math.log(0.2) - 2.3025851 * jax.random.uniform(splits[4], (N,), jnp.float32) ** steps_of(splits[4], (N,), ((0, 8),), -0.2, 0.2)), 0.02, 0.2),
        "pattern": draw_pattern(jax.random.fold_in(splits[7], 71), 0),
        "wanted": draw_wanted(jax.random.fold_in(splits[7], 71), 0),
    }


def reference(incident, history, couplings, block_inverse, load_coeff, pattern, wanted):
    nblk = N // BS
    acc = history
    zmats = couplings.reshape(DELAYS, nblk, BS, ROWNZ * BS)
    row_owner = (jnp.arange(nblk, dtype=jnp.int32) // BLK_DEV).astype(jnp.int32)
    src_owner = (pattern // CAP).astype(jnp.int32)
    src_slot = (pattern % CAP).astype(jnp.int32)
    local = wanted[row_owner[None, :, None], src_owner, src_slot]
    columns = (src_owner * BLK_DEV + jnp.maximum(local, 0)).astype(jnp.int32)
    outputs = []
    for step in range(STEPS):
        rhs = incident[step].astype(jnp.float32) - acc[0]
        solved = jnp.einsum("iab,ibc->iac", block_inverse, rhs.reshape(nblk, BS, EXC),
                            precision=lax.Precision.HIGHEST).reshape(N, EXC)
        current = (solved - load_coeff[:, None] * solved * solved * solved).astype(jnp.bfloat16)
        outputs.append(current)
        blocks = current.reshape(nblk, BS, EXC)

        def one_delay(pair):
            zmat, cols = pair
            picked = blocks[cols].reshape(nblk, ROWNZ * BS, EXC)
            return jnp.einsum("iab,ibc->iac", zmat.astype(jnp.float32), picked.astype(jnp.float32)).reshape(N, EXC)

        products = lax.map(one_delay, (zmats, columns))
        shifted = jnp.concatenate([acc[1:], jnp.zeros((1, N, EXC), jnp.float32)], 0)
        acc = shifted + products
    return jnp.stack(outputs), acc
```

```python
import functools

import jax
import jax.numpy as jnp
from jax import lax
from jax.experimental import pallas as pl
from jax.experimental.pallas import tpu as pltpu
from jax.sharding import PartitionSpec as P

STEPS = 3


def passed_along(value, axis, steps):
    count = lax.axis_size(axis)
    leading, last = (max(0, -steps), min(count, count - steps))
    return lax.ppermute(value, axis, [(source, source + steps) for source in range(leading, last)])


def spread(value, axis, source):
    kept = jnp.where(lax.axis_index(axis) == source, value, 0).astype(value.dtype)
    return lax.psum(kept, axis)


def solve_step(incoming, field, block_inverse, load_coeff):
    blk_rows = block_inverse.shape[0]
    size_blk = block_inverse.shape[1]
    rhs = incoming.astype(jnp.float32) - field
    solved = jnp.einsum(
        "iab,ibc->iac",
        block_inverse,
        rhs.reshape(blk_rows, size_blk, rhs.shape[1]),
        precision=lax.Precision.HIGHEST,
    ).reshape(rhs.shape)
    return (solved - load_coeff[:, None] * solved * solved * solved).astype(jnp.bfloat16)


def local_general(incident, history, couplings, block_inverse, load_coeff, pattern, wanted):
    blk_rows = block_inverse.shape[0]
    size_blk = block_inverse.shape[1]
    excite = incident.shape[2]
    local_delays = history.shape[0]
    nonzero = couplings.shape[2] // size_blk
    owners = lax.axis_size("row")
    owner = lax.axis_index("row")
    slots = wanted.shape[2]
    zmats = couplings.reshape(local_delays, blk_rows, size_blk, nonzero * size_blk)
    outgoing = lax.dynamic_index_in_dim(wanted, owner, 1, keepdims=False)
    send_index = jnp.maximum(outgoing, 0)
    send_live = outgoing >= 0
    acc = history
    outputs = []
    for step in range(STEPS):
        nearest = passed_along(acc[0].astype(jnp.bfloat16), "delay", -1).astype(jnp.float32)
        current = solve_step(incident[step], acc[0], block_inverse, load_coeff)
        current = spread(current, "delay", 0)
        blocks = current.reshape(blk_rows, size_blk, excite)
        parcels = jnp.where(
            send_live[:, :, None, None], blocks[send_index], jnp.zeros((), jnp.bfloat16)
        )
        received = lax.all_to_all(parcels, "row", split_axis=0, concat_axis=0, tiled=True)
        source = received.reshape(owners * slots, size_blk, excite)
        picked = source[pattern].reshape(local_delays, blk_rows, nonzero * size_blk, excite)
        products = jnp.einsum("krab,krbc->krac", zmats, picked, preferred_element_type=jnp.float32)
        products = products.reshape(local_delays, blk_rows * size_blk, excite)
        acc = jnp.concatenate([acc[1:], nearest[None]], 0) + products
        outputs.append(current)
    return (jnp.stack(outputs), acc)


VMEM = pl.BlockSpec(memory_space=pltpu.VMEM)
SMEM = pl.BlockSpec(memory_space=pltpu.SMEM)
PARAMS = pltpu.CompilerParams(vmem_limit_bytes=24 * 1024 * 1024)


def column_of(row_vector):
    size = row_vector.shape[1]
    rows = lax.broadcasted_iota(jnp.int32, (size, size), 0)
    cols = lax.broadcasted_iota(jnp.int32, (size, size), 1)
    spread_out = jnp.where(rows == cols, jnp.broadcast_to(row_vector, (size, size)), 0.0)
    return jnp.sum(spread_out, axis=1, keepdims=True)


def solved_block(incoming, field, inverse, load_row):
    rhs = incoming.astype(jnp.float32) - field
    y = jnp.dot(inverse, rhs, precision=lax.Precision.HIGHEST, preferred_element_type=jnp.float32)
    return (y - column_of(load_row) * y * y * y).astype(jnp.bfloat16)


def block_product(table, base, matrix, row, source, size):
    nonzero = matrix.shape[1] // size
    total = None
    for s in range(0, nonzero, 2):
        pair = jnp.concatenate([source[table[base + s]], source[table[base + s + 1]]], 0)
        part = jnp.dot(
            matrix[pl.ds(row * size, size), s * size : (s + 2) * size],
            pair,
            preferred_element_type=jnp.float32,
        )
        total = part if total is None else total + part
    return total


def split_out(parity, current, keep, send, half):
    keep[...] = current[pl.ds(pl.multiple_of(parity * half, half), half), :]
    send[...] = current[pl.ds(pl.multiple_of((1 - parity) * half, half), half), :]


def first_kernel(meta, incident, field, inverse, load, keep, send, shifted, current):
    blocks, size = inverse.shape[0], inverse.shape[1]
    for i in range(blocks):
        at = slice(i * size, (i + 1) * size)
        current[at, :] = solved_block(incident[at, :], field[at, :], inverse[i], load[i : i + 1, :])
    shifted[...] = field[...].astype(jnp.bfloat16)
    split_out(meta[0], current, keep, send, blocks * size // 2)


def fill(source, mine, other):
    count = mine.shape[0]
    source[:count] = mine[...]
    source[count:] = other[...]


def next_kernel(meta, table, mine, other, matrix, field, incident, inverse, load, keep, send, shifted, source, current):
    blocks, size = inverse.shape[0], inverse.shape[1]
    nonzero = matrix.shape[1] // size
    fill(source, mine, other)
    for i in range(blocks):
        at = slice(i * size, (i + 1) * size)
        total = field[at, :] + block_product(table, i * nonzero, matrix, i, source, size)
        shifted[at, :] = total.astype(jnp.bfloat16)
        current[at, :] = solved_block(incident[at, :], total, inverse[i], load[i : i + 1, :])
    split_out(meta[0], current, keep, send, blocks * size // 2)


def rest_kernel(blocks, size, first, table, mine, other, matrices, fields, out, source):
    nonzero = matrices.shape[2] // size
    fill(source, mine, other)
    for k in range(fields.shape[0]):
        delay = first + k

        def body(i, _, k=k, delay=delay):
            at = pl.ds(pl.multiple_of(i * size, size), size)
            out[k, at, :] = fields[k, at, :] + block_product(
                table, (delay * blocks + i) * nonzero, matrices.at[delay], i, source, size
            )
            return 0

        lax.fori_loop(0, blocks, body, 0)


def struct(shape, dtype):
    return jax.ShapeDtypeStruct(shape, dtype)


def local_paired(incident, history, couplings, block_inverse, load_coeff, pattern, wanted):
    blocks, size = block_inverse.shape[:2]
    rows, excite = incident.shape[1:]
    half = rows // 2
    delays = history.shape[0]
    n_delay, n_row = lax.axis_size("delay"), lax.axis_size("row")
    d, r = lax.axis_index("delay"), lax.axis_index("row")
    parity = d % 2
    slots = wanted.shape[2]
    half_blocks = blocks // 2
    bf16 = jnp.bfloat16

    def swap(value, bit):
        pairs = [(a * n_row + q, (a ^ bit) * n_row + q) for a in range(n_delay) for q in range(n_row)]
        return lax.ppermute(value, ("delay", "row"), pairs)

    def swap_row(value, bit):
        pairs = [(a * n_row + q, a * n_row + (q ^ bit)) for a in range(n_delay) for q in range(n_row)]
        return lax.ppermute(value, ("delay", "row"), pairs)

    needed = lax.dynamic_index_in_dim(wanted, r, 0, keepdims=False).reshape(-1)
    hit = pattern[..., None] == jnp.arange(needed.shape[0], dtype=jnp.int32)
    block = jnp.sum(jnp.where(hit, needed, 0), -1)
    who = pattern // slots
    side = (block // half_blocks) ^ parity
    table = ((side * n_row + (who ^ r)) * half_blocks + block % half_blocks).reshape(-1)
    meta = jnp.stack([parity, parity]).astype(jnp.int32)
    load = load_coeff.reshape(blocks, size)

    halves = [struct((half, excite), bf16)] * 2 + [struct((rows, excite), bf16)]
    current_scratch = pltpu.VMEM((rows, excite), bf16)
    source_scratch = pltpu.VMEM((2 * n_row * half_blocks, size, excite), bf16)

    def exchange(keep, send):
        mine = jnp.where(d == 0, keep, swap(send, 1))
        bit = 2
        while bit < n_delay:
            got = swap(mine, bit)
            mine = jnp.where((d >= bit) & (d < 2 * bit), got, mine)
            bit *= 2
        pieces = [mine] + [swap_row(mine, k) for k in range(1, n_row)]
        mine = jnp.stack(pieces)
        other = swap(mine, 1)
        own, theirs = mine[0], other[0]
        whole = jnp.concatenate([jnp.where(parity == 0, own, theirs), jnp.where(parity == 0, theirs, own)], 0)
        shape = (n_row * half_blocks, size, excite)
        return whole, mine.reshape(shape), other.reshape(shape)

    def rest(first, count, mine, other, fields):
        return pl.pallas_call(
            functools.partial(rest_kernel, blocks, size, first),
            out_shape=struct((count, rows, excite), jnp.float32),
            in_specs=[SMEM, VMEM, VMEM, VMEM, VMEM],
            out_specs=VMEM,
            scratch_shapes=[source_scratch],
            compiler_params=PARAMS,
            name=f"rest{first}",
        )(table, mine, other, couplings, fields)

    keep, send, shifted = pl.pallas_call(
        first_kernel,
        out_shape=halves,
        in_specs=[SMEM, VMEM, VMEM, VMEM, VMEM],
        out_specs=[VMEM] * 3,
        scratch_shapes=[current_scratch],
        compiler_params=PARAMS,
        name="first",
    )(meta, incident[0], history[0], block_inverse, load)
    tails = [shifted]
    outputs = []
    acc = history
    for step in range(STEPS - 1):
        whole, mine, other = exchange(keep, send)
        outputs.append(whole)
        keep, send, shifted = pl.pallas_call(
            next_kernel,
            out_shape=halves,
            in_specs=[SMEM, SMEM] + [VMEM] * 7,
            out_specs=[VMEM] * 3,
            scratch_shapes=[source_scratch, current_scratch],
            compiler_params=PARAMS,
            name="next",
        )(meta, table, mine, other, couplings[0], acc[1], incident[step + 1], block_inverse, load)
        tails.append(shifted)
        fields = jnp.concatenate([acc[2:], jnp.zeros((1, rows, excite), jnp.float32)], 0)
        moved = rest(1, delays - 1, mine, other, fields)
        acc = jnp.concatenate([acc[:1], moved], 0)
    back = [(a * n_row + q, ((a - 1) % n_delay) * n_row + q) for a in range(n_delay) for q in range(n_row)]
    late = lax.ppermute(jnp.stack(tails), ("delay", "row"), back)
    late = jnp.where(d == n_delay - 1, 0, late).astype(jnp.float32)
    whole, mine, other = exchange(keep, send)
    outputs.append(whole)
    fields = jnp.concatenate([acc[1:], jnp.zeros((1, rows, excite), jnp.float32)], 0)
    fields = jnp.concatenate([fields[: delays - STEPS], fields[delays - STEPS :] + late], 0)
    future = rest(0, delays, mine, other, fields)
    return jnp.stack(outputs), future


def fits(mesh, blocks, delays):
    sizes = (mesh.shape["delay"], mesh.shape["row"])
    powers = all(n >= 2 and n & (n - 1) == 0 for n in sizes)
    return powers and blocks % 2 == 0 and delays >= STEPS


def solution(mesh):
    in_specs = (
        P(None, "row", None),
        P("delay", "row", None),
        P("delay", "row", None),
        P("row", None, None),
        P("row"),
        P("delay", "row", None),
        P(),
    )
    out_specs = (P(None, "row", None), P("delay", "row", None))

    def local(*args):
        paired = fits(mesh, args[3].shape[0], args[1].shape[0])
        return (local_paired if paired else local_general)(*args)

    return jax.shard_map(local, mesh=mesh, in_specs=in_specs, out_specs=out_specs, check_vma=False)
```

```python
import functools

import jax
import jax.numpy as jnp
from jax import lax
from jax.experimental import pallas as pl
from jax.experimental.pallas import tpu as pltpu
from jax.sharding import PartitionSpec as P

STEPS = 3


def passed_along(value, axis, steps):
    count = lax.axis_size(axis)
    leading, last = (max(0, -steps), min(count, count - steps))
    return lax.ppermute(value, axis, [(source, source + steps) for source in range(leading, last)])


def spread(value, axis, source):
    kept = jnp.where(lax.axis_index(axis) == source, value, 0).astype(value.dtype)
    return lax.psum(kept, axis)


def solve_step(incoming, field, block_inverse, load_coeff):
    blk_rows = block_inverse.shape[0]
    size_blk = block_inverse.shape[1]
    rhs = incoming.astype(jnp.float32) - field
    solved = jnp.einsum(
        "iab,ibc->iac",
        block_inverse,
        rhs.reshape(blk_rows, size_blk, rhs.shape[1]),
        precision=lax.Precision.HIGHEST,
    ).reshape(rhs.shape)
    return (solved - load_coeff[:, None] * solved * solved * solved).astype(jnp.bfloat16)


def local_general(incident, history, couplings, block_inverse, load_coeff, pattern, wanted):
    blk_rows = block_inverse.shape[0]
    size_blk = block_inverse.shape[1]
    excite = incident.shape[2]
    local_delays = history.shape[0]
    nonzero = couplings.shape[2] // size_blk
    owners = lax.axis_size("row")
    owner = lax.axis_index("row")
    slots = wanted.shape[2]
    zmats = couplings.reshape(local_delays, blk_rows, size_blk, nonzero * size_blk)
    outgoing = lax.dynamic_index_in_dim(wanted, owner, 1, keepdims=False)
    send_index = jnp.maximum(outgoing, 0)
    send_live = outgoing >= 0
    acc = history
    outputs = []
    for step in range(STEPS):
        nearest = passed_along(acc[0].astype(jnp.bfloat16), "delay", -1).astype(jnp.float32)
        current = solve_step(incident[step], acc[0], block_inverse, load_coeff)
        current = spread(current, "delay", 0)
        blocks = current.reshape(blk_rows, size_blk, excite)
        parcels = jnp.where(
            send_live[:, :, None, None], blocks[send_index], jnp.zeros((), jnp.bfloat16)
        )
        received = lax.all_to_all(parcels, "row", split_axis=0, concat_axis=0, tiled=True)
        source = received.reshape(owners * slots, size_blk, excite)
        picked = source[pattern].reshape(local_delays, blk_rows, nonzero * size_blk, excite)
        products = jnp.einsum("krab,krbc->krac", zmats, picked, preferred_element_type=jnp.float32)
        products = products.reshape(local_delays, blk_rows * size_blk, excite)
        acc = jnp.concatenate([acc[1:], nearest[None]], 0) + products
        outputs.append(current)
    return (jnp.stack(outputs), acc)


VMEM = pl.BlockSpec(memory_space=pltpu.VMEM)
SMEM = pl.BlockSpec(memory_space=pltpu.SMEM)
HBM = pl.BlockSpec(memory_space=pltpu.HBM)
PARAMS = pltpu.CompilerParams(vmem_limit_bytes=12 * 1024 * 1024)


def column_of(row_vector):
    size = row_vector.shape[1]
    rows = lax.broadcasted_iota(jnp.int32, (size, size), 0)
    cols = lax.broadcasted_iota(jnp.int32, (size, size), 1)
    spread_out = jnp.where(rows == cols, jnp.broadcast_to(row_vector, (size, size)), 0.0)
    return jnp.sum(spread_out, axis=1, keepdims=True)


def solved_block(incoming, field, inverse, load_row):
    rhs = incoming.astype(jnp.float32) - field
    y = jnp.dot(inverse, rhs, precision=lax.Precision.HIGHEST, preferred_element_type=jnp.float32)
    return y - column_of(load_row) * y * y * y


def turned(value):
    return pltpu.roll(value, value.shape[-1] // 2, value.ndim - 1)


def turned_exact(value):
    return turned(value.astype(jnp.float32)).astype(value.dtype)


def left(shape):
    return lax.broadcasted_iota(jnp.int32, shape, 1) < shape[1] // 2


def block_product(table, base, matrix, row, source, size):
    nonzero = matrix.shape[1] // size
    total = None
    for s in range(0, nonzero, 2):
        pair = jnp.concatenate([source[table[base + s]], source[table[base + s + 1]]], 0)
        part = jnp.dot(
            matrix[row * size : (row + 1) * size, s * size : (s + 2) * size],
            pair,
            preferred_element_type=jnp.float32,
        )
        total = part if total is None else total + part
    return total


def fetch(pairs, sems):
    copies = [pltpu.make_async_copy(a, b, sems.at[n]) for n, (a, b) in enumerate(pairs)]
    for copy in copies:
        copy.start()
    for copy in copies:
        copy.wait()


def first_kernel(incident, history, inverse, load, keep, send, inc, field, inv, sems):
    fetch([(incident.at[0], inc), (history.at[0], field), (inverse, inv)], sems)
    blocks, size = inv.shape[0], inv.shape[1]
    half = blocks // 2
    solved = []
    for i in range(blocks):
        at = slice(i * size, (i + 1) * size)
        solved.append(solved_block(inc[at, :], field[at, :], inv[i], load[i : i + 1, :]))
    side = left(solved[0].shape)
    for j in range(half):
        low, high, at = solved[j], solved[j + half], slice(j * size, (j + 1) * size)
        keep[at, :] = jnp.where(side, low, turned(high)).astype(keep.dtype)
        send[at, :] = jnp.where(side, turned(low), high).astype(send.dtype)


def prepare_kernel(steps, meta, incident, history, partner, inverse, bases, incs, inv, acc, sems):
    fetch([(incident.at[pl.ds(1, steps - 1)], incs), (history, acc), (inverse, inv)], sems)
    odd = meta[0] == 1
    for n in range(1, steps):

        @pl.when(odd)
        def _():
            bases[n - 1] = turned(partner[n])
            incs[n - 1] = turned_exact(incs[n - 1])

        @pl.when(jnp.logical_not(odd))
        def _():
            bases[n - 1] = acc[n]


def unpack_half(mine, source, blocks):
    half = blocks // 2
    for k in range(mine.shape[0] // half):
        for j in range(half):
            packed = mine[k * half + j]
            source[k * blocks + j] = packed
            source[k * blocks + j + half] = turned_exact(packed)


def either(meta, own, partner, run):
    @pl.when(meta[0] == 0)
    def _():
        run(own)

    @pl.when(meta[0] != 0)
    def _():
        run(partner)


def next_kernel(meta, table, mine, own, partner, base, inc, inv, load, keep, source, fields):
    blocks, size = inv.shape[0], inv.shape[1]
    half, nonzero = blocks // 2, own.shape[2] // size
    unpack_half(mine, source, blocks)

    def run(matrices):
        for i in range(blocks):
            fields[i] = block_product(table, i * nonzero, matrices.at[0], i, source, size)

    either(meta, own, partner, run)
    solved = []
    for i in range(blocks):
        at = slice(i * size, (i + 1) * size)
        solved.append(solved_block(inc[at, :], base[at, :] + fields[i], inv[i], load[i : i + 1, :]))
    side = left(solved[0].shape)
    for j in range(half):
        at = slice(j * size, (j + 1) * size)
        keep[at, :] = jnp.where(side, solved[j], turned(solved[j + half])).astype(keep.dtype)


def ahead_kernel(blocks, meta, table, mine, own, partner, base, out, source):
    size = base.shape[0] // blocks
    nonzero = own.shape[2] // size
    unpack_half(mine, source, blocks)

    def run(matrices):
        for i in range(blocks):
            at = slice(i * size, (i + 1) * size)
            out[at, :] = base[at, :] + block_product(
                table, (blocks + i) * nonzero, matrices.at[1], i, source, size
            )

    either(meta, own, partner, run)


def rest_kernel(blocks, last, meta, table, mine, other, matrices, acc, late, out, near, whole, source):
    delays, size = acc.shape[0], acc.shape[1] // blocks
    nonzero = matrices.shape[2] // size
    half = blocks // 2
    odd = meta[0] == 1
    side = left((size, mine.shape[2]))

    def unpack(even_half, odd_half):
        for k in range(mine.shape[0] // half):
            for j in range(half):
                a = even_half[k * half + j].astype(jnp.float32)
                b = odd_half[k * half + j].astype(jnp.float32)
                source[k * blocks + j] = jnp.where(side, a, turned(b)).astype(source.dtype)
                source[k * blocks + j + half] = jnp.where(side, turned(a), b).astype(source.dtype)

    @pl.when(odd)
    def _():
        unpack(other, mine)

    @pl.when(jnp.logical_not(odd))
    def _():
        unpack(mine, other)

    for i in range(blocks):
        whole[i * size : (i + 1) * size, :] = source[i]
    for k in range(delays):
        for i in range(blocks):
            at = slice(i * size, (i + 1) * size)
            total = block_product(table, (k * blocks + i) * nonzero, matrices.at[k], i, source, size)
            if k + 1 < delays:
                total = total + acc[k + 1, at, :]
            if last and k >= delays - late.shape[0]:
                total = total + late[k - (delays - late.shape[0]), at, :].astype(jnp.float32)
            out[k, at, :] = total
            if k == 0 and not last:
                near[at, :] = total.astype(near.dtype)


def struct(shape, dtype):
    return jax.ShapeDtypeStruct(shape, dtype)


def local_paired(incident, history, couplings, block_inverse, load_coeff, pattern, wanted):
    blocks, size = block_inverse.shape[:2]
    rows, excite = incident.shape[1:]
    delays = history.shape[0]
    n_delay, n_row = lax.axis_size("delay"), lax.axis_size("row")
    d, r = lax.axis_index("delay"), lax.axis_index("row")
    parity = d % 2
    slots = wanted.shape[2]
    half = blocks // 2
    bf16, f32 = jnp.bfloat16, jnp.float32
    axes = ("delay", "row")

    def swap(value, bit):
        pairs = [(a * n_row + q, (a ^ bit) * n_row + q) for a in range(n_delay) for q in range(n_row)]
        return lax.ppermute(value, axes, pairs)

    def swap_row(value, bit):
        pairs = [(a * n_row + q, a * n_row + (q ^ bit)) for a in range(n_delay) for q in range(n_row)]
        return lax.ppermute(value, axes, pairs)

    needed = lax.dynamic_index_in_dim(wanted, r, 0, keepdims=False).reshape(-1)
    hit = pattern[..., None] == jnp.arange(needed.shape[0], dtype=jnp.int32)
    block = jnp.sum(jnp.where(hit, needed, 0), -1)
    table = (((pattern // slots) ^ r) * blocks + block).reshape(-1)
    meta = jnp.stack([parity, parity]).astype(jnp.int32)
    load = load_coeff.reshape(blocks, size)

    packed = struct((half * size, excite), bf16)
    gathered = (n_row * half, size, excite)
    source = pltpu.VMEM((n_row * blocks, size, excite), bf16)

    def planes(value):
        bit = 2
        while bit < n_delay:
            got = swap(value, bit)
            value = jnp.where((d >= bit) & (d < 2 * bit), got, value)
            bit *= 2
        return value

    def exchange(value):
        pieces = [None] * n_row
        pieces[0] = value
        for k in sorted(range(1, n_row), key=lambda k: (-(k // 4), k)):
            with jax.named_scope(f"row{k}"):
                pieces[k] = swap_row(value, k)
        return jnp.stack(pieces).reshape(gathered)

    def rest(mine, acc, late, last):
        other = swap(mine, 1)
        return pl.pallas_call(
            functools.partial(rest_kernel, blocks, last),
            out_shape=[
                struct(acc.shape, f32),
                struct((rows, excite) if not last else (size, excite), bf16),
                struct((rows, excite), bf16),
            ],
            in_specs=[SMEM, SMEM] + [VMEM] * 5,
            out_specs=[VMEM] * 3,
            scratch_shapes=[source],
            compiler_params=PARAMS,
            name="last" if last else "rest",
        )(meta, table, mine, other, held, acc, late)

    with jax.named_scope("first"):
        keep, send = pl.pallas_call(
            first_kernel,
            out_shape=[packed] * 2,
            in_specs=[HBM, HBM, HBM, VMEM],
            out_specs=[VMEM] * 2,
            scratch_shapes=[
                pltpu.VMEM((rows, excite), bf16),
                pltpu.VMEM((rows, excite), f32),
                pltpu.VMEM(block_inverse.shape, f32),
                pltpu.SemaphoreType.DMA((3,)),
            ],
            compiler_params=PARAMS,
            name="first",
        )(incident, history, block_inverse, load)
    held = pltpu.with_memory_space_constraint(couplings, pltpu.MemorySpace.VMEM)
    mine = jnp.where(parity == 0, keep, swap(send, 1))
    theirs = pltpu.with_memory_space_constraint(swap(couplings, 1), pltpu.MemorySpace.VMEM)
    partner = swap(history, 1)
    chain = jnp.where(parity == 0, table, swap(table, 1))
    bases, incs, inv, acc = pl.pallas_call(
        functools.partial(prepare_kernel, STEPS),
        out_shape=[
            struct((STEPS - 1, rows, excite), f32),
            struct((STEPS - 1, rows, excite), bf16),
            struct(block_inverse.shape, f32),
            struct(history.shape, f32),
        ],
        in_specs=[SMEM, HBM, HBM, VMEM, HBM],
        out_specs=[VMEM] * 4,
        scratch_shapes=[pltpu.SemaphoreType.DMA((3,))],
        compiler_params=PARAMS,
        name="prepare",
    )(meta, incident, history, partner, block_inverse)
    none = jnp.zeros((1, size, excite), bf16)
    tails = [history[0].astype(bf16)]
    outputs = []
    base = bases[0]
    got = []
    for step in range(STEPS - 1):
        if step > 0:
            mine = planes(mine)
        near = exchange(mine)
        mine = pl.pallas_call(
            next_kernel,
            out_shape=packed,
            in_specs=[SMEM, SMEM] + [VMEM] * 7,
            out_specs=VMEM,
            scratch_shapes=[source, pltpu.VMEM((blocks, size, excite), f32)],
            compiler_params=PARAMS,
            name="next",
        )(meta, chain, near, held, theirs, base, incs[step], inv, load)
        if step == 0:
            base = pl.pallas_call(
                functools.partial(ahead_kernel, blocks),
                out_shape=struct((rows, excite), f32),
                in_specs=[SMEM, SMEM] + [VMEM] * 4,
                out_specs=VMEM,
                scratch_shapes=[source],
                compiler_params=PARAMS,
                name="ahead",
            )(meta, chain, near, held, theirs, bases[1])
            near = planes(near)
        acc, tail, whole = rest(near, acc, none, False)
        tails.append(tail)
        outputs.append(whole)
    back = [(a * n_row + q, ((a - 1) % n_delay) * n_row + q) for a in range(n_delay) for q in range(n_row)]
    late = lax.ppermute(jnp.stack(tails), axes, back)
    late = jnp.where(d == n_delay - 1, jnp.zeros((), bf16), late)
    future, _, whole = rest(exchange(planes(mine)), acc, late, True)
    outputs.append(whole)
    return jnp.stack(outputs), future


def fits(mesh, blocks, delays):
    sizes = (mesh.shape["delay"], mesh.shape["row"])
    powers = all(n >= 2 and n & (n - 1) == 0 for n in sizes)
    return powers and blocks % 2 == 0 and delays >= STEPS and STEPS == 3


def solution(mesh):
    in_specs = (
        P(None, "row", None),
        P("delay", "row", None),
        P("delay", "row", None),
        P("row", None, None),
        P("row"),
        P("delay", "row", None),
        P(),
    )
    out_specs = (P(None, "row", None), P("delay", "row", None))

    def local(*args):
        paired = fits(mesh, args[3].shape[0], args[1].shape[0])
        return (local_paired if paired else local_general)(*args)

    return jax.shard_map(local, mesh=mesh, in_specs=in_specs, out_specs=out_specs, check_vma=False)
```

```python
import functools

import jax
import jax.numpy as jnp
from jax import lax
from jax.experimental import pallas as pl
from jax.experimental.pallas import tpu as pltpu
from jax.sharding import PartitionSpec as P

STEPS = 3


def passed_along(value, axis, steps):
    count = lax.axis_size(axis)
    leading, last = (max(0, -steps), min(count, count - steps))
    return lax.ppermute(value, axis, [(source, source + steps) for source in range(leading, last)])


def spread(value, axis, source):
    kept = jnp.where(lax.axis_index(axis) == source, value, 0).astype(value.dtype)
    return lax.psum(kept, axis)


def solve_step(incoming, field, block_inverse, load_coeff):
    blk_rows = block_inverse.shape[0]
    size_blk = block_inverse.shape[1]
    rhs = incoming.astype(jnp.float32) - field
    solved = jnp.einsum(
        "iab,ibc->iac",
        block_inverse,
        rhs.reshape(blk_rows, size_blk, rhs.shape[1]),
        precision=lax.Precision.HIGHEST,
    ).reshape(rhs.shape)
    return (solved - load_coeff[:, None] * solved * solved * solved).astype(jnp.bfloat16)


def local_general(incident, history, couplings, block_inverse, load_coeff, pattern, wanted):
    blk_rows = block_inverse.shape[0]
    size_blk = block_inverse.shape[1]
    excite = incident.shape[2]
    local_delays = history.shape[0]
    nonzero = couplings.shape[2] // size_blk
    owners = lax.axis_size("row")
    owner = lax.axis_index("row")
    slots = wanted.shape[2]
    zmats = couplings.reshape(local_delays, blk_rows, size_blk, nonzero * size_blk)
    outgoing = lax.dynamic_index_in_dim(wanted, owner, 1, keepdims=False)
    send_index = jnp.maximum(outgoing, 0)
    send_live = outgoing >= 0
    acc = history
    outputs = []
    for step in range(STEPS):
        nearest = passed_along(acc[0].astype(jnp.bfloat16), "delay", -1).astype(jnp.float32)
        current = solve_step(incident[step], acc[0], block_inverse, load_coeff)
        current = spread(current, "delay", 0)
        blocks = current.reshape(blk_rows, size_blk, excite)
        parcels = jnp.where(
            send_live[:, :, None, None], blocks[send_index], jnp.zeros((), jnp.bfloat16)
        )
        received = lax.all_to_all(parcels, "row", split_axis=0, concat_axis=0, tiled=True)
        source = received.reshape(owners * slots, size_blk, excite)
        picked = source[pattern].reshape(local_delays, blk_rows, nonzero * size_blk, excite)
        products = jnp.einsum("krab,krbc->krac", zmats, picked, preferred_element_type=jnp.float32)
        products = products.reshape(local_delays, blk_rows * size_blk, excite)
        acc = jnp.concatenate([acc[1:], nearest[None]], 0) + products
        outputs.append(current)
    return (jnp.stack(outputs), acc)


VMEM = pl.BlockSpec(memory_space=pltpu.VMEM)
SMEM = pl.BlockSpec(memory_space=pltpu.SMEM)
HBM = pl.BlockSpec(memory_space=pltpu.HBM)
PARAMS = pltpu.CompilerParams(vmem_limit_bytes=8 * 1024 * 1024)
LARGE = pltpu.CompilerParams(vmem_limit_bytes=16 * 1024 * 1024)


def column_of(row_vector):
    size = row_vector.shape[1]
    rows = lax.broadcasted_iota(jnp.int32, (size, size), 0)
    cols = lax.broadcasted_iota(jnp.int32, (size, size), 1)
    spread_out = jnp.where(rows == cols, jnp.broadcast_to(row_vector, (size, size)), 0.0)
    return jnp.sum(spread_out, axis=1, keepdims=True)


def solved_block(incoming, field, inverse, load_row):
    rhs = incoming.astype(jnp.float32) - field
    y = jnp.dot(inverse, rhs, precision=lax.Precision.HIGHEST, preferred_element_type=jnp.float32)
    return y - column_of(load_row) * y * y * y


def turned(value):
    return pltpu.roll(value, value.shape[-1] // 2, value.ndim - 1)


def turned_exact(value):
    return turned(value.astype(jnp.float32)).astype(value.dtype)


def left(shape):
    return lax.broadcasted_iota(jnp.int32, shape, 1) < shape[1] // 2


def block_product(table, base, matrix, row, source, size):
    nonzero = matrix.shape[1] // size
    total = None
    for s in range(0, nonzero, 2):
        pair = jnp.concatenate([source[table[base + s]], source[table[base + s + 1]]], 0)
        part = jnp.dot(
            matrix[row * size : (row + 1) * size, s * size : (s + 2) * size],
            pair,
            preferred_element_type=jnp.float32,
        )
        total = part if total is None else total + part
    return total


def fetch(pairs, sems):
    copies = [pltpu.make_async_copy(a, b, sems.at[n]) for n, (a, b) in enumerate(pairs)]
    for copy in copies:
        copy.start()
    for copy in copies:
        copy.wait()


def first_kernel(incident, history, inverse, coeff, keep, send, inc, field, inv, load, sems):
    fetch([(incident.at[0], inc), (history.at[0], field), (inverse, inv), (coeff, load)], sems)
    blocks, size = inv.shape[0], inv.shape[1]
    half = blocks // 2
    solved = []
    for i in range(blocks):
        at = slice(i * size, (i + 1) * size)
        solved.append(solved_block(inc[at, :], field[at, :], inv[i], load[i : i + 1, :]))
    side = left(solved[0].shape)
    for j in range(half):
        low, high, at = solved[j], solved[j + half], slice(j * size, (j + 1) * size)
        keep[at, :] = jnp.where(side, low, turned(high)).astype(keep.dtype)
        send[at, :] = jnp.where(side, turned(low), high).astype(send.dtype)


def prepare_kernel(meta, incident, history, partner, inverse, coeff, *refs):
    count = (len(refs) - 5) // 2
    bases, incs = refs[:count], refs[count : 2 * count]
    inv, load, acc, tail, sems = refs[2 * count :]
    pairs = [(incident.at[n + 1], incs[n]) for n in range(count)]
    fetch(pairs + [(history, acc), (inverse, inv), (coeff, load)], sems)
    tail[...] = acc[0].astype(tail.dtype)
    for n in range(count):

        @pl.when(meta[0] == 1)
        def _():
            bases[n][...] = turned(partner[n + 1])
            incs[n][...] = turned_exact(incs[n][...])

        @pl.when(meta[0] != 1)
        def _():
            bases[n][...] = acc[n + 1]


def unpack_half(mine, source, blocks):
    half = blocks // 2
    for k in range(mine.shape[0] // half):
        for j in range(half):
            packed = mine[k * half + j]
            source[k * blocks + j] = packed
            source[k * blocks + j + half] = turned_exact(packed)


def begin_rows(meta, delay, own, theirs, held, sems):
    blocks, size = held.shape[0], held.shape[1]
    waits = []
    for i in range(blocks):
        rows = pl.ds(i * size, size)
        kept = pltpu.make_async_copy(own.at[delay, rows], held.at[i], sems.at[i])
        sent = pltpu.make_async_copy(theirs.at[delay, rows], held.at[i], sems.at[i])
        pl.when(meta[0] == 0)(kept.start)
        pl.when(meta[0] != 0)(sent.start)
        waits.append(kept.wait)
    return waits


def next_kernel(meta, table, mine, own, theirs, base, inc, inv, load, keep, source, held, sems):
    blocks, size = inv.shape[0], inv.shape[1]
    half, nonzero = blocks // 2, own.shape[2] // size
    waits = begin_rows(meta, 0, own, theirs, held, sems)
    unpack_half(mine, source, blocks)
    solved = []
    for i in range(blocks):
        at = slice(i * size, (i + 1) * size)
        waits[i]()
        field = base[at, :] + block_product(table, i * nonzero, held.at[i], 0, source, size)
        solved.append(solved_block(inc[at, :], field, inv[i], load[i : i + 1, :]))
    side = left(solved[0].shape)
    for j in range(half):
        at = slice(j * size, (j + 1) * size)
        keep[at, :] = jnp.where(side, solved[j], turned(solved[j + half])).astype(keep.dtype)


def ahead_kernel(blocks, meta, table, mine, own, theirs, base, out, source, held, sems):
    size = base.shape[0] // blocks
    nonzero = own.shape[2] // size
    waits = begin_rows(meta, 1, own, theirs, held, sems)
    unpack_half(mine, source, blocks)
    for i in range(blocks):
        at = slice(i * size, (i + 1) * size)
        waits[i]()
        out[at, :] = base[at, :] + block_product(table, (blocks + i) * nonzero, held.at[i], 0, source, size)


def unpack_whole(meta, mine, other, source, blocks):
    half = blocks // 2
    side = left(mine.shape[1:])

    def unpack(even_half, odd_half):
        for k in range(mine.shape[0] // half):
            for j in range(half):
                a = even_half[k * half + j].astype(jnp.float32)
                b = odd_half[k * half + j].astype(jnp.float32)
                source[k * blocks + j] = jnp.where(side, a, turned(b)).astype(source.dtype)
                source[k * blocks + j + half] = jnp.where(side, turned(a), b).astype(source.dtype)

    @pl.when(meta[0] == 1)
    def _():
        unpack(other, mine)

    @pl.when(meta[0] != 1)
    def _():
        unpack(mine, other)


def rest_kernel(blocks, meta, table, mine, other, matrices, acc, out, near, whole, source, held, sems):
    delays, size = acc.shape[0], acc.shape[1] // blocks
    nonzero = matrices.shape[2] // size
    loads = [pltpu.make_async_copy(matrices.at[k], held.at[k], sems.at[k]) for k in range(delays)]
    for load in loads:
        load.start()
    unpack_whole(meta, mine, other, source, blocks)
    for i in range(blocks):
        whole[i * size : (i + 1) * size, :] = source[i]
    for k in range(delays):
        loads[k].wait()
        for i in range(blocks):
            at = slice(i * size, (i + 1) * size)
            total = block_product(table, (k * blocks + i) * nonzero, held.at[k], i, source, size)
            if k + 1 < delays:
                total = total + acc[k + 1, at, :]
            out[k, at, :] = total
            if k == 0:
                near[at, :] = total.astype(near.dtype)


def last_kernel(blocks, meta, table, mine, other, matrices, acc, late, earlier, future, currents, source, held, out, whole, sems):
    delays, size = acc.shape[0], acc.shape[1] // blocks
    nonzero = matrices.shape[2] // size
    loads = [pltpu.make_async_copy(matrices.at[k], held.at[k], sems.at[k]) for k in range(delays)]
    for load in loads:
        load.start()
    stores = [
        pltpu.make_async_copy(one, currents.at[n], sems.at[2 * delays + n]) for n, one in enumerate(earlier + [whole])
    ]
    for store in stores[:-1]:
        store.start()
    unpack_whole(meta, mine, other, source, blocks)
    for i in range(blocks):
        whole[i * size : (i + 1) * size, :] = source[i]
    stores[-1].start()
    for k in range(delays):
        loads[k].wait()
        for i in range(blocks):
            at = slice(i * size, (i + 1) * size)
            total = block_product(table, (k * blocks + i) * nonzero, held.at[k], i, source, size)
            if k + 1 < delays:
                total = total + acc[k + 1, at, :]
            if k >= delays - late.shape[0]:
                total = total + late[k - (delays - late.shape[0]), at, :].astype(jnp.float32)
            out[k, at, :] = total
        stores.append(pltpu.make_async_copy(out.at[k], future.at[k], sems.at[delays + k]))
        stores[-1].start()
    for store in stores:
        store.wait()


def struct(shape, dtype):
    return jax.ShapeDtypeStruct(shape, dtype)


def local_paired(incident, history, couplings, block_inverse, load_coeff, pattern, wanted):
    blocks, size = block_inverse.shape[:2]
    rows, excite = incident.shape[1:]
    delays = history.shape[0]
    n_delay, n_row = lax.axis_size("delay"), lax.axis_size("row")
    d, r = lax.axis_index("delay"), lax.axis_index("row")
    parity = d % 2
    slots = wanted.shape[2]
    half = blocks // 2
    bf16, f32 = jnp.bfloat16, jnp.float32
    axes = ("delay", "row")

    def swap(value, bit):
        pairs = [(a * n_row + q, (a ^ bit) * n_row + q) for a in range(n_delay) for q in range(n_row)]
        return lax.ppermute(value, axes, pairs)

    def swap_row(value, bit):
        pairs = [(a * n_row + q, a * n_row + (q ^ bit)) for a in range(n_delay) for q in range(n_row)]
        return lax.ppermute(value, axes, pairs)

    needed = lax.dynamic_index_in_dim(wanted, r, 0, keepdims=False).reshape(-1)
    hit = pattern[..., None] == jnp.arange(needed.shape[0], dtype=jnp.int32)
    block = jnp.sum(jnp.where(hit, needed, 0), -1)
    table = (((pattern // slots) ^ r) * blocks + block).reshape(-1)
    meta = jnp.stack([parity, parity]).astype(jnp.int32)
    load = load_coeff.reshape(blocks, size)

    packed = struct((half * size, excite), bf16)
    gathered = (n_row * half, size, excite)
    source = pltpu.VMEM((n_row * blocks, size, excite), bf16)

    def planes(value):
        bit = 2
        while bit < n_delay:
            got = swap(value, bit)
            value = jnp.where((d >= bit) & (d < 2 * bit), got, value)
            bit *= 2
        return value

    def exchange(value):
        pieces = [None] * n_row
        pieces[0] = value
        for k in row_order(n_row):
            pieces[k] = swap_row(value, k)
        return jnp.stack(pieces).reshape(gathered)

    def gather_other(mine):
        return swap(mine, 1)

    hbm = lambda value: pltpu.with_memory_space_constraint(value, pltpu.MemorySpace.HBM)
    held = pltpu.VMEM(couplings.shape, bf16)
    row_blocks = pltpu.VMEM((blocks, size, couplings.shape[2]), bf16)
    couplings, history, incident = map(hbm, (couplings, history, incident))
    block_inverse, load = map(hbm, (block_inverse, load))

    keep, send = pl.pallas_call(
        first_kernel,
        out_shape=[packed] * 2,
        in_specs=[HBM] * 4,
        out_specs=[VMEM] * 2,
        scratch_shapes=[
            pltpu.VMEM((rows, excite), bf16),
            pltpu.VMEM((rows, excite), f32),
            pltpu.VMEM(block_inverse.shape, f32),
            pltpu.VMEM(load.shape, f32),
            pltpu.SemaphoreType.DMA((4,)),
        ],
        compiler_params=PARAMS,
        name="first",
    )(incident, history, block_inverse, load)
    got = swap(send, 1)
    mine = jnp.where(parity == 0, keep, got)
    chain_table = jnp.where(parity == 0, table, swap(table, 1))
    theirs = hbm(swap(couplings, 1))
    partner = swap(history, 1)
    count = STEPS - 1
    prepared = pl.pallas_call(
        prepare_kernel,
        out_shape=[struct((rows, excite), f32)] * count
        + [struct((rows, excite), bf16)] * count
        + [
            struct(block_inverse.shape, f32),
            struct(load.shape, f32),
            struct(history.shape, f32),
            struct((rows, excite), bf16),
        ],
        in_specs=[SMEM, HBM, HBM, VMEM, HBM, HBM],
        out_specs=[VMEM] * (2 * count + 4),
        scratch_shapes=[pltpu.SemaphoreType.DMA((count + 3,))],
        compiler_params=PARAMS,
        name="prepare",
    )(meta, incident, history, partner, block_inverse, load)
    bases, incs = prepared[:count], prepared[count : 2 * count]
    inv, load, acc, tail = prepared[2 * count :]
    tails = [tail]
    outputs = []
    base = bases[0]
    for step in range(STEPS - 1):
        if step > 0:
            mine = planes(mine)
        near = exchange(mine)
        mine = pl.pallas_call(
            next_kernel,
            out_shape=packed,
            in_specs=[SMEM, SMEM, VMEM, HBM, HBM] + [VMEM] * 4,
            out_specs=VMEM,
            scratch_shapes=[source, row_blocks, pltpu.SemaphoreType.DMA((blocks,))],
            compiler_params=PARAMS,
            name="next",
        )(meta, chain_table, near, couplings, theirs, base, incs[step], inv, load)
        if step == 0:
            base = pl.pallas_call(
                functools.partial(ahead_kernel, blocks),
                out_shape=struct((rows, excite), f32),
                in_specs=[SMEM, SMEM, VMEM, HBM, HBM, VMEM],
                out_specs=VMEM,
                scratch_shapes=[source, row_blocks, pltpu.SemaphoreType.DMA((blocks,))],
                compiler_params=PARAMS,
                name="ahead",
            )(meta, chain_table, near, couplings, theirs, bases[1])
            near = planes(near)
        other = gather_other(near)
        acc, tail, whole = pl.pallas_call(
            functools.partial(rest_kernel, blocks),
            out_shape=[struct(acc.shape, f32)] + [struct((rows, excite), bf16)] * 2,
            in_specs=[SMEM, SMEM, VMEM, VMEM, HBM, VMEM],
            out_specs=[VMEM] * 3,
            scratch_shapes=[source, held, pltpu.SemaphoreType.DMA((delays,))],
            compiler_params=LARGE,
            name="rest",
        )(meta, table, near, other, couplings, acc)
        tails.append(tail)
        outputs.append(whole)
    back = [(a * n_row + q, ((a - 1) % n_delay) * n_row + q) for a in range(n_delay) for q in range(n_row)]
    late = lax.ppermute(jnp.stack(tails), axes, back)
    late = jnp.where(d == n_delay - 1, jnp.zeros((), bf16), late)
    mine = planes(mine)
    near = exchange(mine)
    other = gather_other(near)

    def finish(*refs):
        at = 7 + STEPS - 1
        last_kernel(blocks, *refs[:7], list(refs[7:at]), *refs[at:])

    future, currents = pl.pallas_call(
        finish,
        out_shape=[struct(history.shape, f32), struct((STEPS, rows, excite), bf16)],
        in_specs=[SMEM, SMEM, VMEM, VMEM, HBM, VMEM, VMEM] + [VMEM] * (STEPS - 1),
        out_specs=[HBM] * 2,
        scratch_shapes=[
            source,
            held,
            pltpu.VMEM(history.shape, f32),
            pltpu.VMEM((rows, excite), bf16),
            pltpu.SemaphoreType.DMA((2 * delays + STEPS,)),
        ],
        compiler_params=LARGE,
        name="last",
    )(meta, table, near, other, couplings, acc, late, *outputs)
    return currents, future


def fits(mesh, blocks, delays):
    sizes = (mesh.shape["delay"], mesh.shape["row"])
    powers = all(n >= 2 and n & (n - 1) == 0 for n in sizes)
    return powers and blocks % 2 == 0 and delays >= STEPS and STEPS == 3


def row_order(n_row):
    return sorted(range(1, n_row), key=lambda k: (k < n_row // 2, k % 2 == 1 and k < n_row // 2, k))


def solution(mesh):
    in_specs = (
        P(None, "row", None),
        P("delay", "row", None),
        P("delay", "row", None),
        P("row", None, None),
        P("row"),
        P("delay", "row", None),
        P(),
    )
    out_specs = (P(None, "row", None), P("delay", "row", None))

    def local(*args):
        if not fits(mesh, args[3].shape[0], args[1].shape[0]):
            return local_general(*args)
        return local_paired(*args)

    return jax.shard_map(local, mesh=mesh, in_specs=in_specs, out_specs=out_specs, check_vma=False)
```

```python
import functools

import jax
import jax.numpy as jnp
from jax import lax
from jax.experimental import pallas as pl
from jax.experimental.pallas import tpu as pltpu
from jax.sharding import PartitionSpec as P

STEPS = 3


def passed_along(value, axis, steps):
    count = lax.axis_size(axis)
    leading, last = (max(0, -steps), min(count, count - steps))
    return lax.ppermute(value, axis, [(source, source + steps) for source in range(leading, last)])


def spread(value, axis, source):
    kept = jnp.where(lax.axis_index(axis) == source, value, 0).astype(value.dtype)
    return lax.psum(kept, axis)


def solve_step(incoming, field, block_inverse, load_coeff):
    blk_rows = block_inverse.shape[0]
    size_blk = block_inverse.shape[1]
    rhs = incoming.astype(jnp.float32) - field
    solved = jnp.einsum(
        "iab,ibc->iac",
        block_inverse,
        rhs.reshape(blk_rows, size_blk, rhs.shape[1]),
        precision=lax.Precision.HIGHEST,
    ).reshape(rhs.shape)
    return (solved - load_coeff[:, None] * solved * solved * solved).astype(jnp.bfloat16)


def local_general(incident, history, couplings, block_inverse, load_coeff, pattern, wanted):
    blk_rows = block_inverse.shape[0]
    size_blk = block_inverse.shape[1]
    excite = incident.shape[2]
    local_delays = history.shape[0]
    nonzero = couplings.shape[2] // size_blk
    owners = lax.axis_size("row")
    owner = lax.axis_index("row")
    slots = wanted.shape[2]
    zmats = couplings.reshape(local_delays, blk_rows, size_blk, nonzero * size_blk)
    outgoing = lax.dynamic_index_in_dim(wanted, owner, 1, keepdims=False)
    send_index = jnp.maximum(outgoing, 0)
    send_live = outgoing >= 0
    acc = history
    outputs = []
    for step in range(STEPS):
        nearest = passed_along(acc[0].astype(jnp.bfloat16), "delay", -1).astype(jnp.float32)
        current = solve_step(incident[step], acc[0], block_inverse, load_coeff)
        current = spread(current, "delay", 0)
        blocks = current.reshape(blk_rows, size_blk, excite)
        parcels = jnp.where(
            send_live[:, :, None, None], blocks[send_index], jnp.zeros((), jnp.bfloat16)
        )
        received = lax.all_to_all(parcels, "row", split_axis=0, concat_axis=0, tiled=True)
        source = received.reshape(owners * slots, size_blk, excite)
        picked = source[pattern].reshape(local_delays, blk_rows, nonzero * size_blk, excite)
        products = jnp.einsum("krab,krbc->krac", zmats, picked, preferred_element_type=jnp.float32)
        products = products.reshape(local_delays, blk_rows * size_blk, excite)
        acc = jnp.concatenate([acc[1:], nearest[None]], 0) + products
        outputs.append(current)
    return (jnp.stack(outputs), acc)


VMEM = pl.BlockSpec(memory_space=pltpu.VMEM)
SMEM = pl.BlockSpec(memory_space=pltpu.SMEM)
HBM = pl.BlockSpec(memory_space=pltpu.HBM)
PARAMS = pltpu.CompilerParams(vmem_limit_bytes=8 * 1024 * 1024)
LARGE = pltpu.CompilerParams(vmem_limit_bytes=16 * 1024 * 1024)


def column_of(row_vector):
    size = row_vector.shape[1]
    rows = lax.broadcasted_iota(jnp.int32, (size, size), 0)
    cols = lax.broadcasted_iota(jnp.int32, (size, size), 1)
    spread_out = jnp.where(rows == cols, jnp.broadcast_to(row_vector, (size, size)), 0.0)
    return jnp.sum(spread_out, axis=1, keepdims=True)


def solved_block(incoming, field, inverse, load_row):
    rhs = incoming.astype(jnp.float32) - field
    y = jnp.dot(inverse, rhs, precision=lax.Precision.HIGHEST, preferred_element_type=jnp.float32)
    return y - column_of(load_row) * y * y * y


def turned(value):
    return pltpu.roll(value, value.shape[-1] // 2, value.ndim - 1)


def turned_exact(value):
    return turned(value.astype(jnp.float32)).astype(value.dtype)


def own_lanes(meta, shape):
    lane = lax.broadcasted_iota(jnp.int32, shape, 1)
    return (lane < shape[1] // 2) == (meta[0] == 0)


def block_product(table, base, matrix, row, source, size):
    nonzero = matrix.shape[1] // size
    total = None
    for s in range(0, nonzero, 2):
        pair = jnp.concatenate([source[table[base + s]], source[table[base + s + 1]]], 0)
        part = jnp.dot(
            matrix[row * size : (row + 1) * size, s * size : (s + 2) * size],
            pair,
            preferred_element_type=jnp.float32,
        )
        total = part if total is None else total + part
    return total


def fetch(pairs, sems):
    copies = [pltpu.make_async_copy(a, b, sems.at[n]) for n, (a, b) in enumerate(pairs)]
    for copy in copies:
        copy.start()
    for copy in copies:
        copy.wait()


def first_kernel(incident, history, inverse, coeff, keep, send, inc, field, inv, load, sems):
    fetch([(incident.at[0], inc), (history.at[0], field), (inverse, inv), (coeff, load)], sems)
    blocks, size = inv.shape[0], inv.shape[1]
    half = blocks // 2
    solved = []
    for i in range(blocks):
        at = slice(i * size, (i + 1) * size)
        solved.append(solved_block(inc[at, :], field[at, :], inv[i], load[i : i + 1, :]))
    shape = solved[0].shape
    left = lax.broadcasted_iota(jnp.int32, shape, 1) < shape[1] // 2
    for j in range(half):
        low, high, at = solved[j], turned(solved[j + half]), slice(j * size, (j + 1) * size)
        keep[at, :] = jnp.where(left, low, high).astype(keep.dtype)
        send[at, :] = jnp.where(left, high, low).astype(send.dtype)


def prepare_kernel(meta, incident, history, partner, inverse, coeff, *refs):
    count = (len(refs) - 5) // 2
    bases, incs = refs[:count], refs[count : 2 * count]
    inv, load, acc, tail, sems = refs[2 * count :]
    pairs = [(incident.at[n + 1], incs[n]) for n in range(count)]
    pairs += [(history.at[pl.ds(1, acc.shape[0])], acc), (inverse, inv), (coeff, load)]
    pairs += [(history.at[0], bases[0])]
    fetch(pairs, sems)
    tail[...] = bases[0][...].astype(tail.dtype)
    for n in range(count):

        @pl.when(meta[0] != 0)
        def _():
            bases[n][...] = partner[n + 1]

        @pl.when(meta[0] == 0)
        def _():
            bases[n][...] = acc[n]


def unpack_half(meta, block_of, owners, source, blocks):
    half, shape = blocks // 2, source.shape[1:]
    own = own_lanes(meta, shape)
    nothing = jnp.zeros(shape, source.dtype)
    for k in range(owners):
        for j in range(half):
            packed = block_of(k, j)
            source[k * blocks + j] = jnp.where(own, packed, nothing)
            source[k * blocks + j + half] = jnp.where(own, nothing, packed)


def begin_rows(meta, delay, own, theirs, held, sems):
    blocks, size = held.shape[0], held.shape[1]
    waits = []
    for i in range(blocks):
        rows = pl.ds(i * size, size)
        kept = pltpu.make_async_copy(own.at[delay, rows], held.at[i], sems.at[i])
        sent = pltpu.make_async_copy(theirs.at[delay, rows], held.at[i], sems.at[i])
        pl.when(meta[0] == 0)(kept.start)
        pl.when(meta[0] != 0)(sent.start)
        waits.append(kept.wait)
    return waits


def next_kernel(meta, table, own, theirs, base, inc, inv, load, *refs):
    keep, joined, source, held, sems = refs[-5:]
    pieces = refs[:-5]
    blocks, size = inv.shape[0], inv.shape[1]
    half, nonzero = blocks // 2, own.shape[2] // size
    waits = begin_rows(meta, 0, own, theirs, held, sems)

    def block_of(k, j):
        packed = pieces[k][j * size : (j + 1) * size, :]
        joined[k * half + j] = packed
        return packed

    unpack_half(meta, block_of, len(pieces), source, blocks)
    solved = []
    for i in range(blocks):
        at = slice(i * size, (i + 1) * size)
        waits[i]()
        total = block_product(table, i * nonzero, held.at[i], 0, source, size)
        field = base[at, :] + (total + turned(total))
        solved.append(solved_block(inc[at, :], field, inv[i], load[i : i + 1, :]))
    lanes = own_lanes(meta, solved[0].shape)
    for j in range(half):
        at = slice(j * size, (j + 1) * size)
        keep[at, :] = jnp.where(lanes, solved[j], turned(solved[j + half])).astype(keep.dtype)


def ahead_kernel(blocks, meta, table, mine, own, theirs, base, out, source, held, sems):
    size = base.shape[0] // blocks
    nonzero = own.shape[2] // size
    waits = begin_rows(meta, 1, own, theirs, held, sems)
    half = blocks // 2
    unpack_half(meta, lambda k, j: mine[k * half + j], mine.shape[0] // half, source, blocks)
    for i in range(blocks):
        at = slice(i * size, (i + 1) * size)
        waits[i]()
        total = block_product(table, (blocks + i) * nonzero, held.at[i], 0, source, size)
        out[at, :] = base[at, :] + (total + turned(total))


def unpack_whole(meta, mine, other, source, blocks):
    half = blocks // 2
    own = own_lanes(meta, mine.shape[1:])
    for k in range(mine.shape[0] // half):
        for j in range(half):
            a, b = mine[k * half + j], other[k * half + j]
            source[k * blocks + j] = jnp.where(own, a, b)
            source[k * blocks + j + half] = turned_exact(jnp.where(own, b, a))


def rest_kernel(blocks, first, meta, table, mine, other, matrices, acc, *refs):
    source, held, sems = refs[-3:]
    outs = list(refs[:-3])
    near = outs.pop(0) if first == 0 else None
    count, size = held.shape[0], acc.shape[1] // blocks
    nonzero = matrices.shape[2] // size
    loads = [pltpu.make_async_copy(matrices.at[first + n], held.at[n], sems.at[n]) for n in range(count)]
    for load in loads:
        load.start()
    unpack_whole(meta, mine, other, source, blocks)
    if outs:
        out, whole = outs
        for i in range(blocks):
            whole[i * size : (i + 1) * size, :] = source[i]
    for n in range(count):
        k = first + n
        loads[n].wait()
        for i in range(blocks):
            at = slice(i * size, (i + 1) * size)
            total = block_product(table, (k * blocks + i) * nonzero, held.at[n], i, source, size)
            if k < acc.shape[0]:
                total = total + acc[k, at, :]
            if k == 0:
                near[at, :] = total.astype(near.dtype)
            else:
                out[k - 1, at, :] = total


def last_kernel(blocks, meta, table, mine, other, matrices, acc, late, earlier, future, currents, source, held, out, whole, sems):
    delays, size = held.shape[0], acc.shape[1] // blocks
    nonzero = matrices.shape[2] // size
    loads = [pltpu.make_async_copy(matrices.at[k], held.at[k], sems.at[k]) for k in range(delays)]
    for load in loads:
        load.start()
    stores = [
        pltpu.make_async_copy(one, currents.at[n], sems.at[2 * delays + n]) for n, one in enumerate(earlier + [whole])
    ]
    for store in stores[:-1]:
        store.start()
    unpack_whole(meta, mine, other, source, blocks)
    for i in range(blocks):
        whole[i * size : (i + 1) * size, :] = source[i]
    stores[-1].start()
    followed = meta[1] == 1
    for k in range(delays):
        loads[k].wait()
        for i in range(blocks):
            at = slice(i * size, (i + 1) * size)
            total = block_product(table, (k * blocks + i) * nonzero, held.at[k], i, source, size)
            if k < acc.shape[0]:
                total = total + acc[k, at, :]
            if k >= delays - late.shape[0]:
                extra = late[k - (delays - late.shape[0]), at, :].astype(jnp.float32)
                total = total + jnp.where(followed, extra, 0.0)
            out[k, at, :] = total
        stores.append(pltpu.make_async_copy(out.at[k], future.at[k], sems.at[delays + k]))
        stores[-1].start()
    for store in stores:
        store.wait()


def struct(shape, dtype):
    return jax.ShapeDtypeStruct(shape, dtype)


def local_paired(incident, history, couplings, block_inverse, load_coeff, pattern, wanted):
    blocks, size = block_inverse.shape[:2]
    rows, excite = incident.shape[1:]
    delays = history.shape[0]
    n_delay, n_row = lax.axis_size("delay"), lax.axis_size("row")
    d, r = lax.axis_index("delay"), lax.axis_index("row")
    parity = d % 2
    slots = wanted.shape[2]
    half = blocks // 2
    bf16, f32 = jnp.bfloat16, jnp.float32
    axes = ("delay", "row")

    def swap(value, bit):
        pairs = [(a * n_row + q, (a ^ bit) * n_row + q) for a in range(n_delay) for q in range(n_row)]
        return lax.ppermute(value, axes, pairs)

    def swap_row(value, bit):
        pairs = [(a * n_row + q, a * n_row + (q ^ bit)) for a in range(n_delay) for q in range(n_row)]
        return lax.ppermute(value, axes, pairs)

    def located(listed):
        needed = lax.dynamic_index_in_dim(wanted, r, 0, keepdims=False).reshape(-1)
        hit = listed[..., None] == jnp.arange(needed.shape[0], dtype=jnp.int32)
        block = jnp.sum(jnp.where(hit, needed, 0), -1)
        return (((listed // slots) ^ r) * blocks + block).reshape(-1)

    meta = jnp.stack([parity, (d < n_delay - 1).astype(jnp.int32)])
    load = load_coeff.reshape(blocks, size)

    packed = struct((half * size, excite), bf16)
    gathered = (n_row * half, size, excite)
    source = pltpu.VMEM((n_row * blocks, size, excite), bf16)

    def planes(value):
        bit = 2
        while bit < n_delay:
            got = swap(value, bit)
            value = jnp.where((d >= bit) & (d < 2 * bit), got, value)
            bit *= 2
        return value

    def exchange(value):
        pieces = [None] * n_row
        pieces[0] = value
        for k in row_order(n_row):
            pieces[k] = swap_row(value, k)
        return pieces

    def gather_other(mine):
        return swap(mine, 1)

    hbm = lambda value: pltpu.with_memory_space_constraint(value, pltpu.MemorySpace.HBM)
    held = pltpu.VMEM(couplings.shape, bf16)
    row_blocks = pltpu.VMEM((blocks, size, couplings.shape[2]), bf16)
    couplings, history, incident = map(hbm, (couplings, history, incident))
    block_inverse, load = map(hbm, (block_inverse, load))

    keep, send = pl.pallas_call(
        first_kernel,
        out_shape=[packed] * 2,
        in_specs=[HBM] * 4,
        out_specs=[VMEM] * 2,
        scratch_shapes=[
            pltpu.VMEM((rows, excite), bf16),
            pltpu.VMEM((rows, excite), f32),
            pltpu.VMEM(block_inverse.shape, f32),
            pltpu.VMEM(load.shape, f32),
            pltpu.SemaphoreType.DMA((4,)),
        ],
        compiler_params=PARAMS,
        name="first",
    )(incident, history, block_inverse, load)
    got = swap(send, 1)
    mine = jnp.where(parity == 0, keep, got)
    count = STEPS - 1
    listed = jnp.where(parity == 0, pattern, swap(pattern, 1))
    partner = swap(history, 1)
    theirs = hbm(swap(couplings, 1))
    table, chain_table = located(pattern), located(listed)
    prepared = pl.pallas_call(
        prepare_kernel,
        out_shape=[struct((rows, excite), f32)] * count
        + [struct((rows, excite), bf16)] * count
        + [
            struct(block_inverse.shape, f32),
            struct(load.shape, f32),
            struct((delays - 1, rows, excite), f32),
            struct((rows, excite), bf16),
        ],
        in_specs=[SMEM, HBM, HBM, VMEM, HBM, HBM],
        out_specs=[VMEM] * (2 * count + 4),
        scratch_shapes=[pltpu.SemaphoreType.DMA((count + 4,))],
        compiler_params=PARAMS,
        name="prepare",
    )(meta, incident, history, partner, block_inverse, load)
    bases, incs = prepared[:count], prepared[count : 2 * count]
    inv, load, acc, tail = prepared[2 * count :]
    tails = [tail]
    outputs = []
    base = bases[0]

    def rest(first, count, near, other, acc):
        out_shape = [struct((rows, excite), bf16)] if first == 0 else []
        if first + count > 1:
            out_shape += [struct(acc.shape, f32), struct((rows, excite), bf16)]
        return pl.pallas_call(
            functools.partial(rest_kernel, blocks, first),
            out_shape=out_shape,
            in_specs=[SMEM, SMEM, VMEM, VMEM, HBM, VMEM],
            out_specs=[VMEM] * len(out_shape),
            scratch_shapes=[
                source,
                pltpu.VMEM((count,) + couplings.shape[1:], bf16),
                pltpu.SemaphoreType.DMA((count,)),
            ],
            compiler_params=LARGE,
        )(meta, table, near, other, couplings, acc)

    for step in range(STEPS - 1):
        mine = planes(mine)
        pieces = exchange(mine)
        mine, near = pl.pallas_call(
            next_kernel,
            out_shape=[packed, struct(gathered, bf16)],
            in_specs=[SMEM, SMEM, HBM, HBM] + [VMEM] * (4 + n_row),
            out_specs=[VMEM] * 2,
            scratch_shapes=[source, row_blocks, pltpu.SemaphoreType.DMA((blocks,))],
            compiler_params=PARAMS,
            name="next",
        )(meta, chain_table, couplings, theirs, base, incs[step], inv, load, *pieces)
        if step == 0:
            base = pl.pallas_call(
                functools.partial(ahead_kernel, blocks),
                out_shape=struct((rows, excite), f32),
                in_specs=[SMEM, SMEM, VMEM, HBM, HBM, VMEM],
                out_specs=VMEM,
                scratch_shapes=[source, row_blocks, pltpu.SemaphoreType.DMA((blocks,))],
                compiler_params=PARAMS,
                name="ahead",
            )(meta, chain_table, near, couplings, theirs, bases[1])
        other = gather_other(near)
        if step == 0:
            tail, acc, whole = rest(0, delays, near, other, acc)
        else:
            (tail,) = rest(0, 1, near, other, acc)
            acc, whole = rest(1, delays - 1, near, other, acc)
        tails.append(tail)
        outputs.append(whole)
    back = [(a * n_row + q, ((a - 1) % n_delay) * n_row + q) for a in range(n_delay) for q in range(n_row)]
    late = lax.ppermute(jnp.stack(tails), axes, back)
    mine = planes(mine)
    near = jnp.stack(exchange(mine)).reshape(gathered)
    other = gather_other(near)

    def finish(*refs):
        at = 7 + STEPS - 1
        last_kernel(blocks, *refs[:7], list(refs[7:at]), *refs[at:])

    future, currents = pl.pallas_call(
        finish,
        out_shape=[struct(history.shape, f32), struct((STEPS, rows, excite), bf16)],
        in_specs=[SMEM, SMEM, VMEM, VMEM, HBM, VMEM, VMEM] + [VMEM] * (STEPS - 1),
        out_specs=[HBM] * 2,
        scratch_shapes=[
            source,
            held,
            pltpu.VMEM(history.shape, f32),
            pltpu.VMEM((rows, excite), bf16),
            pltpu.SemaphoreType.DMA((2 * delays + STEPS,)),
        ],
        compiler_params=LARGE,
        name="last",
    )(meta, table, near, other, couplings, acc, late, *outputs)
    return currents, future


def fits(mesh, blocks, delays):
    sizes = (mesh.shape["delay"], mesh.shape["row"])
    powers = all(n >= 2 and n & (n - 1) == 0 for n in sizes)
    return powers and blocks % 2 == 0 and delays >= STEPS and STEPS == 3


def row_order(n_row):
    return sorted(range(1, n_row), key=lambda k: (k < n_row // 2, k % 2 == 1 and k < n_row // 2, k))


def solution(mesh):
    in_specs = (
        P(None, "row", None),
        P("delay", "row", None),
        P("delay", "row", None),
        P("row", None, None),
        P("row"),
        P("delay", "row", None),
        P(),
    )
    out_specs = (P(None, "row", None), P("delay", "row", None))

    def local(*args):
        if not fits(mesh, args[3].shape[0], args[1].shape[0]):
            return local_general(*args)
        return local_paired(*args)

    return jax.shard_map(local, mesh=mesh, in_specs=in_specs, out_specs=out_specs, check_vma=False)
```

```python
import functools

import jax
import jax.numpy as jnp
from jax import lax
from jax.experimental import pallas as pl
from jax.experimental.pallas import tpu as pltpu
from jax.sharding import PartitionSpec as P

STEPS = 3


def passed_along(value, axis, steps):
    count = lax.axis_size(axis)
    leading, last = (max(0, -steps), min(count, count - steps))
    return lax.ppermute(value, axis, [(source, source + steps) for source in range(leading, last)])


def spread(value, axis, source):
    kept = jnp.where(lax.axis_index(axis) == source, value, 0).astype(value.dtype)
    return lax.psum(kept, axis)


def solve_step(incoming, field, block_inverse, load_coeff):
    blk_rows = block_inverse.shape[0]
    size_blk = block_inverse.shape[1]
    rhs = incoming.astype(jnp.float32) - field
    solved = jnp.einsum(
        "iab,ibc->iac",
        block_inverse,
        rhs.reshape(blk_rows, size_blk, rhs.shape[1]),
        precision=lax.Precision.HIGHEST,
    ).reshape(rhs.shape)
    return (solved - load_coeff[:, None] * solved * solved * solved).astype(jnp.bfloat16)


def local_general(incident, history, couplings, block_inverse, load_coeff, pattern, wanted):
    blk_rows = block_inverse.shape[0]
    size_blk = block_inverse.shape[1]
    excite = incident.shape[2]
    local_delays = history.shape[0]
    nonzero = couplings.shape[2] // size_blk
    owners = lax.axis_size("row")
    owner = lax.axis_index("row")
    slots = wanted.shape[2]
    zmats = couplings.reshape(local_delays, blk_rows, size_blk, nonzero * size_blk)
    outgoing = lax.dynamic_index_in_dim(wanted, owner, 1, keepdims=False)
    send_index = jnp.maximum(outgoing, 0)
    send_live = outgoing >= 0
    acc = history
    outputs = []
    for step in range(STEPS):
        nearest = passed_along(acc[0].astype(jnp.bfloat16), "delay", -1).astype(jnp.float32)
        current = solve_step(incident[step], acc[0], block_inverse, load_coeff)
        current = spread(current, "delay", 0)
        blocks = current.reshape(blk_rows, size_blk, excite)
        parcels = jnp.where(
            send_live[:, :, None, None], blocks[send_index], jnp.zeros((), jnp.bfloat16)
        )
        received = lax.all_to_all(parcels, "row", split_axis=0, concat_axis=0, tiled=True)
        source = received.reshape(owners * slots, size_blk, excite)
        picked = source[pattern].reshape(local_delays, blk_rows, nonzero * size_blk, excite)
        products = jnp.einsum("krab,krbc->krac", zmats, picked, preferred_element_type=jnp.float32)
        products = products.reshape(local_delays, blk_rows * size_blk, excite)
        acc = jnp.concatenate([acc[1:], nearest[None]], 0) + products
        outputs.append(current)
    return (jnp.stack(outputs), acc)


VMEM = pl.BlockSpec(memory_space=pltpu.VMEM)
SMEM = pl.BlockSpec(memory_space=pltpu.SMEM)
HBM = pl.BlockSpec(memory_space=pltpu.HBM)
PARAMS = pltpu.CompilerParams(vmem_limit_bytes=8 * 1024 * 1024)
LARGE = pltpu.CompilerParams(vmem_limit_bytes=16 * 1024 * 1024)


def column_of(row_vector):
    size = row_vector.shape[1]
    rows = lax.broadcasted_iota(jnp.int32, (size, size), 0)
    cols = lax.broadcasted_iota(jnp.int32, (size, size), 1)
    spread_out = jnp.where(rows == cols, jnp.broadcast_to(row_vector, (size, size)), 0.0)
    return jnp.broadcast_to(jnp.sum(spread_out, axis=1, keepdims=True), (size, size))


def in_two(value):
    high = value.astype(jnp.bfloat16)
    return high, (value - high.astype(jnp.float32)).astype(jnp.bfloat16)


def solved_block(incoming, field, inverse, load):
    rhs = in_two(incoming.astype(jnp.float32) - field)
    dot = functools.partial(jnp.dot, preferred_element_type=jnp.float32)
    y = dot(inverse[0], rhs[0]) + (dot(inverse[0], rhs[1]) + dot(inverse[1], rhs[0]))
    return y - load * y * y * y


def turned(value):
    return pltpu.roll(value, value.shape[-1] // 2, value.ndim - 1)


def turned_exact(value):
    return turned(value.astype(jnp.float32)).astype(value.dtype)


def own_lanes(meta, shape):
    lane = lax.broadcasted_iota(jnp.int32, shape, 1)
    return (lane < shape[1] // 2) == (meta[0] == 0)


def block_product(listed, matrix, row, block_of, size):
    nonzero = matrix.shape[1] // size
    total = None
    for s in range(0, nonzero, 2):
        pair = jnp.concatenate([block_of(listed(s)), block_of(listed(s + 1))], 0)
        part = jnp.dot(
            matrix[row * size : (row + 1) * size, s * size : (s + 2) * size],
            pair,
            preferred_element_type=jnp.float32,
        )
        total = part if total is None else total + part
    return total


def fetch(pairs, sems):
    copies = [pltpu.make_async_copy(a, b, sems.at[n]) for n, (a, b) in enumerate(pairs)]
    for copy in copies:
        copy.start()
    for copy in copies:
        copy.wait()


def first_kernel(incident, history, inverse, coeff, keep, send, inc, field, inv, load, sems):
    fetch([(incident.at[0], inc), (history.at[0], field), (inverse, inv), (coeff, load)], sems)
    blocks, size = inv.shape[0], inv.shape[1]
    half = blocks // 2
    solved = []
    for i in range(blocks):
        at = slice(i * size, (i + 1) * size)
        solved.append(solved_block(inc[at, :], field[at, :], in_two(inv[i]), column_of(load[i : i + 1, :])))
    shape = solved[0].shape
    left = lax.broadcasted_iota(jnp.int32, shape, 1) < shape[1] // 2
    for j in range(half):
        low, high, at = solved[j], turned(solved[j + half]), slice(j * size, (j + 1) * size)
        keep[at, :] = jnp.where(left, low, high).astype(keep.dtype)
        send[at, :] = jnp.where(left, high, low).astype(send.dtype)


def by_parity(meta, own, theirs, kept, sem):
    copies = [pltpu.make_async_copy(source, kept, sem) for source in (own, theirs)]

    def start():
        pl.when(meta[0] == 0)(copies[0].start)
        pl.when(meta[0] != 0)(copies[1].start)

    return start, copies[0].wait


def prepare_kernel(meta, incident, history, partner, own, theirs, inverse, coeff, *refs):
    count = (len(refs) - 9) // 3
    bases, incs, mats = (refs[n * count : (n + 1) * count] for n in range(3))
    inv_high, inv_low, load, acc, tail, inv, rows, nearest, sems = refs[3 * count :]
    pairs = [by_parity(meta, history.at[n + 1], partner.at[n + 1], bases[n], sems.at[n]) for n in range(count)]
    pairs += [by_parity(meta, own.at[n], theirs.at[n], mats[n], sems.at[count + n]) for n in range(count)]
    plain = [(inverse, inv), (coeff, rows), (history.at[0], nearest), (history.at[pl.ds(1, acc.shape[0])], acc)]
    plain += [(incident.at[n + 1], incs[n]) for n in range(count)]
    plain = [pltpu.make_async_copy(a, b, sems.at[2 * count + n]) for n, (a, b) in enumerate(plain)]
    for copy in plain:
        copy.start()
    for start, _ in pairs:
        start()
    for copy in plain:
        copy.wait()
    blocks, size = inv.shape[0], inv.shape[1]
    for i in range(blocks):
        inv_high[i], inv_low[i] = in_two(inv[i])
        load[i * size : (i + 1) * size, :] = column_of(rows[i : i + 1, :])
    tail[...] = nearest[...].astype(tail.dtype)
    for _, wait in pairs:
        wait()


def unpack_half(meta, block_of, owners, source, blocks):
    half, shape = blocks // 2, source.shape[1:]
    own = own_lanes(meta, shape)
    nothing = jnp.zeros(shape, source.dtype)
    for k in range(owners):
        for j in range(half):
            packed = block_of(k, j)
            source[k * blocks + j] = jnp.where(own, packed, nothing)
            source[k * blocks + j + half] = jnp.where(own, nothing, packed)


def chained(meta, table, swapped, base):
    return lambda s: jnp.where(meta[0] == 0, table[base + s], swapped[base + s])


def next_kernel(meta, table, swapped, matrix, base, inc, inv_high, inv_low, load, *refs):
    keep, joined, source = refs[-3:]
    pieces = refs[:-3]
    blocks, size = inv_high.shape[0], inv_high.shape[1]
    half, nonzero = blocks // 2, matrix.shape[1] // size

    def block_of(k, j):
        packed = pieces[k][j * size : (j + 1) * size, :]
        joined[k * half + j] = packed
        return packed

    unpack_half(meta, block_of, len(pieces), source, blocks)
    solved = []
    for i in range(blocks):
        at = slice(i * size, (i + 1) * size)
        listed = chained(meta, table, swapped, i * nonzero)
        total = block_product(listed, matrix, i, lambda n: source[n], size)
        field = base[at, :] + (total + turned(total))
        solved.append(solved_block(inc[at, :], field, (inv_high[i], inv_low[i]), load[at, :]))
    lanes = own_lanes(meta, solved[0].shape)
    for j in range(half):
        at = slice(j * size, (j + 1) * size)
        keep[at, :] = jnp.where(lanes, solved[j], turned(solved[j + half])).astype(keep.dtype)


def ahead_kernel(blocks, meta, table, swapped, mine, matrix, base, out, source):
    size = base.shape[0] // blocks
    half, nonzero = blocks // 2, matrix.shape[1] // size
    unpack_half(meta, lambda k, j: mine[k * half + j], mine.shape[0] // half, source, blocks)
    for i in range(blocks):
        at = slice(i * size, (i + 1) * size)
        listed = chained(meta, table, swapped, (blocks + i) * nonzero)
        total = block_product(listed, matrix, i, lambda n: source[n], size)
        out[at, :] = base[at, :] + (total + turned(total))


def unpack_whole(meta, mine, other, source, blocks, lanes=slice(None)):
    half = blocks // 2
    own = own_lanes(meta, mine.shape[1:])
    for k in range(mine.shape[0] // half):
        for j in range(half):
            a, b = mine[k * half + j], other[k * half + j]
            source[k * blocks + j, :, lanes] = jnp.where(own, a, b)
            source[k * blocks + j + half, :, lanes] = turned_exact(jnp.where(own, b, a))


def table_of(table, base):
    return lambda s: table[base + s]


def near_kernel(blocks, meta, table, mine, other, own, theirs, acc, near, ahead, kept, chain, whole, source, held, sems):
    size = acc.shape[1] // blocks
    nonzero = held.shape[1] // size
    start, wait = by_parity(meta, own.at[0], theirs.at[0], chain, sems.at[2])
    loads = [pltpu.make_async_copy(own.at[n], ref, sems.at[n]) for n, ref in enumerate((kept, held))]
    for load in loads:
        load.start()
    start()
    unpack_whole(meta, mine, other, source, blocks)
    for i in range(blocks):
        whole[i * size : (i + 1) * size, :] = source[i]
    for k, (matrix, out) in enumerate(((kept, near), (held, ahead))):
        loads[k].wait()
        for i in range(blocks):
            at = slice(i * size, (i + 1) * size)
            listed = table_of(table, (k * blocks + i) * nonzero)
            total = acc[k, at, :] + block_product(listed, matrix, i, lambda n: source[n], size)
            out[at, :] = total.astype(out.dtype)
    wait()


def nearer_kernel(blocks, meta, table, mine, other, matrix, base, near, source):
    size = base.shape[0] // blocks
    nonzero = matrix.shape[1] // size
    unpack_whole(meta, mine, other, source, blocks)
    for i in range(blocks):
        at = slice(i * size, (i + 1) * size)
        listed = table_of(table, i * nonzero)
        total = base[at, :] + block_product(listed, matrix, i, lambda n: source[n], size)
        near[at, :] = total.astype(near.dtype)


def far_kernel(blocks, meta, table, mine0, other0, mine1, other1, own, acc, out, mats, whole, source, sems):
    delays, size, excite = mats.shape[0], acc.shape[1] // blocks, acc.shape[2]
    nonzero = mats.shape[2] // size
    order = list(range(1, delays)) + [0]
    loads = {k: pltpu.make_async_copy(own.at[k], mats.at[k], sems.at[k]) for k in order}
    for k in order:
        loads[k].start()
    unpack_whole(meta, mine0, other0, source, blocks, slice(0, excite))
    unpack_whole(meta, mine1, other1, source, blocks, slice(excite, 2 * excite))
    for i in range(blocks):
        whole[i * size : (i + 1) * size, :] = source[i, :, excite:]
    for k in range(1, delays):
        loads[k].wait()
        for i in range(blocks):
            at = slice(i * size, (i + 1) * size)
            listed = table_of(table, (k * blocks + i) * nonzero)
            base = acc[k + 1, at, :] if k + 1 < delays - 1 else None
            if k == 1:
                late = block_product(listed, mats.at[k], i, lambda n: source[n, :, excite:], size)
            else:
                both = block_product(listed, mats.at[k], i, lambda n: source[n], size)
                out[k - 2, at, :] = out[k - 2, at, :] + both[:, :excite]
                late = both[:, excite:]
            out[k - 1, at, :] = late if base is None else late + base
    loads[0].wait()


def last_kernel(blocks, meta, table, mine, other, mats, acc, late, earlier, future, currents, source, out, whole, sems):
    delays, size = mats.shape[0], acc.shape[1] // blocks
    nonzero = mats.shape[2] // size
    stores = [
        pltpu.make_async_copy(one, currents.at[n], sems.at[delays + n]) for n, one in enumerate(earlier + [whole])
    ]
    for store in stores[:-1]:
        store.start()
    unpack_whole(meta, mine, other, source, blocks)
    for i in range(blocks):
        whole[i * size : (i + 1) * size, :] = source[i]
    stores[-1].start()
    followed = meta[1] == 1
    for k in range(delays):
        for i in range(blocks):
            at = slice(i * size, (i + 1) * size)
            listed = table_of(table, (k * blocks + i) * nonzero)
            total = block_product(listed, mats.at[k], i, lambda n: source[n], size)
            if k < acc.shape[0]:
                total = total + acc[k, at, :]
            if k >= delays - late.shape[0]:
                extra = late[k - (delays - late.shape[0]), at, :].astype(jnp.float32)
                total = total + jnp.where(followed, extra, 0.0)
            out[k, at, :] = total
        stores.append(pltpu.make_async_copy(out.at[k], future.at[k], sems.at[k]))
        stores[-1].start()
    for store in stores:
        store.wait()


def struct(shape, dtype):
    return jax.ShapeDtypeStruct(shape, dtype)


def local_paired(incident, history, couplings, block_inverse, load_coeff, pattern, wanted):
    blocks, size = block_inverse.shape[:2]
    rows, excite = incident.shape[1:]
    delays = history.shape[0]
    n_delay, n_row = lax.axis_size("delay"), lax.axis_size("row")
    d, r = lax.axis_index("delay"), lax.axis_index("row")
    parity = d % 2
    slots = wanted.shape[2]
    half = blocks // 2
    bf16, f32 = jnp.bfloat16, jnp.float32
    axes = ("delay", "row")

    def swap(value, bit):
        pairs = [(a * n_row + q, (a ^ bit) * n_row + q) for a in range(n_delay) for q in range(n_row)]
        return lax.ppermute(value, axes, pairs)

    def swap_row(value, bit):
        pairs = [(a * n_row + q, a * n_row + (q ^ bit)) for a in range(n_delay) for q in range(n_row)]
        return lax.ppermute(value, axes, pairs)

    def located(listed):
        needed = lax.dynamic_index_in_dim(wanted, r, 0, keepdims=False).reshape(-1)
        hit = listed[..., None] == jnp.arange(needed.shape[0], dtype=jnp.int32)
        block = jnp.sum(jnp.where(hit, needed, 0), -1)
        return (((listed // slots) ^ r) * blocks + block).reshape(-1)

    meta = jnp.stack([parity, (d < n_delay - 1).astype(jnp.int32)])
    load = load_coeff.reshape(blocks, size)

    packed = struct((half * size, excite), bf16)
    gathered = (n_row * half, size, excite)
    source = pltpu.VMEM((n_row * blocks, size, excite), bf16)

    def planes(value):
        bit = 2
        while bit < n_delay:
            got = swap(value, bit)
            value = jnp.where((d >= bit) & (d < 2 * bit), got, value)
            bit *= 2
        return value

    def exchange(value):
        pieces = [None] * n_row
        pieces[0] = value
        for k in row_order(n_row):
            pieces[k] = swap_row(value, k)
        return pieces

    def gather_other(mine):
        return swap(mine, 1)

    hbm = lambda value: pltpu.with_memory_space_constraint(value, pltpu.MemorySpace.HBM)
    couplings, history, incident = map(hbm, (couplings, history, incident))
    block_inverse, load = map(hbm, (block_inverse, load))

    keep, send = pl.pallas_call(
        first_kernel,
        out_shape=[packed] * 2,
        in_specs=[HBM] * 4,
        out_specs=[VMEM] * 2,
        scratch_shapes=[
            pltpu.VMEM((rows, excite), bf16),
            pltpu.VMEM((rows, excite), f32),
            pltpu.VMEM(block_inverse.shape, f32),
            pltpu.VMEM(load.shape, f32),
            pltpu.SemaphoreType.DMA((4,)),
        ],
        compiler_params=PARAMS,
        name="first",
    )(incident, history, block_inverse, load)
    got = swap(send, 1)
    mine = jnp.where(parity == 0, keep, got)
    count = STEPS - 1
    table = located(pattern)
    theirs = hbm(swap(couplings, 1))
    partner = hbm(swap(history, 1))
    swapped = swap(table, 1)
    field, current = struct((rows, excite), f32), struct((rows, excite), bf16)
    matrix = struct(couplings.shape[1:], bf16)
    prepared = pl.pallas_call(
        prepare_kernel,
        out_shape=[field] * count
        + [current] * count
        + [matrix] * count
        + [struct(block_inverse.shape, bf16)] * 2
        + [field, struct((delays - 1, rows, excite), f32), current],
        in_specs=[SMEM] + [HBM] * 7,
        out_specs=[VMEM] * (3 * count + 5),
        scratch_shapes=[
            pltpu.VMEM(block_inverse.shape, f32),
            pltpu.VMEM(load.shape, f32),
            pltpu.VMEM((rows, excite), f32),
            pltpu.SemaphoreType.DMA((3 * count + 4,)),
        ],
        compiler_params=LARGE,
        name="prepare",
    )(meta, incident, history, partner, couplings, theirs, block_inverse, load)
    bases, incs, mats = (prepared[n * count : (n + 1) * count] for n in range(3))
    inv_high, inv_low, load, acc, tail = prepared[3 * count :]

    def advance(step, pieces, mat, base):
        return pl.pallas_call(
            next_kernel,
            out_shape=[packed, struct(gathered, bf16)],
            in_specs=[SMEM] * 3 + [VMEM] * (6 + n_row),
            out_specs=[VMEM] * 2,
            scratch_shapes=[source],
            compiler_params=LARGE,
            name="next",
        )(meta, table, swapped, mat, base, incs[step], inv_high, inv_low, load, *pieces)

    def spread_out(mine):
        mine = planes(mine)
        return exchange(mine)

    pieces = spread_out(mine)
    mine, near0 = advance(0, pieces, mats[0], bases[0])
    base = pl.pallas_call(
        functools.partial(ahead_kernel, blocks),
        out_shape=field,
        in_specs=[SMEM] * 3 + [VMEM] * 3,
        out_specs=VMEM,
        scratch_shapes=[source],
        compiler_params=LARGE,
        name="ahead",
    )(meta, table, swapped, near0, mats[1], bases[1])
    other0 = gather_other(near0)
    first_tail, ahead, kept, chain, whole0 = pl.pallas_call(
        functools.partial(near_kernel, blocks),
        out_shape=[current, field, matrix, matrix, current],
        in_specs=[SMEM, SMEM, VMEM, VMEM, HBM, HBM, VMEM],
        out_specs=[VMEM] * 5,
        scratch_shapes=[source, pltpu.VMEM(couplings.shape[1:], bf16), pltpu.SemaphoreType.DMA((3,))],
        compiler_params=LARGE,
        name="near",
    )(meta, table, near0, other0, couplings, theirs, acc)

    pieces = spread_out(mine)
    mine, near1 = advance(1, pieces, chain, base)
    other1 = gather_other(near1)
    second_tail = pl.pallas_call(
        functools.partial(nearer_kernel, blocks),
        out_shape=current,
        in_specs=[SMEM] * 2 + [VMEM] * 4,
        out_specs=VMEM,
        scratch_shapes=[source],
        compiler_params=LARGE,
        name="nearer",
    )(meta, table, near1, other1, kept, ahead)
    acc, mats, whole1 = pl.pallas_call(
        functools.partial(far_kernel, blocks),
        out_shape=[struct(acc.shape, f32), struct(couplings.shape, bf16), current],
        in_specs=[SMEM] * 2 + [VMEM] * 4 + [HBM, VMEM],
        out_specs=[VMEM] * 3,
        scratch_shapes=[pltpu.VMEM((n_row * blocks, size, 2 * excite), bf16), pltpu.SemaphoreType.DMA((delays,))],
        compiler_params=LARGE,
        name="far",
    )(meta, table, near0, other0, near1, other1, couplings, acc)
    tails = [tail, first_tail, second_tail]
    back = [(a * n_row + q, ((a - 1) % n_delay) * n_row + q) for a in range(n_delay) for q in range(n_row)]
    late = lax.ppermute(jnp.stack(tails), axes, back)

    near2 = jnp.stack(spread_out(mine)).reshape(gathered)
    other2 = gather_other(near2)

    def finish(*refs):
        last_kernel(blocks, *refs[:7], list(refs[7:9]), *refs[9:])

    future, currents = pl.pallas_call(
        finish,
        out_shape=[struct(history.shape, f32), struct((STEPS, rows, excite), bf16)],
        in_specs=[SMEM] * 2 + [VMEM] * 7,
        out_specs=[HBM] * 2,
        scratch_shapes=[
            source,
            pltpu.VMEM(history.shape, f32),
            pltpu.VMEM((rows, excite), bf16),
            pltpu.SemaphoreType.DMA((delays + STEPS,)),
        ],
        compiler_params=LARGE,
        name="last",
    )(meta, table, near2, other2, mats, acc, late, whole0, whole1)
    return currents, future


def fits(mesh, blocks, delays):
    sizes = (mesh.shape["delay"], mesh.shape["row"])
    powers = all(n >= 2 and n & (n - 1) == 0 for n in sizes)
    return powers and blocks % 2 == 0 and delays >= STEPS and STEPS == 3


def row_order(n_row):
    return sorted(range(1, n_row), key=lambda k: (k < n_row // 2, k % 2 == 1 and k < n_row // 2, k))


def solution(mesh):
    in_specs = (
        P(None, "row", None),
        P("delay", "row", None),
        P("delay", "row", None),
        P("row", None, None),
        P("row"),
        P("delay", "row", None),
        P(),
    )
    out_specs = (P(None, "row", None), P("delay", "row", None))

    def local(*args):
        if not fits(mesh, args[3].shape[0], args[1].shape[0]):
            return local_general(*args)
        return local_paired(*args)

    return jax.shard_map(local, mesh=mesh, in_specs=in_specs, out_specs=out_specs, check_vma=False)
```

```python
import functools

import jax
import jax.numpy as jnp
from jax import lax
from jax.experimental import pallas as pl
from jax.experimental.pallas import tpu as pltpu
from jax.sharding import PartitionSpec as P

STEPS = 3


def passed_along(value, axis, steps):
    count = lax.axis_size(axis)
    leading, last = (max(0, -steps), min(count, count - steps))
    return lax.ppermute(value, axis, [(source, source + steps) for source in range(leading, last)])


def spread(value, axis, source):
    kept = jnp.where(lax.axis_index(axis) == source, value, 0).astype(value.dtype)
    return lax.psum(kept, axis)


def solve_step(incoming, field, block_inverse, load_coeff):
    blk_rows = block_inverse.shape[0]
    size_blk = block_inverse.shape[1]
    rhs = incoming.astype(jnp.float32) - field
    solved = jnp.einsum(
        "iab,ibc->iac",
        block_inverse,
        rhs.reshape(blk_rows, size_blk, rhs.shape[1]),
        precision=lax.Precision.HIGHEST,
    ).reshape(rhs.shape)
    return (solved - load_coeff[:, None] * solved * solved * solved).astype(jnp.bfloat16)


def local_general(incident, history, couplings, block_inverse, load_coeff, pattern, wanted):
    blk_rows = block_inverse.shape[0]
    size_blk = block_inverse.shape[1]
    excite = incident.shape[2]
    local_delays = history.shape[0]
    nonzero = couplings.shape[2] // size_blk
    owners = lax.axis_size("row")
    owner = lax.axis_index("row")
    slots = wanted.shape[2]
    zmats = couplings.reshape(local_delays, blk_rows, size_blk, nonzero * size_blk)
    outgoing = lax.dynamic_index_in_dim(wanted, owner, 1, keepdims=False)
    send_index = jnp.maximum(outgoing, 0)
    send_live = outgoing >= 0
    acc = history
    outputs = []
    for step in range(STEPS):
        nearest = passed_along(acc[0].astype(jnp.bfloat16), "delay", -1).astype(jnp.float32)
        current = solve_step(incident[step], acc[0], block_inverse, load_coeff)
        current = spread(current, "delay", 0)
        blocks = current.reshape(blk_rows, size_blk, excite)
        parcels = jnp.where(
            send_live[:, :, None, None], blocks[send_index], jnp.zeros((), jnp.bfloat16)
        )
        received = lax.all_to_all(parcels, "row", split_axis=0, concat_axis=0, tiled=True)
        source = received.reshape(owners * slots, size_blk, excite)
        picked = source[pattern].reshape(local_delays, blk_rows, nonzero * size_blk, excite)
        products = jnp.einsum("krab,krbc->krac", zmats, picked, preferred_element_type=jnp.float32)
        products = products.reshape(local_delays, blk_rows * size_blk, excite)
        acc = jnp.concatenate([acc[1:], nearest[None]], 0) + products
        outputs.append(current)
    return (jnp.stack(outputs), acc)


VMEM = pl.BlockSpec(memory_space=pltpu.VMEM)
SMEM = pl.BlockSpec(memory_space=pltpu.SMEM)
HBM = pl.BlockSpec(memory_space=pltpu.HBM)
ANY = pl.BlockSpec(memory_space=pl.ANY)
PARAMS = pltpu.CompilerParams(vmem_limit_bytes=8 * 1024 * 1024)
LARGE = pltpu.CompilerParams(vmem_limit_bytes=16 * 1024 * 1024)


def column_of(row_vector):
    size = row_vector.shape[1]
    rows = lax.broadcasted_iota(jnp.int32, (size, size), 0)
    cols = lax.broadcasted_iota(jnp.int32, (size, size), 1)
    spread_out = jnp.where(rows == cols, jnp.broadcast_to(row_vector, (size, size)), 0.0)
    return jnp.broadcast_to(jnp.sum(spread_out, axis=1, keepdims=True), (size, size))


def in_two(value):
    high = value.astype(jnp.bfloat16)
    return high, (value - high.astype(jnp.float32)).astype(jnp.bfloat16)


def solved_block(incoming, field, inverse, load):
    rhs = in_two(incoming.astype(jnp.float32) - field)
    dot = functools.partial(jnp.dot, preferred_element_type=jnp.float32)
    y = dot(inverse[0], rhs[0]) + (dot(inverse[0], rhs[1]) + dot(inverse[1], rhs[0]))
    return y - load * y * y * y


def turned(value):
    return pltpu.roll(value, value.shape[-1] // 2, value.ndim - 1)


def turned_exact(value):
    return turned(value.astype(jnp.float32)).astype(value.dtype)


def own_lanes(meta, shape):
    lane = lax.broadcasted_iota(jnp.int32, shape, 1)
    return (lane < shape[1] // 2) == (meta[0] == 0)


def block_product(listed, matrix, row, block_of, size):
    nonzero = matrix.shape[1] // size
    total = None
    for s in range(0, nonzero, 2):
        pair = jnp.concatenate([block_of(listed(s)), block_of(listed(s + 1))], 0)
        part = jnp.dot(
            matrix[row * size : (row + 1) * size, s * size : (s + 2) * size],
            pair,
            preferred_element_type=jnp.float32,
        )
        total = part if total is None else total + part
    return total


def fetch(pairs, sems):
    copies = [pltpu.make_async_copy(a, b, sems.at[n]) for n, (a, b) in enumerate(pairs)]
    for copy in copies:
        copy.start()
    for copy in copies:
        copy.wait()


def first_kernel(incident, history, inverse, coeff, keep, send, inc, field, inv, load, sems):
    fetch([(incident.at[0], inc), (history.at[0], field), (inverse, inv), (coeff, load)], sems)
    blocks, size = inv.shape[0], inv.shape[1]
    half = blocks // 2
    solved = []
    for i in range(blocks):
        at = slice(i * size, (i + 1) * size)
        solved.append(solved_block(inc[at, :], field[at, :], in_two(inv[i]), column_of(load[i : i + 1, :])))
    shape = solved[0].shape
    left = lax.broadcasted_iota(jnp.int32, shape, 1) < shape[1] // 2
    for j in range(half):
        low, high, at = solved[j], turned(solved[j + half]), slice(j * size, (j + 1) * size)
        keep[at, :] = jnp.where(left, low, high).astype(keep.dtype)
        send[at, :] = jnp.where(left, high, low).astype(send.dtype)


def by_parity(meta, own, theirs, kept, sem):
    copies = [pltpu.make_async_copy(source, kept, sem) for source in (own, theirs)]

    def start():
        pl.when(meta[0] == 0)(copies[0].start)
        pl.when(meta[0] != 0)(copies[1].start)

    return start, copies[0].wait


def prepare_kernel(meta, incident, history, partner, own, theirs, inverse, coeff, *refs):
    count = (len(refs) - 6) // 3
    bases, incs, mats = (refs[n * count : (n + 1) * count] for n in range(3))
    inv_high, inv_low, load, inv, rows, sems = refs[3 * count :]
    pairs = [by_parity(meta, history.at[n + 1], partner.at[n + 1], bases[n], sems.at[n]) for n in range(count)]
    pairs += [by_parity(meta, own.at[n], theirs.at[n], mats[n], sems.at[count + n]) for n in range(count)]
    plain = [(inverse, inv), (coeff, rows)] + [(incident.at[n + 1], incs[n]) for n in range(count)]
    plain = [pltpu.make_async_copy(a, b, sems.at[2 * count + n]) for n, (a, b) in enumerate(plain)]
    for copy in plain:
        copy.start()
    for start, _ in pairs:
        start()
    for copy in plain:
        copy.wait()
    blocks, size = inv.shape[0], inv.shape[1]
    for i in range(blocks):
        inv_high[i], inv_low[i] = in_two(inv[i])
        load[i * size : (i + 1) * size, :] = column_of(rows[i : i + 1, :])
    for _, wait in pairs:
        wait()


def unpack_half(meta, block_of, owners, source, blocks):
    half, shape = blocks // 2, source.shape[1:]
    own = own_lanes(meta, shape)
    nothing = jnp.zeros(shape, source.dtype)
    for k in range(owners):
        for j in range(half):
            packed = block_of(k, j)
            source[k * blocks + j] = jnp.where(own, packed, nothing)
            source[k * blocks + j + half] = jnp.where(own, nothing, packed)


def chained(meta, table, swapped, base):
    return lambda s: jnp.where(meta[0] == 0, table[base + s], swapped[base + s])


def next_kernel(places, meta, table, swapped, matrix, base, inc, inv_high, inv_low, load, *refs):
    keep, joined, source = refs[-3:]
    blocks, size = inv_high.shape[0], inv_high.shape[1]
    half, nonzero = blocks // 2, matrix.shape[1] // size

    def block_of(k, j):
        which, row = places[k]
        packed = refs[which][row + j * size : row + (j + 1) * size, :]
        joined[k * half + j] = packed
        return packed

    unpack_half(meta, block_of, len(places), source, blocks)
    solved = []
    for i in range(blocks):
        at = slice(i * size, (i + 1) * size)
        listed = chained(meta, table, swapped, i * nonzero)
        total = block_product(listed, matrix, i, lambda n: source[n], size)
        field = base[at, :] + (total + turned(total))
        solved.append(solved_block(inc[at, :], field, (inv_high[i], inv_low[i]), load[at, :]))
    lanes = own_lanes(meta, solved[0].shape)
    for j in range(half):
        at = slice(j * size, (j + 1) * size)
        keep[at, :] = jnp.where(lanes, solved[j], turned(solved[j + half])).astype(keep.dtype)


def ahead_kernel(blocks, meta, table, swapped, mine, matrix, base, out, source):
    size = base.shape[0] // blocks
    half, nonzero = blocks // 2, matrix.shape[1] // size
    unpack_half(meta, lambda k, j: mine[k * half + j], mine.shape[0] // half, source, blocks)
    for i in range(blocks):
        at = slice(i * size, (i + 1) * size)
        listed = chained(meta, table, swapped, (blocks + i) * nonzero)
        total = block_product(listed, matrix, i, lambda n: source[n], size)
        out[at, :] = base[at, :] + (total + turned(total))


def unpack_whole(meta, mine, other, source, blocks, lanes=slice(None)):
    half = blocks // 2
    own = own_lanes(meta, mine.shape[1:])
    for k in range(mine.shape[0] // half):
        for j in range(half):
            a, b = mine[k * half + j], other[k * half + j]
            source[k * blocks + j, :, lanes] = jnp.where(own, a, b)
            source[k * blocks + j + half, :, lanes] = turned_exact(jnp.where(own, b, a))


def table_of(table, base):
    return lambda s: table[base + s]


def near_kernel(blocks, meta, table, mine, other, own, theirs, history, *refs):
    first, near, ahead, kept, chain, whole, source, held, acc, sems = refs
    size = acc.shape[1] // blocks
    nonzero = held.shape[1] // size
    start, wait = by_parity(meta, own.at[0], theirs.at[0], chain, sems.at[2])
    loads = [pltpu.make_async_copy(own.at[n], ref, sems.at[n]) for n, ref in enumerate((kept, held))]
    fields = pltpu.make_async_copy(history.at[pl.ds(0, acc.shape[0])], acc, sems.at[3])
    loads[0].start()
    fields.start()
    loads[1].start()
    start()
    unpack_whole(meta, mine, other, source, blocks)
    for i in range(blocks):
        whole[i * size : (i + 1) * size, :] = source[i]
    fields.wait()
    first[...] = acc[0].astype(first.dtype)
    for k, (matrix, out) in enumerate(((kept, near), (held, ahead))):
        loads[k].wait()
        for i in range(blocks):
            at = slice(i * size, (i + 1) * size)
            listed = table_of(table, (k * blocks + i) * nonzero)
            total = acc[k + 1, at, :] + block_product(listed, matrix, i, lambda n: source[n], size)
            out[at, :] = total.astype(out.dtype)
    wait()


def nearer_kernel(blocks, meta, table, mine, other, matrix, base, near, source):
    size = base.shape[0] // blocks
    nonzero = matrix.shape[1] // size
    unpack_whole(meta, mine, other, source, blocks)
    for i in range(blocks):
        at = slice(i * size, (i + 1) * size)
        listed = table_of(table, i * nonzero)
        total = base[at, :] + block_product(listed, matrix, i, lambda n: source[n], size)
        near[at, :] = total.astype(near.dtype)


def far_kernel(blocks, meta, table, mine0, other0, mine1, other1, own, history, out, mats, whole, *refs):
    source, sems = refs[0], refs[-1]
    delays, size, excite = own.shape[0], out.shape[1] // blocks, out.shape[2]
    nonzero = mats.shape[2] // size
    fields = []
    if len(refs) == 3:
        acc = refs[1]
        fields = [pltpu.make_async_copy(history.at[pl.ds(STEPS, acc.shape[0])], acc, sems.at[0])]
    loads = {k: pltpu.make_async_copy(own.at[k], mats.at[k - 1], sems.at[k]) for k in range(1, delays)}
    for copy in [loads[1]] + fields + [loads[k] for k in range(2, delays)]:
        copy.start()
    unpack_whole(meta, mine0, other0, source, blocks, slice(0, excite))
    unpack_whole(meta, mine1, other1, source, blocks, slice(excite, 2 * excite))
    for i in range(blocks):
        whole[i * size : (i + 1) * size, :] = source[i, :, excite:]
    for copy in fields:
        copy.wait()
    for k in range(1, delays):
        loads[k].wait()
        for i in range(blocks):
            at = slice(i * size, (i + 1) * size)
            listed = table_of(table, (k * blocks + i) * nonzero)
            base = acc[k + 2 - STEPS, at, :] if STEPS <= k + 2 < delays else None
            if k == 1:
                late = block_product(listed, mats.at[k - 1], i, lambda n: source[n, :, excite:], size)
            else:
                both = block_product(listed, mats.at[k - 1], i, lambda n: source[n], size)
                out[k - 2, at, :] = out[k - 2, at, :] + both[:, :excite]
                late = both[:, excite:]
            out[k - 1, at, :] = late if base is None else late + base


def last_kernel(blocks, meta, table, mine, other, kept, mats, acc, late, earlier, future, currents, *refs):
    source, out, whole, sems = refs
    delays, size = out.shape[0], acc.shape[1] // blocks
    nonzero = mats.shape[2] // size
    stores = [
        pltpu.make_async_copy(one, currents.at[n], sems.at[delays + n]) for n, one in enumerate(earlier + [whole])
    ]
    for store in stores[:-1]:
        store.start()
    unpack_whole(meta, mine, other, source, blocks)
    for i in range(blocks):
        whole[i * size : (i + 1) * size, :] = source[i]
    stores[-1].start()
    followed = meta[1] == 1
    for k in range(delays):
        for i in range(blocks):
            at = slice(i * size, (i + 1) * size)
            listed = table_of(table, (k * blocks + i) * nonzero)
            total = block_product(listed, mats.at[k - 1] if k else kept, i, lambda n: source[n], size)
            if k < acc.shape[0]:
                total = total + acc[k, at, :]
            if k >= delays - late.shape[0]:
                extra = late[k - (delays - late.shape[0]), at, :].astype(jnp.float32)
                total = total + jnp.where(followed, extra, 0.0)
            out[k, at, :] = total
        stores.append(pltpu.make_async_copy(out.at[k], future.at[k], sems.at[k]))
        stores[-1].start()
    for store in stores:
        store.wait()


def struct(shape, dtype):
    return jax.ShapeDtypeStruct(shape, dtype)


def local_paired(incident, history, couplings, block_inverse, load_coeff, pattern, wanted):
    blocks, size = block_inverse.shape[:2]
    rows, excite = incident.shape[1:]
    delays = history.shape[0]
    n_delay, n_row = lax.axis_size("delay"), lax.axis_size("row")
    d, r = lax.axis_index("delay"), lax.axis_index("row")
    parity = d % 2
    slots = wanted.shape[2]
    half = blocks // 2
    bf16, f32 = jnp.bfloat16, jnp.float32
    axes = ("delay", "row")

    def swap(value, bit):
        pairs = [(a * n_row + q, (a ^ bit) * n_row + q) for a in range(n_delay) for q in range(n_row)]
        return lax.ppermute(value, axes, pairs)

    def swap_row(value, bit):
        pairs = [(a * n_row + q, a * n_row + (q ^ bit)) for a in range(n_delay) for q in range(n_row)]
        return lax.ppermute(value, axes, pairs)

    def located(listed):
        needed = lax.dynamic_index_in_dim(wanted, r, 0, keepdims=False).reshape(-1)
        hit = listed[..., None] == jnp.arange(needed.shape[0], dtype=jnp.int32)
        block = jnp.sum(jnp.where(hit, needed, 0), -1)
        return (((listed // slots) ^ r) * blocks + block).reshape(-1)

    meta = jnp.stack([parity, (d < n_delay - 1).astype(jnp.int32)])
    load = load_coeff.reshape(blocks, size)

    packed = struct((half * size, excite), bf16)
    gathered = (n_row * half, size, excite)
    source = pltpu.VMEM((n_row * blocks, size, excite), bf16)

    def planes(value):
        bit = 2
        while bit < n_delay:
            got = swap(value, bit)
            value = jnp.where((d >= bit) & (d < 2 * bit), got, value)
            bit *= 2
        return value

    def exchange(value):
        direct, bases = row_plan(n_row)
        pieces = [None] * n_row
        pieces[0] = (value, 0)
        for k in direct:
            pieces[k] = (swap_row(value, k), 0)
        if bases:
            passed = swap_row(jnp.concatenate([pieces[k][0] for k in bases], 0), 1)
            for n, k in enumerate(bases):
                pieces[k ^ 1] = (passed, n * half * size)
        return pieces

    def gather_other(mine):
        return swap(mine, 1)

    hbm = lambda value: pltpu.with_memory_space_constraint(value, pltpu.MemorySpace.HBM)
    couplings, history, incident = map(hbm, (couplings, history, incident))
    block_inverse, load = map(hbm, (block_inverse, load))

    keep, send = pl.pallas_call(
        first_kernel,
        out_shape=[packed] * 2,
        in_specs=[HBM] * 4,
        out_specs=[VMEM] * 2,
        scratch_shapes=[
            pltpu.VMEM((rows, excite), bf16),
            pltpu.VMEM((rows, excite), f32),
            pltpu.VMEM(block_inverse.shape, f32),
            pltpu.VMEM(load.shape, f32),
            pltpu.SemaphoreType.DMA((4,)),
        ],
        compiler_params=PARAMS,
        name="first",
    )(incident, history, block_inverse, load)
    got = swap(send, 1)
    mine = jnp.where(parity == 0, keep, got)
    count = STEPS - 1
    table = located(pattern)
    theirs = hbm(swap(couplings, 1))
    partner = swap(history, 1)
    swapped = swap(table, 1)
    field, current = struct((rows, excite), f32), struct((rows, excite), bf16)
    matrix = struct(couplings.shape[1:], bf16)
    prepared = pl.pallas_call(
        prepare_kernel,
        out_shape=[field] * count
        + [current] * count
        + [matrix] * count
        + [struct(block_inverse.shape, bf16)] * 2
        + [field],
        in_specs=[SMEM, HBM, HBM, ANY] + [HBM] * 4,
        out_specs=[VMEM] * (3 * count + 3),
        scratch_shapes=[
            pltpu.VMEM(block_inverse.shape, f32),
            pltpu.VMEM(load.shape, f32),
            pltpu.SemaphoreType.DMA((3 * count + 2,)),
        ],
        compiler_params=LARGE,
        name="prepare",
    )(meta, incident, history, partner, couplings, theirs, block_inverse, load)
    bases, incs, mats = (prepared[n * count : (n + 1) * count] for n in range(3))
    inv_high, inv_low, load = prepared[3 * count :]

    def advance(step, pieces, mat, base):
        arrays = []
        places = []
        for array, row in pieces:
            seen = [n for n, one in enumerate(arrays) if one is array]
            places.append((seen[0] if seen else len(arrays), row))
            arrays += [] if seen else [array]
        return pl.pallas_call(
            functools.partial(next_kernel, places),
            out_shape=[packed, struct(gathered, bf16)],
            in_specs=[SMEM] * 3 + [VMEM] * (6 + len(arrays)),
            out_specs=[VMEM] * 2,
            scratch_shapes=[source],
            compiler_params=LARGE,
            name="next",
        )(meta, table, swapped, mat, base, incs[step], inv_high, inv_low, load, *arrays)

    def spread_out(mine):
        mine = planes(mine)
        return exchange(mine)

    pieces = spread_out(mine)
    mine, near0 = advance(0, pieces, mats[0], bases[0])
    base = pl.pallas_call(
        functools.partial(ahead_kernel, blocks),
        out_shape=field,
        in_specs=[SMEM] * 3 + [VMEM] * 3,
        out_specs=VMEM,
        scratch_shapes=[source],
        compiler_params=LARGE,
        name="ahead",
    )(meta, table, swapped, near0, mats[1], bases[1])
    other0 = gather_other(near0)
    tail, first_tail, ahead, kept, chain, whole0 = pl.pallas_call(
        functools.partial(near_kernel, blocks),
        out_shape=[current, current, field, matrix, matrix, current],
        in_specs=[SMEM, SMEM, VMEM, VMEM, HBM, HBM, HBM],
        out_specs=[VMEM] * 6,
        scratch_shapes=[
            source,
            pltpu.VMEM(couplings.shape[1:], bf16),
            pltpu.VMEM((STEPS, rows, excite), f32),
            pltpu.SemaphoreType.DMA((4,)),
        ],
        compiler_params=LARGE,
        name="near",
    )(meta, table, near0, other0, couplings, theirs, history)

    pieces = spread_out(mine)
    mine, near1 = advance(1, pieces, chain, base)
    other1 = gather_other(near1)
    second_tail = pl.pallas_call(
        functools.partial(nearer_kernel, blocks),
        out_shape=current,
        in_specs=[SMEM] * 2 + [VMEM] * 4,
        out_specs=VMEM,
        scratch_shapes=[source],
        compiler_params=LARGE,
        name="nearer",
    )(meta, table, near1, other1, kept, ahead)
    acc, mats, whole1 = pl.pallas_call(
        functools.partial(far_kernel, blocks),
        out_shape=[struct((delays - 1, rows, excite), f32), struct((delays - 1,) + couplings.shape[1:], bf16), current],
        in_specs=[SMEM] * 2 + [VMEM] * 4 + [HBM] * 2,
        out_specs=[VMEM] * 3,
        scratch_shapes=[pltpu.VMEM((n_row * blocks, size, 2 * excite), bf16)]
        + [pltpu.VMEM((delays - STEPS, rows, excite), f32)] * (delays > STEPS)
        + [pltpu.SemaphoreType.DMA((delays,))],
        compiler_params=LARGE,
        name="far",
    )(meta, table, near0, other0, near1, other1, couplings, history)
    tails = [tail, first_tail, second_tail]
    back = [(a * n_row + q, ((a - 1) % n_delay) * n_row + q) for a in range(n_delay) for q in range(n_row)]
    late = lax.ppermute(jnp.stack(tails), axes, back)

    pieces = spread_out(mine)
    near2 = jnp.concatenate([array[row : row + half * size] for array, row in pieces], 0).reshape(gathered)
    other2 = gather_other(near2)

    def finish(*refs):
        last_kernel(blocks, *refs[:8], list(refs[8:10]), *refs[10:])

    future, currents = pl.pallas_call(
        finish,
        out_shape=[struct(history.shape, f32), struct((STEPS, rows, excite), bf16)],
        in_specs=[SMEM] * 2 + [VMEM] * 8,
        out_specs=[HBM] * 2,
        scratch_shapes=[
            source,
            pltpu.VMEM(history.shape, f32),
            pltpu.VMEM((rows, excite), bf16),
            pltpu.SemaphoreType.DMA((delays + STEPS,)),
        ],
        compiler_params=LARGE,
        name="last",
    )(meta, table, near2, other2, kept, mats, acc, late, whole0, whole1)
    return currents, future


def fits(mesh, blocks, delays):
    sizes = (mesh.shape["delay"], mesh.shape["row"])
    powers = all(n >= 2 and n & (n - 1) == 0 for n in sizes)
    return powers and blocks % 2 == 0 and delays >= STEPS and STEPS == 3


def row_plan(n_row):
    bases = sorted({n_row // 2, 2} - {1}, reverse=True) if n_row > 2 else []
    far = [k for k in range(n_row // 2, n_row) if k ^ 1 not in bases and k not in bases]
    near = [k for k in range(2, n_row // 2) if k ^ 1 not in bases and k not in bases]
    return bases + far + near + [1], bases


def solution(mesh):
    in_specs = (
        P(None, "row", None),
        P("delay", "row", None),
        P("delay", "row", None),
        P("row", None, None),
        P("row"),
        P("delay", "row", None),
        P(),
    )
    out_specs = (P(None, "row", None), P("delay", "row", None))

    def local(*args):
        if not fits(mesh, args[3].shape[0], args[1].shape[0]):
            return local_general(*args)
        return local_paired(*args)

    return jax.shard_map(local, mesh=mesh, in_specs=in_specs, out_specs=out_specs, check_vma=False)
```

```python
import functools

import jax
import jax.numpy as jnp
from jax import lax
from jax.experimental import pallas as pl
from jax.experimental.pallas import tpu as pltpu
from jax.sharding import PartitionSpec as P

STEPS = 3


def passed_along(value, axis, steps):
    count = lax.axis_size(axis)
    leading, last = (max(0, -steps), min(count, count - steps))
    return lax.ppermute(value, axis, [(source, source + steps) for source in range(leading, last)])


def spread(value, axis, source):
    kept = jnp.where(lax.axis_index(axis) == source, value, 0).astype(value.dtype)
    return lax.psum(kept, axis)


def solve_step(incoming, field, block_inverse, load_coeff):
    blk_rows = block_inverse.shape[0]
    size_blk = block_inverse.shape[1]
    rhs = incoming.astype(jnp.float32) - field
    solved = jnp.einsum(
        "iab,ibc->iac",
        block_inverse,
        rhs.reshape(blk_rows, size_blk, rhs.shape[1]),
        precision=lax.Precision.HIGHEST,
    ).reshape(rhs.shape)
    return (solved - load_coeff[:, None] * solved * solved * solved).astype(jnp.bfloat16)


def local_general(incident, history, couplings, block_inverse, load_coeff, pattern, wanted):
    blk_rows = block_inverse.shape[0]
    size_blk = block_inverse.shape[1]
    excite = incident.shape[2]
    local_delays = history.shape[0]
    nonzero = couplings.shape[2] // size_blk
    owners = lax.axis_size("row")
    owner = lax.axis_index("row")
    slots = wanted.shape[2]
    zmats = couplings.reshape(local_delays, blk_rows, size_blk, nonzero * size_blk)
    outgoing = lax.dynamic_index_in_dim(wanted, owner, 1, keepdims=False)
    send_index = jnp.maximum(outgoing, 0)
    send_live = outgoing >= 0
    acc = history
    outputs = []
    for step in range(STEPS):
        nearest = passed_along(acc[0].astype(jnp.bfloat16), "delay", -1).astype(jnp.float32)
        current = solve_step(incident[step], acc[0], block_inverse, load_coeff)
        current = spread(current, "delay", 0)
        blocks = current.reshape(blk_rows, size_blk, excite)
        parcels = jnp.where(
            send_live[:, :, None, None], blocks[send_index], jnp.zeros((), jnp.bfloat16)
        )
        received = lax.all_to_all(parcels, "row", split_axis=0, concat_axis=0, tiled=True)
        source = received.reshape(owners * slots, size_blk, excite)
        picked = source[pattern].reshape(local_delays, blk_rows, nonzero * size_blk, excite)
        products = jnp.einsum("krab,krbc->krac", zmats, picked, preferred_element_type=jnp.float32)
        products = products.reshape(local_delays, blk_rows * size_blk, excite)
        acc = jnp.concatenate([acc[1:], nearest[None]], 0) + products
        outputs.append(current)
    return (jnp.stack(outputs), acc)


VMEM = pl.BlockSpec(memory_space=pltpu.VMEM)
SMEM = pl.BlockSpec(memory_space=pltpu.SMEM)
HBM = pl.BlockSpec(memory_space=pltpu.HBM)
PARAMS = pltpu.CompilerParams(vmem_limit_bytes=8 * 1024 * 1024)
LARGE = pltpu.CompilerParams(vmem_limit_bytes=16 * 1024 * 1024)


def column_of(row_vector):
    size = row_vector.shape[1]
    rows = lax.broadcasted_iota(jnp.int32, (size, size), 0)
    cols = lax.broadcasted_iota(jnp.int32, (size, size), 1)
    spread_out = jnp.where(rows == cols, jnp.broadcast_to(row_vector, (size, size)), 0.0)
    return jnp.broadcast_to(jnp.sum(spread_out, axis=1, keepdims=True), (size, size))


def in_two(value):
    high = value.astype(jnp.bfloat16)
    return high, (value - high.astype(jnp.float32)).astype(jnp.bfloat16)


def solved_block(incoming, field, inverse, load):
    rhs = in_two(incoming.astype(jnp.float32) - field)
    dot = functools.partial(jnp.dot, preferred_element_type=jnp.float32)
    y = dot(inverse[0], rhs[0]) + (dot(inverse[0], rhs[1]) + dot(inverse[1], rhs[0]))
    return y - load * y * y * y


def turned(value):
    return pltpu.roll(value, value.shape[-1] // 2, value.ndim - 1)


def turned_exact(value):
    return turned(value.astype(jnp.float32)).astype(value.dtype)


def own_lanes(meta, shape):
    lane = lax.broadcasted_iota(jnp.int32, shape, 1)
    return (lane < shape[1] // 2) == (meta[0] == 0)


def block_product(listed, matrix, row, block_of, size):
    nonzero = matrix.shape[1] // size
    total = None
    for s in range(0, nonzero, 2):
        pair = jnp.concatenate([block_of(listed(s)), block_of(listed(s + 1))], 0)
        part = jnp.dot(
            matrix[row * size : (row + 1) * size, s * size : (s + 2) * size],
            pair,
            preferred_element_type=jnp.float32,
        )
        total = part if total is None else total + part
    return total


def fetch(pairs, sems):
    copies = [pltpu.make_async_copy(a, b, sems.at[n]) for n, (a, b) in enumerate(pairs)]
    for copy in copies:
        copy.start()
    for copy in copies:
        copy.wait()


def first_kernel(incident, history, inverse, coeff, keep, send, inc, field, inv, load, sems):
    fetch([(incident.at[0], inc), (history.at[0], field), (inverse, inv), (coeff, load)], sems)
    blocks, size = inv.shape[0], inv.shape[1]
    half = blocks // 2
    solved = []
    for i in range(blocks):
        at = slice(i * size, (i + 1) * size)
        solved.append(solved_block(inc[at, :], field[at, :], in_two(inv[i]), column_of(load[i : i + 1, :])))
    shape = solved[0].shape
    left = lax.broadcasted_iota(jnp.int32, shape, 1) < shape[1] // 2
    for j in range(half):
        low, high, at = solved[j], turned(solved[j + half]), slice(j * size, (j + 1) * size)
        keep[at, :] = jnp.where(left, low, high).astype(keep.dtype)
        send[at, :] = jnp.where(left, high, low).astype(send.dtype)


def by_parity(meta, own, theirs, kept, sem):
    copies = [pltpu.make_async_copy(source, kept, sem) for source in (own, theirs)]

    def start():
        pl.when(meta[0] == 0)(copies[0].start)
        pl.when(meta[0] != 0)(copies[1].start)

    return start, copies[0].wait


def prepare_kernel(meta, incident, history, partner, own, theirs, inverse, coeff, *refs):
    count = (len(refs) - 6) // 3
    bases, incs, mats = (refs[n * count : (n + 1) * count] for n in range(3))
    inv_high, inv_low, load, inv, rows, sems = refs[3 * count :]
    pairs = [by_parity(meta, history.at[n + 1], partner.at[n + 1], bases[n], sems.at[n]) for n in range(count)]
    pairs += [by_parity(meta, own.at[n], theirs.at[n], mats[n], sems.at[count + n]) for n in range(count)]
    plain = [(inverse, inv), (coeff, rows)] + [(incident.at[n + 1], incs[n]) for n in range(count)]
    plain = [pltpu.make_async_copy(a, b, sems.at[2 * count + n]) for n, (a, b) in enumerate(plain)]
    for copy in plain:
        copy.start()
    for start, _ in pairs:
        start()
    for copy in plain:
        copy.wait()
    blocks, size = inv.shape[0], inv.shape[1]
    for i in range(blocks):
        inv_high[i], inv_low[i] = in_two(inv[i])
        load[i * size : (i + 1) * size, :] = column_of(rows[i : i + 1, :])
    for _, wait in pairs:
        wait()


def unpack_half(meta, block_of, owners, source, blocks):
    half, shape = blocks // 2, source.shape[1:]
    own = own_lanes(meta, shape)
    nothing = jnp.zeros(shape, source.dtype)
    for k in range(owners):
        for j in range(half):
            packed = block_of(k, j)
            source[k * blocks + j] = jnp.where(own, packed, nothing)
            source[k * blocks + j + half] = jnp.where(own, nothing, packed)


def chained(meta, table, swapped, base):
    return lambda s: jnp.where(meta[0] == 0, table[base + s], swapped[base + s])


def next_kernel(places, meta, table, swapped, matrix, base, inc, inv_high, inv_low, load, *refs):
    keep, joined, source = refs[-3:]
    blocks, size = inv_high.shape[0], inv_high.shape[1]
    half, nonzero = blocks // 2, matrix.shape[1] // size

    def block_of(k, j):
        which, row = places[k]
        packed = refs[which][row + j * size : row + (j + 1) * size, :]
        joined[k * half + j] = packed
        return packed

    unpack_half(meta, block_of, len(places), source, blocks)
    solved = []
    for i in range(blocks):
        at = slice(i * size, (i + 1) * size)
        listed = chained(meta, table, swapped, i * nonzero)
        total = block_product(listed, matrix, i, lambda n: source[n], size)
        field = base[at, :] + (total + turned(total))
        solved.append(solved_block(inc[at, :], field, (inv_high[i], inv_low[i]), load[at, :]))
    lanes = own_lanes(meta, solved[0].shape)
    for j in range(half):
        at = slice(j * size, (j + 1) * size)
        keep[at, :] = jnp.where(lanes, solved[j], turned(solved[j + half])).astype(keep.dtype)


def ahead_kernel(blocks, meta, table, swapped, mine, matrix, base, out, source):
    size = base.shape[0] // blocks
    half, nonzero = blocks // 2, matrix.shape[1] // size
    unpack_half(meta, lambda k, j: mine[k * half + j], mine.shape[0] // half, source, blocks)
    for i in range(blocks):
        at = slice(i * size, (i + 1) * size)
        listed = chained(meta, table, swapped, (blocks + i) * nonzero)
        total = block_product(listed, matrix, i, lambda n: source[n], size)
        out[at, :] = base[at, :] + (total + turned(total))


def unpack_whole(meta, mine, other, source, blocks, lanes=slice(None)):
    half = blocks // 2
    own = own_lanes(meta, mine.shape[1:])
    for k in range(mine.shape[0] // half):
        for j in range(half):
            a, b = mine[k * half + j], other[k * half + j]
            source[k * blocks + j, :, lanes] = jnp.where(own, a, b)
            source[k * blocks + j + half, :, lanes] = turned_exact(jnp.where(own, b, a))


def table_of(table, base):
    return lambda s: table[base + s]


def near_kernel(blocks, meta, table, mine, other, own, history, *refs):
    first, near, ahead, kept0, kept1, whole, source, acc, sems = refs
    size = acc.shape[1] // blocks
    nonzero = kept0.shape[1] // size
    loads = [pltpu.make_async_copy(own.at[n], ref, sems.at[n]) for n, ref in enumerate((kept0, kept1))]
    fields = pltpu.make_async_copy(history.at[pl.ds(0, acc.shape[0])], acc, sems.at[2])
    for copy in (loads[0], fields, loads[1]):
        copy.start()
    unpack_whole(meta, mine, other, source, blocks)
    for i in range(blocks):
        whole[i * size : (i + 1) * size, :] = source[i]
    for copy in (loads[0], fields):
        copy.wait()
    for k, (matrix, out) in enumerate(((kept0, near), (kept1, ahead))):
        if k == 1:
            loads[1].wait()
        for i in range(blocks):
            at = slice(i * size, (i + 1) * size)
            listed = table_of(table, (k * blocks + i) * nonzero)
            total = acc[k + 1, at, :] + block_product(listed, matrix, i, lambda n: source[n], size)
            out[at, :] = total.astype(out.dtype)
    first[...] = acc[0].astype(first.dtype)


def nearer_kernel(blocks, meta, table, mine, other, matrix, base, near, source):
    size = base.shape[0] // blocks
    nonzero = matrix.shape[1] // size
    unpack_whole(meta, mine, other, source, blocks)
    for i in range(blocks):
        at = slice(i * size, (i + 1) * size)
        listed = table_of(table, i * nonzero)
        total = base[at, :] + block_product(listed, matrix, i, lambda n: source[n], size)
        near[at, :] = total.astype(near.dtype)


def far_kernel(blocks, meta, table, mine0, other0, mine1, other1, kept, own, history, out, mats, whole, *refs):
    source, sems = refs[0], refs[-1]
    delays, size, excite = own.shape[0], out.shape[1] // blocks, out.shape[2]
    nonzero = mats.shape[2] // size
    fields = []
    if len(refs) == 3:
        acc = refs[1]
        fields = [pltpu.make_async_copy(history.at[pl.ds(STEPS, acc.shape[0])], acc, sems.at[0])]
    loads = {k: pltpu.make_async_copy(own.at[k], mats.at[k - 2], sems.at[k]) for k in range(2, delays)}
    for copy in fields + list(loads.values()):
        copy.start()
    unpack_whole(meta, mine0, other0, source, blocks, slice(0, excite))
    unpack_whole(meta, mine1, other1, source, blocks, slice(excite, 2 * excite))
    for i in range(blocks):
        whole[i * size : (i + 1) * size, :] = source[i, :, excite:]
    for copy in fields:
        copy.wait()
    for k in range(1, delays):
        matrix = kept if k == 1 else mats.at[k - 2]
        if k > 1:
            loads[k].wait()
        for i in range(blocks):
            at = slice(i * size, (i + 1) * size)
            listed = table_of(table, (k * blocks + i) * nonzero)
            base = acc[k + 2 - STEPS, at, :] if STEPS <= k + 2 < delays else None
            if k == 1:
                late = block_product(listed, matrix, i, lambda n: source[n, :, excite:], size)
            else:
                both = block_product(listed, matrix, i, lambda n: source[n], size)
                out[k - 2, at, :] = out[k - 2, at, :] + both[:, :excite]
                late = both[:, excite:]
            out[k - 1, at, :] = late if base is None else late + base


def last_kernel(blocks, meta, table, mine, other, kept0, kept1, mats, acc, late, earlier, future, currents, *refs):
    source, out, whole, sems = refs
    delays, size = out.shape[0], acc.shape[1] // blocks
    nonzero = mats.shape[2] // size
    stores = [
        pltpu.make_async_copy(one, currents.at[n], sems.at[delays + n]) for n, one in enumerate(earlier + [whole])
    ]
    for store in stores[:-1]:
        store.start()
    unpack_whole(meta, mine, other, source, blocks)
    for i in range(blocks):
        whole[i * size : (i + 1) * size, :] = source[i]
    stores[-1].start()
    followed = meta[1] == 1
    matrices = [kept0, kept1] + [mats.at[k] for k in range(mats.shape[0])]
    for k in range(delays):
        for i in range(blocks):
            at = slice(i * size, (i + 1) * size)
            listed = table_of(table, (k * blocks + i) * nonzero)
            total = block_product(listed, matrices[k], i, lambda n: source[n], size)
            if k < acc.shape[0]:
                total = total + acc[k, at, :]
            if k >= delays - late.shape[0]:
                extra = late[k - (delays - late.shape[0]), at, :].astype(jnp.float32)
                total = total + jnp.where(followed, extra, 0.0)
            out[k, at, :] = total
        stores.append(pltpu.make_async_copy(out.at[k], future.at[k], sems.at[k]))
        stores[-1].start()
    for store in stores:
        store.wait()


def struct(shape, dtype):
    return jax.ShapeDtypeStruct(shape, dtype)


def local_paired(incident, history, couplings, block_inverse, load_coeff, pattern, wanted):
    blocks, size = block_inverse.shape[:2]
    rows, excite = incident.shape[1:]
    delays = history.shape[0]
    n_delay, n_row = lax.axis_size("delay"), lax.axis_size("row")
    d, r = lax.axis_index("delay"), lax.axis_index("row")
    parity = d % 2
    slots = wanted.shape[2]
    half = blocks // 2
    bf16, f32 = jnp.bfloat16, jnp.float32
    axes = ("delay", "row")

    def swap(value, bit):
        pairs = [(a * n_row + q, (a ^ bit) * n_row + q) for a in range(n_delay) for q in range(n_row)]
        return lax.ppermute(value, axes, pairs)

    def swap_row(value, bit):
        pairs = [(a * n_row + q, a * n_row + (q ^ bit)) for a in range(n_delay) for q in range(n_row)]
        return lax.ppermute(value, axes, pairs)

    def located(listed):
        needed = lax.dynamic_index_in_dim(wanted, r, 0, keepdims=False).reshape(-1)
        hit = listed[..., None] == jnp.arange(needed.shape[0], dtype=jnp.int32)
        block = jnp.sum(jnp.where(hit, needed, 0), -1)
        return (((listed // slots) ^ r) * blocks + block).reshape(-1)

    meta = jnp.stack([parity, (d < n_delay - 1).astype(jnp.int32)])
    load = load_coeff.reshape(blocks, size)

    packed = struct((half * size, excite), bf16)
    gathered = (n_row * half, size, excite)
    source = pltpu.VMEM((n_row * blocks, size, excite), bf16)

    def planes(value):
        bit = 2
        while bit < n_delay:
            got = swap(value, bit)
            value = jnp.where((d >= bit) & (d < 2 * bit), got, value)
            bit *= 2
        return value

    def exchange(value):
        direct, bases = row_plan(n_row)
        pieces = [None] * n_row
        pieces[0] = (value, 0)
        for k in direct:
            pieces[k] = (swap_row(value, k), 0)
        if bases:
            passed = swap_row(jnp.concatenate([pieces[k][0] for k in bases], 0), 1)
            for n, k in enumerate(bases):
                pieces[k ^ 1] = (passed, n * half * size)
        return pieces

    def gather_other(mine):
        return swap(mine, 1)

    hbm = lambda value: pltpu.with_memory_space_constraint(value, pltpu.MemorySpace.HBM)
    couplings, history, incident = map(hbm, (couplings, history, incident))
    block_inverse, load = map(hbm, (block_inverse, load))

    keep, send = pl.pallas_call(
        first_kernel,
        out_shape=[packed] * 2,
        in_specs=[HBM] * 4,
        out_specs=[VMEM] * 2,
        scratch_shapes=[
            pltpu.VMEM((rows, excite), bf16),
            pltpu.VMEM((rows, excite), f32),
            pltpu.VMEM(block_inverse.shape, f32),
            pltpu.VMEM(load.shape, f32),
            pltpu.SemaphoreType.DMA((4,)),
        ],
        compiler_params=PARAMS,
        name="first",
    )(incident, history, block_inverse, load)
    got = swap(send, 1)
    mine = jnp.where(parity == 0, keep, got)
    count = STEPS - 1
    table = located(pattern)
    theirs = hbm(swap(couplings, 1))
    partner = swap(history, 1)
    swapped = swap(table, 1)
    field, current = struct((rows, excite), f32), struct((rows, excite), bf16)
    matrix = struct(couplings.shape[1:], bf16)
    prepared = pl.pallas_call(
        prepare_kernel,
        out_shape=[field] * count
        + [current] * count
        + [matrix] * count
        + [struct(block_inverse.shape, bf16)] * 2
        + [field],
        in_specs=[SMEM, HBM, HBM, VMEM] + [HBM] * 4,
        out_specs=[VMEM] * (3 * count + 3),
        scratch_shapes=[
            pltpu.VMEM(block_inverse.shape, f32),
            pltpu.VMEM(load.shape, f32),
            pltpu.SemaphoreType.DMA((3 * count + 2,)),
        ],
        compiler_params=LARGE,
        name="prepare",
    )(meta, incident, history, partner, couplings, theirs, block_inverse, load)
    bases, incs, mats = (prepared[n * count : (n + 1) * count] for n in range(3))
    inv_high, inv_low, load = prepared[3 * count :]

    def advance(step, pieces, mat, base):
        arrays = []
        places = []
        for array, row in pieces:
            seen = [n for n, one in enumerate(arrays) if one is array]
            places.append((seen[0] if seen else len(arrays), row))
            arrays += [] if seen else [array]
        return pl.pallas_call(
            functools.partial(next_kernel, places),
            out_shape=[packed, struct(gathered, bf16)],
            in_specs=[SMEM] * 3 + [VMEM] * (6 + len(arrays)),
            out_specs=[VMEM] * 2,
            scratch_shapes=[source],
            compiler_params=LARGE,
            name="next",
        )(meta, table, swapped, mat, base, incs[step], inv_high, inv_low, load, *arrays)

    def spread_out(mine):
        mine = planes(mine)
        return exchange(mine)

    pieces = spread_out(mine)
    mine, near0 = advance(0, pieces, mats[0], bases[0])
    base = pl.pallas_call(
        functools.partial(ahead_kernel, blocks),
        out_shape=field,
        in_specs=[SMEM] * 3 + [VMEM] * 3,
        out_specs=VMEM,
        scratch_shapes=[source],
        compiler_params=LARGE,
        name="ahead",
    )(meta, table, swapped, near0, mats[1], bases[1])
    other0 = gather_other(near0)
    tail, first_tail, ahead, kept, kept1, whole0 = pl.pallas_call(
        functools.partial(near_kernel, blocks),
        out_shape=[current, current, field, matrix, matrix, current],
        in_specs=[SMEM, SMEM, VMEM, VMEM, HBM, HBM],
        out_specs=[VMEM] * 6,
        scratch_shapes=[
            source,
            pltpu.VMEM((STEPS, rows, excite), f32),
            pltpu.SemaphoreType.DMA((3,)),
        ],
        compiler_params=LARGE,
        name="near",
    )(meta, table, near0, other0, couplings, history)

    pieces = spread_out(mine)
    mine, near1 = advance(1, pieces, mats[0], base)
    other1 = gather_other(near1)
    second_tail = pl.pallas_call(
        functools.partial(nearer_kernel, blocks),
        out_shape=current,
        in_specs=[SMEM] * 2 + [VMEM] * 4,
        out_specs=VMEM,
        scratch_shapes=[source],
        compiler_params=LARGE,
        name="nearer",
    )(meta, table, near1, other1, kept, ahead)
    acc, mats, whole1 = pl.pallas_call(
        functools.partial(far_kernel, blocks),
        out_shape=[struct((delays - 1, rows, excite), f32), struct((delays - 2,) + couplings.shape[1:], bf16), current],
        in_specs=[SMEM] * 2 + [VMEM] * 5 + [HBM] * 2,
        out_specs=[VMEM] * 3,
        scratch_shapes=[pltpu.VMEM((n_row * blocks, size, 2 * excite), bf16)]
        + [pltpu.VMEM((delays - STEPS, rows, excite), f32)] * (delays > STEPS)
        + [pltpu.SemaphoreType.DMA((delays,))],
        compiler_params=LARGE,
        name="far",
    )(meta, table, near0, other0, near1, other1, kept1, couplings, history)
    tails = [tail, first_tail, second_tail]
    back = [(a * n_row + q, ((a - 1) % n_delay) * n_row + q) for a in range(n_delay) for q in range(n_row)]
    late = lax.ppermute(jnp.stack(tails), axes, back)

    pieces = spread_out(mine)
    near2 = jnp.concatenate([array[row : row + half * size] for array, row in pieces], 0).reshape(gathered)
    other2 = gather_other(near2)

    def finish(*refs):
        last_kernel(blocks, *refs[:9], list(refs[9:11]), *refs[11:])

    future, currents = pl.pallas_call(
        finish,
        out_shape=[struct(history.shape, f32), struct((STEPS, rows, excite), bf16)],
        in_specs=[SMEM] * 2 + [VMEM] * 9,
        out_specs=[HBM] * 2,
        scratch_shapes=[
            source,
            pltpu.VMEM(history.shape, f32),
            pltpu.VMEM((rows, excite), bf16),
            pltpu.SemaphoreType.DMA((delays + STEPS,)),
        ],
        compiler_params=LARGE,
        name="last",
    )(meta, table, near2, other2, kept, kept1, mats, acc, late, whole0, whole1)
    return currents, future


def fits(mesh, blocks, delays):
    sizes = (mesh.shape["delay"], mesh.shape["row"])
    powers = all(n >= 2 and n & (n - 1) == 0 for n in sizes)
    return powers and blocks % 2 == 0 and delays >= STEPS and STEPS == 3


def row_plan(n_row):
    bases = sorted({n_row // 2, 2} - {1}, reverse=True) if n_row > 2 else []
    far = [k for k in range(n_row // 2, n_row) if k ^ 1 not in bases and k not in bases]
    near = [k for k in range(2, n_row // 2) if k ^ 1 not in bases and k not in bases]
    return bases + far + near + [1], bases


def solution(mesh):
    in_specs = (
        P(None, "row", None),
        P("delay", "row", None),
        P("delay", "row", None),
        P("row", None, None),
        P("row"),
        P("delay", "row", None),
        P(),
    )
    out_specs = (P(None, "row", None), P("delay", "row", None))

    def local(*args):
        if not fits(mesh, args[3].shape[0], args[1].shape[0]):
            return local_general(*args)
        return local_paired(*args)

    return jax.shard_map(local, mesh=mesh, in_specs=in_specs, out_specs=out_specs, check_vma=False)
```

```python
import functools

import jax
import jax.numpy as jnp
from jax import lax
from jax.experimental import pallas as pl
from jax.experimental.pallas import tpu as pltpu
from jax.sharding import PartitionSpec as P

STEPS = 3


def passed_along(value, axis, steps):
    count = lax.axis_size(axis)
    leading, last = (max(0, -steps), min(count, count - steps))
    return lax.ppermute(value, axis, [(source, source + steps) for source in range(leading, last)])


def spread(value, axis, source):
    kept = jnp.where(lax.axis_index(axis) == source, value, 0).astype(value.dtype)
    return lax.psum(kept, axis)


def solve_step(incoming, field, block_inverse, load_coeff):
    blk_rows = block_inverse.shape[0]
    size_blk = block_inverse.shape[1]
    rhs = incoming.astype(jnp.float32) - field
    solved = jnp.einsum(
        "iab,ibc->iac",
        block_inverse,
        rhs.reshape(blk_rows, size_blk, rhs.shape[1]),
        precision=lax.Precision.HIGHEST,
    ).reshape(rhs.shape)
    return (solved - load_coeff[:, None] * solved * solved * solved).astype(jnp.bfloat16)


def local_general(incident, history, couplings, block_inverse, load_coeff, pattern, wanted):
    blk_rows = block_inverse.shape[0]
    size_blk = block_inverse.shape[1]
    excite = incident.shape[2]
    local_delays = history.shape[0]
    nonzero = couplings.shape[2] // size_blk
    owners = lax.axis_size("row")
    owner = lax.axis_index("row")
    slots = wanted.shape[2]
    zmats = couplings.reshape(local_delays, blk_rows, size_blk, nonzero * size_blk)
    outgoing = lax.dynamic_index_in_dim(wanted, owner, 1, keepdims=False)
    send_index = jnp.maximum(outgoing, 0)
    send_live = outgoing >= 0
    acc = history
    outputs = []
    for step in range(STEPS):
        nearest = passed_along(acc[0].astype(jnp.bfloat16), "delay", -1).astype(jnp.float32)
        current = solve_step(incident[step], acc[0], block_inverse, load_coeff)
        current = spread(current, "delay", 0)
        blocks = current.reshape(blk_rows, size_blk, excite)
        parcels = jnp.where(
            send_live[:, :, None, None], blocks[send_index], jnp.zeros((), jnp.bfloat16)
        )
        received = lax.all_to_all(parcels, "row", split_axis=0, concat_axis=0, tiled=True)
        source = received.reshape(owners * slots, size_blk, excite)
        picked = source[pattern].reshape(local_delays, blk_rows, nonzero * size_blk, excite)
        products = jnp.einsum("krab,krbc->krac", zmats, picked, preferred_element_type=jnp.float32)
        products = products.reshape(local_delays, blk_rows * size_blk, excite)
        acc = jnp.concatenate([acc[1:], nearest[None]], 0) + products
        outputs.append(current)
    return (jnp.stack(outputs), acc)


VMEM = pl.BlockSpec(memory_space=pltpu.VMEM)
SMEM = pl.BlockSpec(memory_space=pltpu.SMEM)
HBM = pl.BlockSpec(memory_space=pltpu.HBM)
PARAMS = pltpu.CompilerParams(vmem_limit_bytes=8 * 1024 * 1024)
LARGE = pltpu.CompilerParams(vmem_limit_bytes=16 * 1024 * 1024)


def column_of(row_vector):
    size = row_vector.shape[1]
    rows = lax.broadcasted_iota(jnp.int32, (size, size), 0)
    cols = lax.broadcasted_iota(jnp.int32, (size, size), 1)
    spread_out = jnp.where(rows == cols, jnp.broadcast_to(row_vector, (size, size)), 0.0)
    return jnp.broadcast_to(jnp.sum(spread_out, axis=1, keepdims=True), (size, size))


def in_two(value):
    high = value.astype(jnp.bfloat16)
    return high, (value - high.astype(jnp.float32)).astype(jnp.bfloat16)


def solved_block(incoming, field, inverse, load):
    rhs = in_two(incoming.astype(jnp.float32) - field)
    dot = functools.partial(jnp.dot, preferred_element_type=jnp.float32)
    y = dot(inverse[0], rhs[0]) + (dot(inverse[0], rhs[1]) + dot(inverse[1], rhs[0]))
    return y - load * y * y * y


def turned(value):
    return pltpu.roll(value, value.shape[-1] // 2, value.ndim - 1)


def turned_exact(value):
    return turned(value.astype(jnp.float32)).astype(value.dtype)


def own_lanes(meta, shape):
    lane = lax.broadcasted_iota(jnp.int32, shape, 1)
    return (lane < shape[1] // 2) == (meta[0] == 0)


def block_product(listed, matrix, row, block_of, size):
    nonzero = matrix.shape[1] // size
    total = None
    for s in range(0, nonzero, 2):
        pair = jnp.concatenate([block_of(listed(s)), block_of(listed(s + 1))], 0)
        part = jnp.dot(
            matrix[row * size : (row + 1) * size, s * size : (s + 2) * size],
            pair,
            preferred_element_type=jnp.float32,
        )
        total = part if total is None else total + part
    return total


def fetch(pairs, sems, later):
    copies = [pltpu.make_async_copy(a, b, sems.at[n]) for n, (a, b) in enumerate(pairs)]
    for copy in copies + [later]:
        copy.start()
    for copy in copies:
        copy.wait()


def first_kernel(incident, history, inverse, coeff, keep, send, bases, inc, field, inv, load, sems):
    later = pltpu.make_async_copy(history.at[pl.ds(1, bases.shape[0])], bases, sems.at[4])
    fetch([(incident.at[0], inc), (history.at[0], field), (inverse, inv), (coeff, load)], sems, later)
    blocks, size = inv.shape[0], inv.shape[1]
    half = blocks // 2
    solved = []
    for i in range(blocks):
        at = slice(i * size, (i + 1) * size)
        solved.append(solved_block(inc[at, :], field[at, :], in_two(inv[i]), column_of(load[i : i + 1, :])))
    shape = solved[0].shape
    left = lax.broadcasted_iota(jnp.int32, shape, 1) < shape[1] // 2
    for j in range(half):
        low, high, at = solved[j], turned(solved[j + half]), slice(j * size, (j + 1) * size)
        keep[at, :] = jnp.where(left, low, high).astype(keep.dtype)
        send[at, :] = jnp.where(left, high, low).astype(send.dtype)
    later.wait()


def by_parity(meta, own, theirs, kept, sem):
    copies = [pltpu.make_async_copy(source, kept, sem) for source in (own, theirs)]

    def start():
        pl.when(meta[0] == 0)(copies[0].start)
        pl.when(meta[0] != 0)(copies[1].start)

    return start, copies[0].wait


def prepare_kernel(meta, incident, own, theirs, inverse, coeff, *refs):
    count = (len(refs) - 6) // 2
    incs, mats = refs[:count], refs[count : 2 * count]
    inv_high, inv_low, load, inv, rows, sems = refs[2 * count :]
    pairs = [by_parity(meta, own.at[n], theirs.at[n], mats[n], sems.at[n]) for n in range(count)]
    plain = [(inverse, inv), (coeff, rows)] + [(incident.at[n + 1], incs[n]) for n in range(count)]
    plain = [pltpu.make_async_copy(a, b, sems.at[count + n]) for n, (a, b) in enumerate(plain)]
    for copy in plain:
        copy.start()
    for start, _ in pairs:
        start()
    for copy in plain:
        copy.wait()
    blocks, size = inv.shape[0], inv.shape[1]
    for i in range(blocks):
        inv_high[i], inv_low[i] = in_two(inv[i])
        load[i * size : (i + 1) * size, :] = column_of(rows[i : i + 1, :])
    for _, wait in pairs:
        wait()


def unpack_half(meta, block_of, owners, source, blocks):
    half, shape = blocks // 2, source.shape[1:]
    own = own_lanes(meta, shape)
    nothing = jnp.zeros(shape, source.dtype)
    for k in range(owners):
        for j in range(half):
            packed = block_of(k, j)
            source[k * blocks + j] = jnp.where(own, packed, nothing)
            source[k * blocks + j + half] = jnp.where(own, nothing, packed)


def chained(meta, table, swapped, base):
    return lambda s: jnp.where(meta[0] == 0, table[base + s], swapped[base + s])


def base_of(meta, bases, at):
    own, partner, n = bases
    return own[at, :] if partner is None else jnp.where(meta[0] == 0, own[n, at, :], partner[n, at, :])


def next_kernel(places, own_base, meta, table, swapped, matrix, base, partner, inc, inv_high, inv_low, load, *refs):
    keep, joined, source = refs[-3:]
    bases = (base, None, 0) if own_base else (base, partner, 0)
    blocks, size = inv_high.shape[0], inv_high.shape[1]
    half, nonzero = blocks // 2, matrix.shape[1] // size

    def block_of(k, j):
        which, row = places[k]
        packed = refs[which][row + j * size : row + (j + 1) * size, :]
        joined[k * half + j] = packed
        return packed

    unpack_half(meta, block_of, len(places), source, blocks)
    solved = []
    for i in range(blocks):
        at = slice(i * size, (i + 1) * size)
        listed = chained(meta, table, swapped, i * nonzero)
        total = block_product(listed, matrix, i, lambda n: source[n], size)
        field = base_of(meta, bases, at) + (total + turned(total))
        solved.append(solved_block(inc[at, :], field, (inv_high[i], inv_low[i]), load[at, :]))
    lanes = own_lanes(meta, solved[0].shape)
    for j in range(half):
        at = slice(j * size, (j + 1) * size)
        keep[at, :] = jnp.where(lanes, solved[j], turned(solved[j + half])).astype(keep.dtype)


def ahead_kernel(blocks, meta, table, swapped, mine, matrix, base, partner, out, source):
    size = out.shape[0] // blocks
    half, nonzero = blocks // 2, matrix.shape[1] // size
    unpack_half(meta, lambda k, j: mine[k * half + j], mine.shape[0] // half, source, blocks)
    for i in range(blocks):
        at = slice(i * size, (i + 1) * size)
        listed = chained(meta, table, swapped, (blocks + i) * nonzero)
        total = block_product(listed, matrix, i, lambda n: source[n], size)
        out[at, :] = base_of(meta, (base, partner, 1), at) + (total + turned(total))


def unpack_whole(meta, mine, other, source, blocks, lanes=slice(None)):
    half = blocks // 2
    own = own_lanes(meta, mine.shape[1:])
    for k in range(mine.shape[0] // half):
        for j in range(half):
            a, b = mine[k * half + j], other[k * half + j]
            source[k * blocks + j, :, lanes] = jnp.where(own, a, b)
            source[k * blocks + j + half, :, lanes] = turned_exact(jnp.where(own, b, a))


def table_of(table, base):
    return lambda s: table[base + s]


def near_kernel(blocks, meta, table, mine, other, own, history, *refs):
    first, near, ahead, kept0, kept1, whole, source, acc, sems = refs
    size = acc.shape[1] // blocks
    nonzero = kept0.shape[1] // size
    loads = [pltpu.make_async_copy(own.at[n], ref, sems.at[n]) for n, ref in enumerate((kept0, kept1))]
    fields = pltpu.make_async_copy(history.at[pl.ds(0, acc.shape[0])], acc, sems.at[2])
    for copy in (loads[0], fields, loads[1]):
        copy.start()
    unpack_whole(meta, mine, other, source, blocks)
    for i in range(blocks):
        whole[i * size : (i + 1) * size, :] = source[i]
    for copy in (loads[0], fields):
        copy.wait()
    for k, (matrix, out) in enumerate(((kept0, near), (kept1, ahead))):
        if k == 1:
            loads[1].wait()
        for i in range(blocks):
            at = slice(i * size, (i + 1) * size)
            listed = table_of(table, (k * blocks + i) * nonzero)
            total = acc[k + 1, at, :] + block_product(listed, matrix, i, lambda n: source[n], size)
            out[at, :] = total.astype(out.dtype)
    first[...] = acc[0].astype(first.dtype)


def nearer_kernel(blocks, meta, table, mine, other, matrix, base, near, source):
    size = base.shape[0] // blocks
    nonzero = matrix.shape[1] // size
    unpack_whole(meta, mine, other, source, blocks)
    for i in range(blocks):
        at = slice(i * size, (i + 1) * size)
        listed = table_of(table, i * nonzero)
        total = base[at, :] + block_product(listed, matrix, i, lambda n: source[n], size)
        near[at, :] = total.astype(near.dtype)


def far_kernel(blocks, meta, table, mine0, other0, mine1, other1, kept, own, history, out, mats, whole, *refs):
    source, sems = refs[0], refs[-1]
    delays, size, excite = own.shape[0], out.shape[1] // blocks, out.shape[2]
    nonzero = mats.shape[2] // size
    fields = []
    if len(refs) == 3:
        acc = refs[1]
        fields = [pltpu.make_async_copy(history.at[pl.ds(STEPS, acc.shape[0])], acc, sems.at[0])]
    loads = {k: pltpu.make_async_copy(own.at[k], mats.at[k - 2], sems.at[k]) for k in range(2, delays)}
    for copy in fields + list(loads.values()):
        copy.start()
    unpack_whole(meta, mine0, other0, source, blocks, slice(0, excite))
    unpack_whole(meta, mine1, other1, source, blocks, slice(excite, 2 * excite))
    for i in range(blocks):
        whole[i * size : (i + 1) * size, :] = source[i, :, excite:]
    for copy in fields:
        copy.wait()
    for k in range(1, delays):
        matrix = kept if k == 1 else mats.at[k - 2]
        if k > 1:
            loads[k].wait()
        for i in range(blocks):
            at = slice(i * size, (i + 1) * size)
            listed = table_of(table, (k * blocks + i) * nonzero)
            base = acc[k + 2 - STEPS, at, :] if STEPS <= k + 2 < delays else None
            if k == 1:
                late = block_product(listed, matrix, i, lambda n: source[n, :, excite:], size)
            else:
                both = block_product(listed, matrix, i, lambda n: source[n], size)
                out[k - 2, at, :] = out[k - 2, at, :] + both[:, :excite]
                late = both[:, excite:]
            out[k - 1, at, :] = late if base is None else late + base


def last_kernel(blocks, meta, table, mine, other, kept0, kept1, mats, acc, late, earlier, future, currents, *refs):
    source, out, whole, sems = refs
    delays, size = out.shape[0], acc.shape[1] // blocks
    nonzero = mats.shape[2] // size
    stores = [
        pltpu.make_async_copy(one, currents.at[n], sems.at[delays + n]) for n, one in enumerate(earlier + [whole])
    ]
    for store in stores[:-1]:
        store.start()
    unpack_whole(meta, mine, other, source, blocks)
    for i in range(blocks):
        whole[i * size : (i + 1) * size, :] = source[i]
    stores[-1].start()
    followed = meta[1] == 1
    matrices = [kept0, kept1] + [mats.at[k] for k in range(mats.shape[0])]
    for k in range(delays):
        for i in range(blocks):
            at = slice(i * size, (i + 1) * size)
            listed = table_of(table, (k * blocks + i) * nonzero)
            total = block_product(listed, matrices[k], i, lambda n: source[n], size)
            if k < acc.shape[0]:
                total = total + acc[k, at, :]
            if k >= delays - late.shape[0]:
                extra = late[k - (delays - late.shape[0]), at, :].astype(jnp.float32)
                total = total + jnp.where(followed, extra, 0.0)
            out[k, at, :] = total
        stores.append(pltpu.make_async_copy(out.at[k], future.at[k], sems.at[k]))
        stores[-1].start()
    for store in stores:
        store.wait()


def struct(shape, dtype):
    return jax.ShapeDtypeStruct(shape, dtype)


def local_paired(incident, history, couplings, block_inverse, load_coeff, pattern, wanted):
    blocks, size = block_inverse.shape[:2]
    rows, excite = incident.shape[1:]
    delays = history.shape[0]
    n_delay, n_row = lax.axis_size("delay"), lax.axis_size("row")
    d, r = lax.axis_index("delay"), lax.axis_index("row")
    parity = d % 2
    slots = wanted.shape[2]
    half = blocks // 2
    bf16, f32 = jnp.bfloat16, jnp.float32
    axes = ("delay", "row")

    def swap(value, bit):
        pairs = [(a * n_row + q, (a ^ bit) * n_row + q) for a in range(n_delay) for q in range(n_row)]
        return lax.ppermute(value, axes, pairs)

    def swap_row(value, bit):
        pairs = [(a * n_row + q, a * n_row + (q ^ bit)) for a in range(n_delay) for q in range(n_row)]
        return lax.ppermute(value, axes, pairs)

    def located(listed):
        needed = lax.dynamic_index_in_dim(wanted, r, 0, keepdims=False).reshape(-1)
        hit = listed[..., None] == jnp.arange(needed.shape[0], dtype=jnp.int32)
        block = jnp.sum(jnp.where(hit, needed, 0), -1)
        return (((listed // slots) ^ r) * blocks + block).reshape(-1)

    meta = jnp.stack([parity, (d < n_delay - 1).astype(jnp.int32)])
    load = load_coeff.reshape(blocks, size)

    packed = struct((half * size, excite), bf16)
    gathered = (n_row * half, size, excite)
    source = pltpu.VMEM((n_row * blocks, size, excite), bf16)

    def planes(value):
        bit = 2
        while bit < n_delay:
            got = swap(value, bit)
            value = jnp.where((d >= bit) & (d < 2 * bit), got, value)
            bit *= 2
        return value

    def exchange(value):
        direct, groups = row_plan(n_row)
        pieces = [None] * n_row
        pieces[0] = (value, 0)
        for k in direct:
            pieces[k] = (swap_row(value, k), 0)
        for group in groups:
            passed = [pieces[k][0] for k in group]
            passed = swap_row(jnp.concatenate(passed, 0) if len(group) > 1 else passed[0], 1)
            for m, k in enumerate(group):
                pieces[k ^ 1] = (passed, m * half * size)
        return pieces

    def gather_other(mine):
        return swap(mine, 1)

    hbm = lambda value: pltpu.with_memory_space_constraint(value, pltpu.MemorySpace.HBM)
    couplings, history, incident = map(hbm, (couplings, history, incident))
    block_inverse, load = map(hbm, (block_inverse, load))

    count = STEPS - 1
    keep, send, bases = pl.pallas_call(
        first_kernel,
        out_shape=[packed] * 2 + [struct((count, rows, excite), f32)],
        in_specs=[HBM] * 4,
        out_specs=[VMEM] * 3,
        scratch_shapes=[
            pltpu.VMEM((rows, excite), bf16),
            pltpu.VMEM((rows, excite), f32),
            pltpu.VMEM(block_inverse.shape, f32),
            pltpu.VMEM(load.shape, f32),
            pltpu.SemaphoreType.DMA((5,)),
        ],
        compiler_params=PARAMS,
        name="first",
    )(incident, history, block_inverse, load)
    got = swap(send, 1)
    mine = jnp.where(parity == 0, keep, got)
    table = located(pattern)
    theirs = hbm(swap(couplings, 1))
    partner = swap(bases, 1)
    swapped = swap(table, 1)
    field, current = struct((rows, excite), f32), struct((rows, excite), bf16)
    matrix = struct(couplings.shape[1:], bf16)
    prepared = pl.pallas_call(
        prepare_kernel,
        out_shape=[current] * count + [matrix] * count + [struct(block_inverse.shape, bf16)] * 2 + [field],
        in_specs=[SMEM] + [HBM] * 5,
        out_specs=[VMEM] * (2 * count + 3),
        scratch_shapes=[
            pltpu.VMEM(block_inverse.shape, f32),
            pltpu.VMEM(load.shape, f32),
            pltpu.SemaphoreType.DMA((2 * count + 2,)),
        ],
        compiler_params=LARGE,
        name="prepare",
    )(meta, incident, couplings, theirs, block_inverse, load)
    incs, mats = prepared[:count], prepared[count : 2 * count]
    inv_high, inv_low, load = prepared[2 * count :]

    def advance(step, pieces, mat, base):
        arrays = []
        places = []
        for array, row in pieces:
            seen = [n for n, one in enumerate(arrays) if one is array]
            places.append((seen[0] if seen else len(arrays), row))
            arrays += [] if seen else [array]
        return pl.pallas_call(
            functools.partial(next_kernel, places, step > 0),
            out_shape=[packed, struct(gathered, bf16)],
            in_specs=[SMEM] * 3 + [VMEM] * (7 + len(arrays)),
            out_specs=[VMEM] * 2,
            scratch_shapes=[source],
            compiler_params=LARGE,
            name="next",
        )(meta, table, swapped, mat, base, base if step else partner, incs[step], inv_high, inv_low, load, *arrays)

    def spread_out(mine):
        mine = planes(mine)
        return exchange(mine)

    pieces = spread_out(mine)
    mine, near0 = advance(0, pieces, mats[0], bases)
    base = pl.pallas_call(
        functools.partial(ahead_kernel, blocks),
        out_shape=field,
        in_specs=[SMEM] * 3 + [VMEM] * 4,
        out_specs=VMEM,
        scratch_shapes=[source],
        compiler_params=LARGE,
        name="ahead",
    )(meta, table, swapped, near0, mats[1], bases, partner)
    other0 = gather_other(near0)
    tail, first_tail, ahead, kept, kept1, whole0 = pl.pallas_call(
        functools.partial(near_kernel, blocks),
        out_shape=[current, current, field, matrix, matrix, current],
        in_specs=[SMEM, SMEM, VMEM, VMEM, HBM, HBM],
        out_specs=[VMEM] * 6,
        scratch_shapes=[
            source,
            pltpu.VMEM((STEPS, rows, excite), f32),
            pltpu.SemaphoreType.DMA((3,)),
        ],
        compiler_params=LARGE,
        name="near",
    )(meta, table, near0, other0, couplings, history)

    pieces = spread_out(mine)
    mine, near1 = advance(1, pieces, mats[0], base)
    other1 = gather_other(near1)
    second_tail = pl.pallas_call(
        functools.partial(nearer_kernel, blocks),
        out_shape=current,
        in_specs=[SMEM] * 2 + [VMEM] * 4,
        out_specs=VMEM,
        scratch_shapes=[source],
        compiler_params=LARGE,
        name="nearer",
    )(meta, table, near1, other1, kept, ahead)
    acc, mats, whole1 = pl.pallas_call(
        functools.partial(far_kernel, blocks),
        out_shape=[struct((delays - 1, rows, excite), f32), struct((delays - 2,) + couplings.shape[1:], bf16), current],
        in_specs=[SMEM] * 2 + [VMEM] * 5 + [HBM] * 2,
        out_specs=[VMEM] * 3,
        scratch_shapes=[pltpu.VMEM((n_row * blocks, size, 2 * excite), bf16)]
        + [pltpu.VMEM((delays - STEPS, rows, excite), f32)] * (delays > STEPS)
        + [pltpu.SemaphoreType.DMA((delays,))],
        compiler_params=LARGE,
        name="far",
    )(meta, table, near0, other0, near1, other1, kept1, couplings, history)
    tails = [tail, first_tail, second_tail]
    back = [(a * n_row + q, ((a - 1) % n_delay) * n_row + q) for a in range(n_delay) for q in range(n_row)]
    late = lax.ppermute(jnp.stack(tails), axes, back)

    pieces = spread_out(mine)
    near2 = jnp.concatenate([array[row : row + half * size] for array, row in pieces], 0).reshape(gathered)
    other2 = gather_other(near2)

    def finish(*refs):
        last_kernel(blocks, *refs[:9], list(refs[9:11]), *refs[11:])

    future, currents = pl.pallas_call(
        finish,
        out_shape=[struct(history.shape, f32), struct((STEPS, rows, excite), bf16)],
        in_specs=[SMEM] * 2 + [VMEM] * 9,
        out_specs=[HBM] * 2,
        scratch_shapes=[
            source,
            pltpu.VMEM(history.shape, f32),
            pltpu.VMEM((rows, excite), bf16),
            pltpu.SemaphoreType.DMA((delays + STEPS,)),
        ],
        compiler_params=LARGE,
        name="last",
    )(meta, table, near2, other2, kept, kept1, mats, acc, late, whole0, whole1)
    return currents, future


def fits(mesh, blocks, delays):
    sizes = (mesh.shape["delay"], mesh.shape["row"])
    powers = all(n >= 2 and n & (n - 1) == 0 for n in sizes)
    return powers and blocks % 2 == 0 and delays >= STEPS and STEPS == 3


def row_plan(n_row):
    far, near = n_row // 2, 2
    groups = [] if n_row < 4 else [[far]] if far == near else [[far, near], [far + near]]
    passed = [k for group in groups for k in group]
    others = [k for k in range(n_row - 1, 1, -1) if k not in passed and k ^ 1 not in passed]
    return passed + others + [1], groups


def solution(mesh):
    in_specs = (
        P(None, "row", None),
        P("delay", "row", None),
        P("delay", "row", None),
        P("row", None, None),
        P("row"),
        P("delay", "row", None),
        P(),
    )
    out_specs = (P(None, "row", None), P("delay", "row", None))

    def local(*args):
        if not fits(mesh, args[3].shape[0], args[1].shape[0]):
            return local_general(*args)
        return local_paired(*args)

    return jax.shard_map(local, mesh=mesh, in_specs=in_specs, out_specs=out_specs, check_vma=False)
```

```python
import functools

import jax
import jax.numpy as jnp
from jax import lax
from jax.experimental import pallas as pl
from jax.experimental.pallas import tpu as pltpu
from jax.sharding import PartitionSpec as P

STEPS = 3


def passed_along(value, axis, steps):
    count = lax.axis_size(axis)
    leading, last = (max(0, -steps), min(count, count - steps))
    return lax.ppermute(value, axis, [(source, source + steps) for source in range(leading, last)])


def spread(value, axis, source):
    kept = jnp.where(lax.axis_index(axis) == source, value, 0).astype(value.dtype)
    return lax.psum(kept, axis)


def solve_step(incoming, field, block_inverse, load_coeff):
    blk_rows = block_inverse.shape[0]
    size_blk = block_inverse.shape[1]
    rhs = incoming.astype(jnp.float32) - field
    solved = jnp.einsum(
        "iab,ibc->iac",
        block_inverse,
        rhs.reshape(blk_rows, size_blk, rhs.shape[1]),
        precision=lax.Precision.HIGHEST,
    ).reshape(rhs.shape)
    return (solved - load_coeff[:, None] * solved * solved * solved).astype(jnp.bfloat16)


def local_general(incident, history, couplings, block_inverse, load_coeff, pattern, wanted):
    blk_rows = block_inverse.shape[0]
    size_blk = block_inverse.shape[1]
    excite = incident.shape[2]
    local_delays = history.shape[0]
    nonzero = couplings.shape[2] // size_blk
    owners = lax.axis_size("row")
    owner = lax.axis_index("row")
    slots = wanted.shape[2]
    zmats = couplings.reshape(local_delays, blk_rows, size_blk, nonzero * size_blk)
    outgoing = lax.dynamic_index_in_dim(wanted, owner, 1, keepdims=False)
    send_index = jnp.maximum(outgoing, 0)
    send_live = outgoing >= 0
    acc = history
    outputs = []
    for step in range(STEPS):
        nearest = passed_along(acc[0].astype(jnp.bfloat16), "delay", -1).astype(jnp.float32)
        current = solve_step(incident[step], acc[0], block_inverse, load_coeff)
        current = spread(current, "delay", 0)
        blocks = current.reshape(blk_rows, size_blk, excite)
        parcels = jnp.where(
            send_live[:, :, None, None], blocks[send_index], jnp.zeros((), jnp.bfloat16)
        )
        received = lax.all_to_all(parcels, "row", split_axis=0, concat_axis=0, tiled=True)
        source = received.reshape(owners * slots, size_blk, excite)
        picked = source[pattern].reshape(local_delays, blk_rows, nonzero * size_blk, excite)
        products = jnp.einsum("krab,krbc->krac", zmats, picked, preferred_element_type=jnp.float32)
        products = products.reshape(local_delays, blk_rows * size_blk, excite)
        acc = jnp.concatenate([acc[1:], nearest[None]], 0) + products
        outputs.append(current)
    return (jnp.stack(outputs), acc)


VMEM = pl.BlockSpec(memory_space=pltpu.VMEM)
SMEM = pl.BlockSpec(memory_space=pltpu.SMEM)
HBM = pl.BlockSpec(memory_space=pltpu.HBM)
PARAMS = pltpu.CompilerParams(vmem_limit_bytes=8 * 1024 * 1024)
LARGE = pltpu.CompilerParams(vmem_limit_bytes=16 * 1024 * 1024)


def column_of(row_vector):
    size = row_vector.shape[1]
    rows = lax.broadcasted_iota(jnp.int32, (size, size), 0)
    cols = lax.broadcasted_iota(jnp.int32, (size, size), 1)
    spread_out = jnp.where(rows == cols, jnp.broadcast_to(row_vector, (size, size)), 0.0)
    return jnp.broadcast_to(jnp.sum(spread_out, axis=1, keepdims=True), (size, size))


def in_two(value):
    high = value.astype(jnp.bfloat16)
    return high, (value - high.astype(jnp.float32)).astype(jnp.bfloat16)


def solved_block(incoming, field, inverse, load):
    rhs = in_two(incoming.astype(jnp.float32) - field)
    dot = functools.partial(jnp.dot, preferred_element_type=jnp.float32)
    y = dot(inverse[0], rhs[0]) + (dot(inverse[0], rhs[1]) + dot(inverse[1], rhs[0]))
    return y - load * y * y * y


def turned(value):
    return pltpu.roll(value, value.shape[-1] // 2, value.ndim - 1)


def turned_exact(value):
    return turned(value.astype(jnp.float32)).astype(value.dtype)


def own_lanes(meta, shape):
    lane = lax.broadcasted_iota(jnp.int32, shape, 1)
    return (lane < shape[1] // 2) == (meta[0] == 0)


def block_product(listed, matrix, row, block_of, size):
    nonzero = matrix.shape[1] // size
    total = None
    for s in range(0, nonzero, 2):
        pair = jnp.concatenate([block_of(listed(s)), block_of(listed(s + 1))], 0)
        part = jnp.dot(
            matrix[row * size : (row + 1) * size, s * size : (s + 2) * size],
            pair,
            preferred_element_type=jnp.float32,
        )
        total = part if total is None else total + part
    return total


def fetch(pairs, sems, later):
    copies = [pltpu.make_async_copy(a, b, sems.at[n]) for n, (a, b) in enumerate(pairs)]
    for copy in copies + [later]:
        copy.start()
    for copy in copies:
        copy.wait()


def first_kernel(incident, history, inverse, coeff, keep, send, bases, inc, field, inv, load, sems):
    later = pltpu.make_async_copy(history.at[pl.ds(1, bases.shape[0])], bases, sems.at[4])
    fetch([(incident.at[0], inc), (history.at[0], field), (inverse, inv), (coeff, load)], sems, later)
    blocks, size = inv.shape[0], inv.shape[1]
    half = blocks // 2
    solved = []
    for i in range(blocks):
        at = slice(i * size, (i + 1) * size)
        solved.append(solved_block(inc[at, :], field[at, :], in_two(inv[i]), column_of(load[i : i + 1, :])))
    shape = solved[0].shape
    left = lax.broadcasted_iota(jnp.int32, shape, 1) < shape[1] // 2
    for j in range(half):
        low, high, at = solved[j], turned(solved[j + half]), slice(j * size, (j + 1) * size)
        keep[at, :] = jnp.where(left, low, high).astype(keep.dtype)
        send[at, :] = jnp.where(left, high, low).astype(send.dtype)
    later.wait()


def by_parity(meta, own, theirs, kept, sem):
    copies = [pltpu.make_async_copy(source, kept, sem) for source in (own, theirs)]

    def start():
        pl.when(meta[0] == 0)(copies[0].start)
        pl.when(meta[0] != 0)(copies[1].start)

    return start, copies[0].wait


def prepare_kernel(meta, incident, own, theirs, inverse, coeff, *refs):
    count = (len(refs) - 6) // 2
    incs, mats = refs[:count], refs[count : 2 * count]
    inv_high, inv_low, load, inv, rows, sems = refs[2 * count :]
    pairs = [by_parity(meta, own.at[n], theirs.at[n], mats[n], sems.at[n]) for n in range(count)]
    plain = [(inverse, inv), (coeff, rows)] + [(incident.at[n + 1], incs[n]) for n in range(count)]
    plain = [pltpu.make_async_copy(a, b, sems.at[count + n]) for n, (a, b) in enumerate(plain)]
    for copy in plain:
        copy.start()
    for start, _ in pairs:
        start()
    for copy in plain:
        copy.wait()
    blocks, size = inv.shape[0], inv.shape[1]
    for i in range(blocks):
        inv_high[i], inv_low[i] = in_two(inv[i])
        load[i * size : (i + 1) * size, :] = column_of(rows[i : i + 1, :])
    for _, wait in pairs:
        wait()


def unpack_half(meta, block_of, owners, source, blocks):
    half, shape = blocks // 2, source.shape[1:]
    own = own_lanes(meta, shape)
    nothing = jnp.zeros(shape, source.dtype)
    for k in range(owners):
        for j in range(half):
            packed = block_of(k, j)
            source[k * blocks + j] = jnp.where(own, packed, nothing)
            source[k * blocks + j + half] = jnp.where(own, nothing, packed)


def chained(meta, table, swapped, base):
    return lambda s: jnp.where(meta[0] == 0, table[base + s], swapped[base + s])


def base_of(meta, bases, at):
    own, partner, n = bases
    return own[at, :] if partner is None else jnp.where(meta[0] == 0, own[n, at, :], partner[n, at, :])


def next_kernel(places, own_base, meta, table, swapped, matrix, base, partner, inc, inv_high, inv_low, load, *refs):
    keep, joined, source = refs[-3:]
    bases = (base, None, 0) if own_base else (base, partner, 0)
    blocks, size = inv_high.shape[0], inv_high.shape[1]
    half, nonzero = blocks // 2, matrix.shape[1] // size

    def block_of(k, j):
        which, row = places[k]
        packed = refs[which][row + j * size : row + (j + 1) * size, :]
        joined[k * half + j] = packed
        return packed

    unpack_half(meta, block_of, len(places), source, blocks)
    solved = []
    for i in range(blocks):
        at = slice(i * size, (i + 1) * size)
        listed = chained(meta, table, swapped, i * nonzero)
        total = block_product(listed, matrix, i, lambda n: source[n], size)
        field = base_of(meta, bases, at) + (total + turned(total))
        solved.append(solved_block(inc[at, :], field, (inv_high[i], inv_low[i]), load[at, :]))
    lanes = own_lanes(meta, solved[0].shape)
    for j in range(half):
        at = slice(j * size, (j + 1) * size)
        keep[at, :] = jnp.where(lanes, solved[j], turned(solved[j + half])).astype(keep.dtype)


def ahead_kernel(blocks, meta, table, swapped, mine, matrix, base, partner, own, out, kept0, kept1, source, sems):
    loads = [pltpu.make_async_copy(own.at[n], ref, sems.at[n]) for n, ref in enumerate((kept0, kept1))]
    for load in loads:
        load.start()
    size = out.shape[0] // blocks
    half, nonzero = blocks // 2, matrix.shape[1] // size
    unpack_half(meta, lambda k, j: mine[k * half + j], mine.shape[0] // half, source, blocks)
    for i in range(blocks):
        at = slice(i * size, (i + 1) * size)
        listed = chained(meta, table, swapped, (blocks + i) * nonzero)
        total = block_product(listed, matrix, i, lambda n: source[n], size)
        out[at, :] = base_of(meta, (base, partner, 1), at) + (total + turned(total))
    for load in loads:
        load.wait()


def unpack_whole(meta, mine, other, source, blocks, lanes=slice(None)):
    half = blocks // 2
    own = own_lanes(meta, mine.shape[1:])
    for k in range(mine.shape[0] // half):
        for j in range(half):
            a, b = mine[k * half + j], other[k * half + j]
            source[k * blocks + j, :, lanes] = jnp.where(own, a, b)
            source[k * blocks + j + half, :, lanes] = turned_exact(jnp.where(own, b, a))


def table_of(table, base):
    return lambda s: table[base + s]


def near_kernel(blocks, meta, table, mine, other, kept0, kept1, own, history, *refs):
    first, near, ahead, mats, whole, source, acc, sems = refs
    size = acc.shape[1] // blocks
    nonzero = kept0.shape[1] // size
    fields = pltpu.make_async_copy(history.at[pl.ds(0, acc.shape[0])], acc, sems.at[0])
    loads = pltpu.make_async_copy(own.at[pl.ds(2, mats.shape[0])], mats, sems.at[1])
    fields.start()
    loads.start()
    unpack_whole(meta, mine, other, source, blocks)
    for i in range(blocks):
        whole[i * size : (i + 1) * size, :] = source[i]
    fields.wait()
    for k, (matrix, out) in enumerate(((kept0, near), (kept1, ahead))):
        for i in range(blocks):
            at = slice(i * size, (i + 1) * size)
            listed = table_of(table, (k * blocks + i) * nonzero)
            total = acc[k + 1, at, :] + block_product(listed, matrix, i, lambda n: source[n], size)
            out[at, :] = total.astype(out.dtype)
    first[...] = acc[0].astype(first.dtype)
    loads.wait()


def nearer_kernel(blocks, meta, table, mine, other, matrix, base, near, source):
    size = base.shape[0] // blocks
    nonzero = matrix.shape[1] // size
    unpack_whole(meta, mine, other, source, blocks)
    for i in range(blocks):
        at = slice(i * size, (i + 1) * size)
        listed = table_of(table, i * nonzero)
        total = base[at, :] + block_product(listed, matrix, i, lambda n: source[n], size)
        near[at, :] = total.astype(near.dtype)


def far_kernel(blocks, meta, table, mine, other, mats, history, out, *refs):
    source, sems = refs[0], refs[-1]
    size, count = out.shape[1] // blocks, mats.shape[0]
    nonzero = mats.shape[2] // size
    later = None
    if len(refs) == 3:
        later = pltpu.make_async_copy(history.at[pl.ds(STEPS, count - 1)], refs[1], sems.at[0])
        later.start()
    unpack_whole(meta, mine, other, source, blocks)
    for n in reversed(range(count)):
        for i in range(blocks):
            at = slice(i * size, (i + 1) * size)
            listed = table_of(table, ((n + 2) * blocks + i) * nonzero)
            out[n, at, :] = block_product(listed, mats.at[n], i, lambda m: source[m], size)
    if later is not None:
        later.wait()
        for n in range(count - 1):
            out[n] = out[n] + refs[1][n]


def last_kernel(blocks, meta, table, mine1, other1, mine, other, kept0, kept1, mats, acc, late, first, *refs):
    future, currents, source, out, whole1, whole2, sems = refs
    delays, size, excite = out.shape[0], out.shape[1] // blocks, out.shape[2]
    nonzero = kept0.shape[1] // size
    matrices = [kept0, kept1] + [mats.at[k] for k in range(mats.shape[0])]
    stores = []

    def store(value, place):
        stores.append(pltpu.make_async_copy(value, place, sems.at[len(stores)]))
        stores[-1].start()

    store(first, currents.at[0])
    for n, (a, b, whole) in enumerate(((mine1, other1, whole1), (mine, other, whole2))):
        lanes = slice(n * excite, (n + 1) * excite)
        unpack_whole(meta, a, b, source, blocks, lanes)
        for i in range(blocks):
            whole[i * size : (i + 1) * size, :] = source[i, :, lanes]
        store(whole, currents.at[n + 1])
    followed = meta[1] == 1
    for k in range(delays):
        for i in range(blocks):
            at = slice(i * size, (i + 1) * size)
            listed = table_of(table, (k * blocks + i) * nonzero)
            if k == 0:
                total = block_product(listed, matrices[k], i, lambda n: source[n, :, excite:], size)
            else:
                both = block_product(listed, matrices[k], i, lambda n: source[n], size)
                out[k - 1, at, :] = out[k - 1, at, :] + both[:, :excite]
                total = both[:, excite:]
            if k < acc.shape[0]:
                total = total + acc[k, at, :]
            if k >= delays - late.shape[0]:
                extra = late[k - (delays - late.shape[0]), at, :].astype(jnp.float32)
                total = total + jnp.where(followed, extra, 0.0)
            out[k, at, :] = total
        if k > 0:
            store(out.at[k - 1], future.at[k - 1])
    store(out.at[delays - 1], future.at[delays - 1])
    for one in stores:
        one.wait()


def struct(shape, dtype):
    return jax.ShapeDtypeStruct(shape, dtype)


def local_paired(incident, history, couplings, block_inverse, load_coeff, pattern, wanted):
    blocks, size = block_inverse.shape[:2]
    rows, excite = incident.shape[1:]
    delays = history.shape[0]
    n_delay, n_row = lax.axis_size("delay"), lax.axis_size("row")
    d, r = lax.axis_index("delay"), lax.axis_index("row")
    parity = d % 2
    slots = wanted.shape[2]
    half = blocks // 2
    bf16, f32 = jnp.bfloat16, jnp.float32
    axes = ("delay", "row")

    def swap(value, bit):
        pairs = [(a * n_row + q, (a ^ bit) * n_row + q) for a in range(n_delay) for q in range(n_row)]
        return lax.ppermute(value, axes, pairs)

    def swap_row(value, bit):
        pairs = [(a * n_row + q, a * n_row + (q ^ bit)) for a in range(n_delay) for q in range(n_row)]
        return lax.ppermute(value, axes, pairs)

    def located(listed):
        needed = lax.dynamic_index_in_dim(wanted, r, 0, keepdims=False).reshape(-1)
        hit = listed[..., None] == jnp.arange(needed.shape[0], dtype=jnp.int32)
        block = jnp.sum(jnp.where(hit, needed, 0), -1)
        return (((listed // slots) ^ r) * blocks + block).reshape(-1)

    meta = jnp.stack([parity, (d < n_delay - 1).astype(jnp.int32)])
    load = load_coeff.reshape(blocks, size)

    packed = struct((half * size, excite), bf16)
    gathered = (n_row * half, size, excite)
    source = pltpu.VMEM((n_row * blocks, size, excite), bf16)

    def planes(value):
        bit = 2
        while bit < n_delay:
            got = swap(value, bit)
            value = jnp.where((d >= bit) & (d < 2 * bit), got, value)
            bit *= 2
        return value

    def exchange(value):
        direct, groups = row_plan(n_row)
        pieces = [None] * n_row
        pieces[0] = (value, 0)
        for k in direct:
            pieces[k] = (swap_row(value, k), 0)
        for group in groups:
            passed = [pieces[k][0] for k in group]
            passed = swap_row(jnp.concatenate(passed, 0) if len(group) > 1 else passed[0], 1)
            for m, k in enumerate(group):
                pieces[k ^ 1] = (passed, m * half * size)
        return pieces

    def gather_other(mine):
        return swap(mine, 1)

    hbm = lambda value: pltpu.with_memory_space_constraint(value, pltpu.MemorySpace.HBM)
    couplings, history, incident = map(hbm, (couplings, history, incident))
    block_inverse, load = map(hbm, (block_inverse, load))

    count = STEPS - 1
    keep, send, bases = pl.pallas_call(
        first_kernel,
        out_shape=[packed] * 2 + [struct((count, rows, excite), f32)],
        in_specs=[HBM] * 4,
        out_specs=[VMEM] * 3,
        scratch_shapes=[
            pltpu.VMEM((rows, excite), bf16),
            pltpu.VMEM((rows, excite), f32),
            pltpu.VMEM(block_inverse.shape, f32),
            pltpu.VMEM(load.shape, f32),
            pltpu.SemaphoreType.DMA((5,)),
        ],
        compiler_params=PARAMS,
        name="first",
    )(incident, history, block_inverse, load)
    got = swap(send, 1)
    mine = jnp.where(parity == 0, keep, got)
    table = located(pattern)
    theirs = hbm(swap(couplings, 1))
    partner = swap(bases, 1)
    swapped = swap(table, 1)
    field, current = struct((rows, excite), f32), struct((rows, excite), bf16)
    matrix = struct(couplings.shape[1:], bf16)
    prepared = pl.pallas_call(
        prepare_kernel,
        out_shape=[current] * count + [matrix] * count + [struct(block_inverse.shape, bf16)] * 2 + [field],
        in_specs=[SMEM] + [HBM] * 5,
        out_specs=[VMEM] * (2 * count + 3),
        scratch_shapes=[
            pltpu.VMEM(block_inverse.shape, f32),
            pltpu.VMEM(load.shape, f32),
            pltpu.SemaphoreType.DMA((2 * count + 2,)),
        ],
        compiler_params=LARGE,
        name="prepare",
    )(meta, incident, couplings, theirs, block_inverse, load)
    incs, mats = prepared[:count], prepared[count : 2 * count]
    inv_high, inv_low, load = prepared[2 * count :]

    def advance(step, pieces, mat, base):
        arrays = []
        places = []
        for array, row in pieces:
            seen = [n for n, one in enumerate(arrays) if one is array]
            places.append((seen[0] if seen else len(arrays), row))
            arrays += [] if seen else [array]
        return pl.pallas_call(
            functools.partial(next_kernel, places, step > 0),
            out_shape=[packed, struct(gathered, bf16)],
            in_specs=[SMEM] * 3 + [VMEM] * (7 + len(arrays)),
            out_specs=[VMEM] * 2,
            scratch_shapes=[source],
            compiler_params=LARGE,
            name="next",
        )(meta, table, swapped, mat, base, base if step else partner, incs[step], inv_high, inv_low, load, *arrays)

    def spread_out(mine):
        mine = planes(mine)
        return exchange(mine)

    pieces = spread_out(mine)
    mine, near0 = advance(0, pieces, mats[0], bases)
    base, kept0, kept1 = pl.pallas_call(
        functools.partial(ahead_kernel, blocks),
        out_shape=[field, matrix, matrix],
        in_specs=[SMEM] * 3 + [VMEM] * 4 + [HBM],
        out_specs=[VMEM] * 3,
        scratch_shapes=[source, pltpu.SemaphoreType.DMA((2,))],
        compiler_params=LARGE,
        name="ahead",
    )(meta, table, swapped, near0, mats[1], bases, partner, couplings)
    other0 = gather_other(near0)
    tail, first_tail, ahead, mats_rest, whole0 = pl.pallas_call(
        functools.partial(near_kernel, blocks),
        out_shape=[current, current, field, struct((delays - 2,) + couplings.shape[1:], bf16), current],
        in_specs=[SMEM] * 2 + [VMEM] * 4 + [HBM] * 2,
        out_specs=[VMEM] * 5,
        scratch_shapes=[source, pltpu.VMEM((STEPS, rows, excite), f32), pltpu.SemaphoreType.DMA((2,))],
        compiler_params=LARGE,
        name="near",
    )(meta, table, near0, other0, kept0, kept1, couplings, history)

    pieces = spread_out(mine)
    mine, near1 = advance(1, pieces, mats[0], base)
    other1 = gather_other(near1)
    second_tail = pl.pallas_call(
        functools.partial(nearer_kernel, blocks),
        out_shape=current,
        in_specs=[SMEM] * 2 + [VMEM] * 4,
        out_specs=VMEM,
        scratch_shapes=[source],
        compiler_params=LARGE,
        name="nearer",
    )(meta, table, near1, other1, kept0, ahead)
    acc = pl.pallas_call(
        functools.partial(far_kernel, blocks),
        out_shape=struct((delays - 2, rows, excite), f32),
        in_specs=[SMEM] * 2 + [VMEM] * 3 + [HBM],
        out_specs=VMEM,
        scratch_shapes=[source]
        + [pltpu.VMEM((delays - STEPS, rows, excite), f32)] * (delays > STEPS)
        + [pltpu.SemaphoreType.DMA((1,))],
        compiler_params=LARGE,
        name="far",
    )(meta, table, near0, other0, mats_rest, history)
    tails = [tail, first_tail, second_tail]
    back = [(a * n_row + q, ((a - 1) % n_delay) * n_row + q) for a in range(n_delay) for q in range(n_row)]
    late = lax.ppermute(jnp.stack(tails), axes, back)

    pieces = spread_out(mine)
    near2 = jnp.concatenate([array[row : row + half * size] for array, row in pieces], 0).reshape(gathered)
    other2 = gather_other(near2)

    future, currents = pl.pallas_call(
        functools.partial(last_kernel, blocks),
        out_shape=[struct(history.shape, f32), struct((STEPS, rows, excite), bf16)],
        in_specs=[SMEM] * 2 + [VMEM] * 10,
        out_specs=[HBM] * 2,
        scratch_shapes=[
            pltpu.VMEM((n_row * blocks, size, 2 * excite), bf16),
            pltpu.VMEM(history.shape, f32),
            pltpu.VMEM((rows, excite), bf16),
            pltpu.VMEM((rows, excite), bf16),
            pltpu.SemaphoreType.DMA((delays + STEPS,)),
        ],
        compiler_params=LARGE,
        name="last",
    )(meta, table, near1, other1, near2, other2, kept0, kept1, mats_rest, acc, late, whole0)
    return currents, future


def fits(mesh, blocks, delays):
    sizes = (mesh.shape["delay"], mesh.shape["row"])
    powers = all(n >= 2 and n & (n - 1) == 0 for n in sizes)
    return powers and blocks % 2 == 0 and delays >= STEPS and STEPS == 3


def row_plan(n_row):
    far, near = n_row // 2, 2
    groups = [] if n_row < 4 else [[far]] if far == near else [[far, near], [far + near]]
    passed = [k for group in groups for k in group]
    others = [k for k in range(n_row - 1, 1, -1) if k not in passed and k ^ 1 not in passed]
    return passed + others + [1], groups


def solution(mesh):
    in_specs = (
        P(None, "row", None),
        P("delay", "row", None),
        P("delay", "row", None),
        P("row", None, None),
        P("row"),
        P("delay", "row", None),
        P(),
    )
    out_specs = (P(None, "row", None), P("delay", "row", None))

    def local(*args):
        if not fits(mesh, args[3].shape[0], args[1].shape[0]):
            return local_general(*args)
        return local_paired(*args)

    return jax.shard_map(local, mesh=mesh, in_specs=in_specs, out_specs=out_specs, check_vma=False)
```

```python
import functools

import jax
import jax.numpy as jnp
from jax import lax
from jax.experimental import pallas as pl
from jax.experimental.pallas import tpu as pltpu
from jax.sharding import PartitionSpec as P

STEPS = 3


def passed_along(value, axis, steps):
    count = lax.axis_size(axis)
    leading, last = (max(0, -steps), min(count, count - steps))
    return lax.ppermute(value, axis, [(source, source + steps) for source in range(leading, last)])


def spread(value, axis, source):
    kept = jnp.where(lax.axis_index(axis) == source, value, 0).astype(value.dtype)
    return lax.psum(kept, axis)


def solve_step(incoming, field, block_inverse, load_coeff):
    blk_rows = block_inverse.shape[0]
    size_blk = block_inverse.shape[1]
    rhs = incoming.astype(jnp.float32) - field
    solved = jnp.einsum(
        "iab,ibc->iac",
        block_inverse,
        rhs.reshape(blk_rows, size_blk, rhs.shape[1]),
        precision=lax.Precision.HIGHEST,
    ).reshape(rhs.shape)
    return (solved - load_coeff[:, None] * solved * solved * solved).astype(jnp.bfloat16)


def local_general(incident, history, couplings, block_inverse, load_coeff, pattern, wanted):
    blk_rows = block_inverse.shape[0]
    size_blk = block_inverse.shape[1]
    excite = incident.shape[2]
    local_delays = history.shape[0]
    nonzero = couplings.shape[2] // size_blk
    owners = lax.axis_size("row")
    owner = lax.axis_index("row")
    slots = wanted.shape[2]
    zmats = couplings.reshape(local_delays, blk_rows, size_blk, nonzero * size_blk)
    outgoing = lax.dynamic_index_in_dim(wanted, owner, 1, keepdims=False)
    send_index = jnp.maximum(outgoing, 0)
    send_live = outgoing >= 0
    acc = history
    outputs = []
    for step in range(STEPS):
        nearest = passed_along(acc[0].astype(jnp.bfloat16), "delay", -1).astype(jnp.float32)
        current = solve_step(incident[step], acc[0], block_inverse, load_coeff)
        current = spread(current, "delay", 0)
        blocks = current.reshape(blk_rows, size_blk, excite)
        parcels = jnp.where(
            send_live[:, :, None, None], blocks[send_index], jnp.zeros((), jnp.bfloat16)
        )
        received = lax.all_to_all(parcels, "row", split_axis=0, concat_axis=0, tiled=True)
        source = received.reshape(owners * slots, size_blk, excite)
        picked = source[pattern].reshape(local_delays, blk_rows, nonzero * size_blk, excite)
        products = jnp.einsum("krab,krbc->krac", zmats, picked, preferred_element_type=jnp.float32)
        products = products.reshape(local_delays, blk_rows * size_blk, excite)
        acc = jnp.concatenate([acc[1:], nearest[None]], 0) + products
        outputs.append(current)
    return (jnp.stack(outputs), acc)


VMEM = pl.BlockSpec(memory_space=pltpu.VMEM)
SMEM = pl.BlockSpec(memory_space=pltpu.SMEM)
HBM = pl.BlockSpec(memory_space=pltpu.HBM)
PARAMS = pltpu.CompilerParams(vmem_limit_bytes=8 * 1024 * 1024)
LARGE = pltpu.CompilerParams(vmem_limit_bytes=16 * 1024 * 1024)


def column_of(row_vector):
    size = row_vector.shape[1]
    rows = lax.broadcasted_iota(jnp.int32, (size, size), 0)
    cols = lax.broadcasted_iota(jnp.int32, (size, size), 1)
    spread_out = jnp.where(rows == cols, jnp.broadcast_to(row_vector, (size, size)), 0.0)
    return jnp.broadcast_to(jnp.sum(spread_out, axis=1, keepdims=True), (size, size))


def in_two(value):
    high = value.astype(jnp.bfloat16)
    return high, (value - high.astype(jnp.float32)).astype(jnp.bfloat16)


def solved_block(incoming, field, inverse, load):
    rhs = in_two(incoming.astype(jnp.float32) - field)
    dot = functools.partial(jnp.dot, preferred_element_type=jnp.float32)
    y = dot(inverse[0], rhs[0]) + (dot(inverse[0], rhs[1]) + dot(inverse[1], rhs[0]))
    return y - load * y * y * y


def turned(value):
    return pltpu.roll(value, value.shape[-1] // 2, value.ndim - 1)


def turned_exact(value):
    return turned(value.astype(jnp.float32)).astype(value.dtype)


def own_lanes(meta, shape):
    lane = lax.broadcasted_iota(jnp.int32, shape, 1)
    return (lane < shape[1] // 2) == (meta[0] == 0)


def block_product(listed, matrix, row, block_of, size):
    nonzero = matrix.shape[1] // size
    total = None
    for s in range(0, nonzero, 2):
        pair = jnp.concatenate([block_of(listed(s)), block_of(listed(s + 1))], 0)
        part = jnp.dot(
            matrix[row * size : (row + 1) * size, s * size : (s + 2) * size],
            pair,
            preferred_element_type=jnp.float32,
        )
        total = part if total is None else total + part
    return total


def fetch(pairs, sems, later):
    copies = [pltpu.make_async_copy(a, b, sems.at[n]) for n, (a, b) in enumerate(pairs)]
    for copy in copies + [later]:
        copy.start()
    for copy in copies:
        copy.wait()


def first_kernel(incident, history, inverse, coeff, keep, send, bases, inc, field, inv, load, sems):
    later = pltpu.make_async_copy(history.at[pl.ds(1, bases.shape[0])], bases, sems.at[4])
    fetch([(incident.at[0], inc), (history.at[0], field), (inverse, inv), (coeff, load)], sems, later)
    blocks, size = inv.shape[0], inv.shape[1]
    half = blocks // 2
    solved = []
    for i in range(blocks):
        at = slice(i * size, (i + 1) * size)
        solved.append(solved_block(inc[at, :], field[at, :], in_two(inv[i]), column_of(load[i : i + 1, :])))
    shape = solved[0].shape
    left = lax.broadcasted_iota(jnp.int32, shape, 1) < shape[1] // 2
    for j in range(half):
        low, high, at = solved[j], turned(solved[j + half]), slice(j * size, (j + 1) * size)
        keep[at, :] = jnp.where(left, low, high).astype(keep.dtype)
        send[at, :] = jnp.where(left, high, low).astype(send.dtype)
    later.wait()


def by_parity(meta, own, theirs, kept, sem):
    copies = [pltpu.make_async_copy(source, kept, sem) for source in (own, theirs)]

    def start():
        pl.when(meta[0] == 0)(copies[0].start)
        pl.when(meta[0] != 0)(copies[1].start)

    return start, copies[0].wait


def fill_table(meta, wanted, listed, table, blocks, delays):
    slots = wanted.shape[2]
    owner = meta[2]
    per_row = listed.shape[2]
    for k in range(delays):
        for i in range(blocks):

            def body(s, _, k=k, i=i):
                slot = listed[k, i, s]
                who = slot // slots
                block = jnp.maximum(wanted[owner, who, slot - who * slots], 0)
                table[(k * blocks + i) * per_row + s] = (who ^ owner) * blocks + block
                return 0

            lax.fori_loop(0, per_row, body, 0, unroll=True)


def prepare_kernel(meta, wanted, listed, listed_there, incident, own, theirs, inverse, coeff, *refs):
    count = (len(refs) - 8) // 2
    incs, mats = refs[:count], refs[count : 2 * count]
    inv_high, inv_low, load, table, chain, inv, rows, sems = refs[2 * count :]
    pairs = [by_parity(meta, own.at[n], theirs.at[n], mats[n], sems.at[n]) for n in range(count)]
    plain = [(inverse, inv), (coeff, rows)] + [(incident.at[n + 1], incs[n]) for n in range(count)]
    plain = [pltpu.make_async_copy(a, b, sems.at[count + n]) for n, (a, b) in enumerate(plain)]
    for copy in plain:
        copy.start()
    for start, _ in pairs:
        start()
    blocks, size = inv.shape[0], inv.shape[1]
    fill_table(meta, wanted, listed, table, blocks, listed.shape[0])
    for parity, source in enumerate((listed, listed_there)):

        @pl.when(meta[0] == parity)
        def _():
            fill_table(meta, wanted, source, chain, blocks, count)

    for copy in plain:
        copy.wait()
    for i in range(blocks):
        inv_high[i], inv_low[i] = in_two(inv[i])
        load[i * size : (i + 1) * size, :] = column_of(rows[i : i + 1, :])
    for _, wait in pairs:
        wait()


def unpack_half(meta, block_of, owners, source, blocks):
    half, shape = blocks // 2, source.shape[1:]
    own = own_lanes(meta, shape)
    nothing = jnp.zeros(shape, source.dtype)
    for k in range(owners):
        for j in range(half):
            packed = block_of(k, j)
            source[k * blocks + j] = jnp.where(own, packed, nothing)
            source[k * blocks + j + half] = jnp.where(own, nothing, packed)


def base_of(meta, bases, at):
    own, partner, n = bases
    return own[at, :] if partner is None else jnp.where(meta[0] == 0, own[n, at, :], partner[n, at, :])


def next_kernel(places, step, meta, table, matrix, base, partner, inc, inv_high, inv_low, load, own, *refs):
    keep, joined, kept, source, sem = refs[-5:]
    bases = (base, None, 0) if step else (base, partner, 0)
    coming = pltpu.make_async_copy(own.at[step], kept, sem)
    coming.start()
    blocks, size = inv_high.shape[0], inv_high.shape[1]
    half, nonzero = blocks // 2, matrix.shape[1] // size

    def block_of(k, j):
        which, row = places[k]
        packed = refs[which][row + j * size : row + (j + 1) * size, :]
        joined[k * half + j] = packed
        return packed

    unpack_half(meta, block_of, len(places), source, blocks)
    solved = []
    for i in range(blocks):
        at = slice(i * size, (i + 1) * size)
        listed = table_of(table, i * nonzero)
        total = block_product(listed, matrix, i, lambda n: source[n], size)
        field = base_of(meta, bases, at) + (total + turned(total))
        solved.append(solved_block(inc[at, :], field, (inv_high[i], inv_low[i]), load[at, :]))
    lanes = own_lanes(meta, solved[0].shape)
    for j in range(half):
        at = slice(j * size, (j + 1) * size)
        keep[at, :] = jnp.where(lanes, solved[j], turned(solved[j + half])).astype(keep.dtype)
    coming.wait()


def ahead_kernel(blocks, meta, table, mine, matrix, base, partner, out, source):
    size = out.shape[0] // blocks
    half, nonzero = blocks // 2, matrix.shape[1] // size
    unpack_half(meta, lambda k, j: mine[k * half + j], mine.shape[0] // half, source, blocks)
    for i in range(blocks):
        at = slice(i * size, (i + 1) * size)
        listed = table_of(table, (blocks + i) * nonzero)
        total = block_product(listed, matrix, i, lambda n: source[n], size)
        out[at, :] = base_of(meta, (base, partner, 1), at) + (total + turned(total))


def unpack_whole(meta, mine, other, source, blocks, lanes=slice(None)):
    half = blocks // 2
    own = own_lanes(meta, mine.shape[1:])
    for k in range(mine.shape[0] // half):
        for j in range(half):
            a, b = mine[k * half + j], other[k * half + j]
            source[k * blocks + j, :, lanes] = jnp.where(own, a, b)
            source[k * blocks + j + half, :, lanes] = turned_exact(jnp.where(own, b, a))


def table_of(table, base):
    return lambda s: table[base + s]


def near_kernel(blocks, meta, table, mine, other, kept0, kept1, own, history, *refs):
    first, near, ahead, mats, whole, source, acc, sems = refs
    size = acc.shape[1] // blocks
    nonzero = kept0.shape[1] // size
    fields = pltpu.make_async_copy(history.at[pl.ds(0, acc.shape[0])], acc, sems.at[0])
    loads = pltpu.make_async_copy(own.at[pl.ds(2, mats.shape[0])], mats, sems.at[1])
    fields.start()
    loads.start()
    unpack_whole(meta, mine, other, source, blocks)
    for i in range(blocks):
        whole[i * size : (i + 1) * size, :] = source[i]
    fields.wait()
    for k, (matrix, out) in enumerate(((kept0, near), (kept1, ahead))):
        for i in range(blocks):
            at = slice(i * size, (i + 1) * size)
            listed = table_of(table, (k * blocks + i) * nonzero)
            total = acc[k + 1, at, :] + block_product(listed, matrix, i, lambda n: source[n], size)
            out[at, :] = total.astype(out.dtype)
    first[...] = acc[0].astype(first.dtype)
    loads.wait()


def nearer_kernel(blocks, meta, table, mine, other, matrix, base, near, source):
    size = base.shape[0] // blocks
    nonzero = matrix.shape[1] // size
    unpack_whole(meta, mine, other, source, blocks)
    for i in range(blocks):
        at = slice(i * size, (i + 1) * size)
        listed = table_of(table, i * nonzero)
        total = base[at, :] + block_product(listed, matrix, i, lambda n: source[n], size)
        near[at, :] = total.astype(near.dtype)


def far_kernel(blocks, meta, table, mine, other, mats, history, out, *refs):
    source, sems = refs[0], refs[-1]
    size, count = out.shape[1] // blocks, mats.shape[0]
    nonzero = mats.shape[2] // size
    later = None
    if len(refs) == 3:
        later = pltpu.make_async_copy(history.at[pl.ds(STEPS, count - 1)], refs[1], sems.at[0])
        later.start()
    unpack_whole(meta, mine, other, source, blocks)
    for n in reversed(range(count)):
        for i in range(blocks):
            at = slice(i * size, (i + 1) * size)
            listed = table_of(table, ((n + 2) * blocks + i) * nonzero)
            out[n, at, :] = block_product(listed, mats.at[n], i, lambda m: source[m], size)
    if later is not None:
        later.wait()
        for n in range(count - 1):
            out[n] = out[n] + refs[1][n]


def last_kernel(blocks, meta, table, mine1, other1, mine, other, kept0, kept1, mats, acc, late, first, *refs):
    future, currents, source, out, whole1, whole2, sems = refs
    delays, size, excite = out.shape[0], out.shape[1] // blocks, out.shape[2]
    nonzero = kept0.shape[1] // size
    matrices = [kept0, kept1] + [mats.at[k] for k in range(mats.shape[0])]
    stores = []

    def store(value, place):
        stores.append(pltpu.make_async_copy(value, place, sems.at[len(stores)]))
        stores[-1].start()

    store(first, currents.at[0])
    for n, (a, b, whole) in enumerate(((mine1, other1, whole1), (mine, other, whole2))):
        lanes = slice(n * excite, (n + 1) * excite)
        unpack_whole(meta, a, b, source, blocks, lanes)
        for i in range(blocks):
            whole[i * size : (i + 1) * size, :] = source[i, :, lanes]
        store(whole, currents.at[n + 1])
    followed = meta[1] == 1
    for k in range(delays):
        for i in range(blocks):
            at = slice(i * size, (i + 1) * size)
            listed = table_of(table, (k * blocks + i) * nonzero)
            if k == 0:
                total = block_product(listed, matrices[k], i, lambda n: source[n, :, excite:], size)
            else:
                both = block_product(listed, matrices[k], i, lambda n: source[n], size)
                out[k - 1, at, :] = out[k - 1, at, :] + both[:, :excite]
                total = both[:, excite:]
            if k < acc.shape[0]:
                total = total + acc[k, at, :]
            if k >= delays - late.shape[0]:
                extra = late[k - (delays - late.shape[0]), at, :].astype(jnp.float32)
                total = total + jnp.where(followed, extra, 0.0)
            out[k, at, :] = total
        if k > 0:
            store(out.at[k - 1], future.at[k - 1])
    store(out.at[delays - 1], future.at[delays - 1])
    for one in stores:
        one.wait()


def struct(shape, dtype):
    return jax.ShapeDtypeStruct(shape, dtype)


def local_paired(incident, history, couplings, block_inverse, load_coeff, pattern, wanted):
    blocks, size = block_inverse.shape[:2]
    rows, excite = incident.shape[1:]
    delays = history.shape[0]
    n_delay, n_row = lax.axis_size("delay"), lax.axis_size("row")
    d, r = lax.axis_index("delay"), lax.axis_index("row")
    parity = d % 2
    half = blocks // 2
    bf16, f32 = jnp.bfloat16, jnp.float32
    axes = ("delay", "row")

    def swap(value, bit):
        pairs = [(a * n_row + q, (a ^ bit) * n_row + q) for a in range(n_delay) for q in range(n_row)]
        return lax.ppermute(value, axes, pairs)

    def swap_row(value, bit):
        pairs = [(a * n_row + q, a * n_row + (q ^ bit)) for a in range(n_delay) for q in range(n_row)]
        return lax.ppermute(value, axes, pairs)

    meta = jnp.stack([parity, (d < n_delay - 1).astype(jnp.int32), r])
    load = load_coeff.reshape(blocks, size)

    packed = struct((half * size, excite), bf16)
    gathered = (n_row * half, size, excite)
    source = pltpu.VMEM((n_row * blocks, size, excite), bf16)

    def planes(value):
        bit = 2
        while bit < n_delay:
            got = swap(value, bit)
            value = jnp.where((d >= bit) & (d < 2 * bit), got, value)
            bit *= 2
        return value

    def exchange(value):
        direct, groups = row_plan(n_row)
        pieces = [None] * n_row
        pieces[0] = (value, 0)
        for k in direct:
            pieces[k] = (swap_row(value, k), 0)
        for group in groups:
            passed = [pieces[k][0] for k in group]
            passed = swap_row(jnp.concatenate(passed, 0) if len(group) > 1 else passed[0], 1)
            for m, k in enumerate(group):
                pieces[k ^ 1] = (passed, m * half * size)
        return pieces

    def gather_other(mine):
        return swap(mine, 1)

    hbm = lambda value: pltpu.with_memory_space_constraint(value, pltpu.MemorySpace.HBM)
    couplings, history, incident = map(hbm, (couplings, history, incident))
    block_inverse, load = map(hbm, (block_inverse, load))

    count = STEPS - 1
    keep, send, bases = pl.pallas_call(
        first_kernel,
        out_shape=[packed] * 2 + [struct((count, rows, excite), f32)],
        in_specs=[HBM] * 4,
        out_specs=[VMEM] * 3,
        scratch_shapes=[
            pltpu.VMEM((rows, excite), bf16),
            pltpu.VMEM((rows, excite), f32),
            pltpu.VMEM(block_inverse.shape, f32),
            pltpu.VMEM(load.shape, f32),
            pltpu.SemaphoreType.DMA((5,)),
        ],
        compiler_params=PARAMS,
        name="first",
    )(incident, history, block_inverse, load)
    got = swap(send, 1)
    mine = jnp.where(parity == 0, keep, got)
    theirs = hbm(swap(couplings, 1))
    partner = swap(bases, 1)
    listed_there = swap(pattern, 1)
    tables = [struct((n * blocks * pattern.shape[2],), jnp.int32) for n in (delays, count)]
    field, current = struct((rows, excite), f32), struct((rows, excite), bf16)
    matrix = struct(couplings.shape[1:], bf16)
    prepared = pl.pallas_call(
        prepare_kernel,
        out_shape=[current] * count + [matrix] * count + [struct(block_inverse.shape, bf16)] * 2 + [field] + tables,
        in_specs=[SMEM] * 4 + [HBM] * 5,
        out_specs=[VMEM] * (2 * count + 3) + [SMEM] * 2,
        scratch_shapes=[
            pltpu.VMEM(block_inverse.shape, f32),
            pltpu.VMEM(load.shape, f32),
            pltpu.SemaphoreType.DMA((2 * count + 2,)),
        ],
        compiler_params=LARGE,
        name="prepare",
    )(meta, wanted, pattern, listed_there, incident, couplings, theirs, block_inverse, load)
    incs, mats = prepared[:count], prepared[count : 2 * count]
    inv_high, inv_low, load, table, chain = prepared[2 * count :]

    def advance(step, pieces, mat, base):
        arrays = []
        places = []
        for array, row in pieces:
            seen = [n for n, one in enumerate(arrays) if one is array]
            places.append((seen[0] if seen else len(arrays), row))
            arrays += [] if seen else [array]
        return pl.pallas_call(
            functools.partial(next_kernel, places, step),
            out_shape=[packed, struct(gathered, bf16), matrix],
            in_specs=[SMEM] * 2 + [VMEM] * 7 + [HBM] + [VMEM] * len(arrays),
            out_specs=[VMEM] * 3,
            scratch_shapes=[source, pltpu.SemaphoreType.DMA(())],
            compiler_params=LARGE,
            name="next",
        )(meta, chain, mat, base, base if step else partner, incs[step], inv_high, inv_low, load, couplings, *arrays)

    def spread_out(mine):
        mine = planes(mine)
        return exchange(mine)

    pieces = spread_out(mine)
    mine, near0, kept0 = advance(0, pieces, mats[0], bases)
    base = pl.pallas_call(
        functools.partial(ahead_kernel, blocks),
        out_shape=field,
        in_specs=[SMEM] * 2 + [VMEM] * 4,
        out_specs=VMEM,
        scratch_shapes=[source],
        compiler_params=LARGE,
        name="ahead",
    )(meta, chain, near0, mats[1], bases, partner)

    pieces = spread_out(mine)
    mine, near1, kept1 = advance(1, pieces, mats[0], base)
    other0 = gather_other(near0)
    tail, first_tail, ahead, mats_rest, whole0 = pl.pallas_call(
        functools.partial(near_kernel, blocks),
        out_shape=[current, current, field, struct((delays - 2,) + couplings.shape[1:], bf16), current],
        in_specs=[SMEM] * 2 + [VMEM] * 4 + [HBM] * 2,
        out_specs=[VMEM] * 5,
        scratch_shapes=[source, pltpu.VMEM((STEPS, rows, excite), f32), pltpu.SemaphoreType.DMA((2,))],
        compiler_params=LARGE,
        name="near",
    )(meta, table, near0, other0, kept0, kept1, couplings, history)
    other1 = gather_other(near1)
    second_tail = pl.pallas_call(
        functools.partial(nearer_kernel, blocks),
        out_shape=current,
        in_specs=[SMEM] * 2 + [VMEM] * 4,
        out_specs=VMEM,
        scratch_shapes=[source],
        compiler_params=LARGE,
        name="nearer",
    )(meta, table, near1, other1, kept0, ahead)
    acc = pl.pallas_call(
        functools.partial(far_kernel, blocks),
        out_shape=struct((delays - 2, rows, excite), f32),
        in_specs=[SMEM] * 2 + [VMEM] * 3 + [HBM],
        out_specs=VMEM,
        scratch_shapes=[source]
        + [pltpu.VMEM((delays - STEPS, rows, excite), f32)] * (delays > STEPS)
        + [pltpu.SemaphoreType.DMA((1,))],
        compiler_params=LARGE,
        name="far",
    )(meta, table, near0, other0, mats_rest, history)
    tails = [tail, first_tail, second_tail]
    back = [(a * n_row + q, ((a - 1) % n_delay) * n_row + q) for a in range(n_delay) for q in range(n_row)]
    late = lax.ppermute(jnp.stack(tails), axes, back)

    pieces = spread_out(mine)
    near2 = jnp.concatenate([array[row : row + half * size] for array, row in pieces], 0).reshape(gathered)
    other2 = gather_other(near2)

    future, currents = pl.pallas_call(
        functools.partial(last_kernel, blocks),
        out_shape=[struct(history.shape, f32), struct((STEPS, rows, excite), bf16)],
        in_specs=[SMEM] * 2 + [VMEM] * 10,
        out_specs=[HBM] * 2,
        scratch_shapes=[
            pltpu.VMEM((n_row * blocks, size, 2 * excite), bf16),
            pltpu.VMEM(history.shape, f32),
            pltpu.VMEM((rows, excite), bf16),
            pltpu.VMEM((rows, excite), bf16),
            pltpu.SemaphoreType.DMA((delays + STEPS,)),
        ],
        compiler_params=LARGE,
        name="last",
    )(meta, table, near1, other1, near2, other2, kept0, kept1, mats_rest, acc, late, whole0)
    return currents, future


def fits(mesh, blocks, delays):
    sizes = (mesh.shape["delay"], mesh.shape["row"])
    powers = all(n >= 2 and n & (n - 1) == 0 for n in sizes)
    return powers and blocks % 2 == 0 and delays >= STEPS and STEPS == 3


def row_plan(n_row):
    far, near = n_row // 2, 2
    groups = [] if n_row < 4 else [[far]] if far == near else [[far, near], [far + near]]
    passed = [k for group in groups for k in group]
    others = [k for k in range(n_row - 1, 1, -1) if k not in passed and k ^ 1 not in passed]
    return passed + others + [1], groups


def solution(mesh):
    in_specs = (
        P(None, "row", None),
        P("delay", "row", None),
        P("delay", "row", None),
        P("row", None, None),
        P("row"),
        P("delay", "row", None),
        P(),
    )
    out_specs = (P(None, "row", None), P("delay", "row", None))

    def local(*args):
        if not fits(mesh, args[3].shape[0], args[1].shape[0]):
            return local_general(*args)
        return local_paired(*args)

    return jax.shard_map(local, mesh=mesh, in_specs=in_specs, out_specs=out_specs, check_vma=False)
```
